32 devices in a mesh: uv: 8 (over y, x, core), tm: 4 (over z).
Axes of the slice: x: 2, y: 2, z: 4, core: 2. Of those that a mesh axis runs over, the one named last changes fastest.
Arguments:
- visibilities: bfloat16 [8, 128, 16384], P(None, 'uv', 'tm'), may hold values from -0.75 to 0.75
- positions: float32 [2, 128, 16384], P(None, 'uv', 'tm'), may hold values from 4 to 60
- owner: int32 [128, 1], P('uv'), may hold values from 0 to 7; in each aligned block of 16 rows (0 to 15, 16 to 31, ...) at most 4 rows name the same one
- w_plane: int32 [128], P('uv'), may hold values from 0 to 7
- row_offset: int32 [128], P('uv'), may hold values from 0 to 127
- col_offset: int32 [128], P('uv'), may hold values from 0 to 1984
Outputs:
- grid: float32 [8, 8, 1024, 2048], P('tm', None, 'uv')
The draws below stay inside these ranges and needn't reach their ends.
Inputs may be any that keep to these rules, and one draw needn't show every extreme that they name: `owner`: among the 16 subgrids of one index of uv (aligned blocks of rows), no tile is named by more than 4 of them.
All inputs are finite; a program needn't handle non-finite values.
Results may differ from the reference program's by a relative error of at most 0.0037.
Values may be sent and summed in bfloat16 or wider, within the bound.
No kernel may reach another device: no remote copies, remote signals or barrier semaphores. Data moves between devices by JAX's collectives and lax.ppermute only.
A program may use at most 128 MiB of HBM per device.

```python
import math
import jax
import jax.numpy as jnp
import numpy as np
from jax import lax

C2 = 8
W = 8
SUB = 64
TAPS = 8
SUB_DEV = 16
VT = 4096
TU = 128
NV = 2048
NSUB = 128
TROWS = 16384
NU = 1024
CAP = 4
N_UV = 8
N_TM = 4


def set_ends(result, stream_key, low, high):
    longest = result.shape.index(max(result.shape))
    spots = []
    for shift in (0, 1):
        where = [jax.random.randint(jax.random.fold_in(stream_key, axis), (), 0, length) for axis, length in enumerate(result.shape)]
        where[longest] = (where[longest] + shift) % result.shape[longest]
        spots.append(tuple(where))
    return result.at[spots[0]].set(low).at[spots[1]].set(high)


def block_levels(own_key, shape, split, least, high):
    factor_of = 1.0
    for axis_at, shards_of in split:
        draws = jax.random.uniform(jax.random.fold_in(jax.random.fold_in(own_key, 6), axis_at), (shards_of,), jnp.float32, least / len(split), high / len(split))
        factor_of = factor_of * jnp.repeat(jnp.exp(draws), shape[axis_at] // shards_of).reshape((-1,) + (1,) * (len(shape) - 1 - axis_at))
    return factor_of


def shared_out(own_key, own, number, rows, count, top, limit, lean):
    sequence = jax.random.permutation(own_key, count)
    packed, ordinary = load_shares(count, rows * top, limit, lean, True), load_shares(count, rows * top, limit, lean, False)
    places = jnp.arange(count)

    def named(tallies, rotation):
        used = int((tallies > 0).sum())
        fixed = max(1, used // 4)
        passed = fixed + (places - fixed + rotation * (used - fixed)) % max(1, count - fixed)
        return jnp.zeros((count,), jnp.int32).at[sequence[jnp.where(places < fixed, places, passed)]].set(jnp.asarray(tallies, jnp.int32))

    tallies = jnp.where(number % 4 == 0, named(packed, number // 4), named(ordinary, number - number // 4 - 1))
    mixed = jax.random.permutation(jax.random.fold_in(own, 3), count)
    giver, sink = mixed[0:count // 2 * 2:2], mixed[1:count // 2 * 2:2]
    margin = jnp.minimum(tallies[giver] - 1, limit - tallies[sink]) // 2
    margin = jnp.where((giver == sequence[0]) | (sink == sequence[0]) | (tallies[sink] == 0), 0, jnp.maximum(margin, 0))
    passed = jax.random.randint(jax.random.fold_in(own, 4), (count // 2,), 0, 1 << 20) % (margin + 1)
    tallies = tallies.at[giver].add(-passed).at[sink].add(passed)
    members = jnp.searchsorted(jnp.cumsum(tallies), jnp.arange(rows * top), side="right").astype(jnp.int32)
    table = members.reshape(top, rows).T
    table = table[jax.random.permutation(jax.random.fold_in(own, 1), rows)]
    rotation = jax.random.randint(jax.random.fold_in(own, 2), (rows, 1), 0, top)
    return jnp.take_along_axis(table, (jnp.arange(top)[None, :] + rotation) % top, axis=1)


def load_shares(count, total, most, lean, full):
    portions = [(1 << 20) // math.isqrt(grade ** lean) + 1 for grade in range(1, count + 1)]
    largest = most if full else min(most, max(-(-total // count), total * portions[0] // sum(portions)))
    least = 1 if total - largest >= count - 1 else 0
    holding, spare = [largest] + [least] * (count - 1), total - largest - least * (count - 1)
    while spare > 0:
        free = [i for i in range(1, count) if holding[i] < largest] or [i for i in range(1, count) if holding[i] < most]
        mass, left = sum([portions[i] for i in free]), spare
        for i in free:
            extra = min(most - holding[i], max(1, left * portions[i] // mass), spare)
            holding[i] = holding[i] + extra
            spare = spare - extra
    return np.array(holding)


def noise(rng, dims, scale, limit, cuts=(), kind=jnp.bfloat16):
    array = scale * jax.random.normal(rng, dims, jnp.float32)
    if cuts:
        array = array * block_levels(rng, dims, cuts, -0.22, 0.18)
    return jnp.clip(array, -limit, limit).astype(kind)


def setup_inputs(seed: int = 0) -> dict:
    arg_keys = jax.random.split(jax.random.key(seed), 7)
    visibilities = noise(arg_keys[0], (C2, NSUB, TROWS), (16.0 / (VT * N_TM) ** 0.5), 0.75, ((1, 8), (2, 4)))
    positions = jnp.clip(4.0 + 56.0 * jax.random.uniform(arg_keys[1], (2, NSUB, TROWS), jnp.float32) ** block_levels(arg_keys[1], (2, NSUB, TROWS), ((1, 8), (2, 4)), -0.2, 0.2), 4.0, 60.0)
    owner_keys = jax.random.split(jax.random.fold_in(arg_keys[2], 1), NSUB // SUB_DEV)
    owner_turns = jax.random.permutation(jax.random.fold_in(arg_keys[2], 3), NSUB // SUB_DEV)
    owner = jax.vmap(lambda own, number: shared_out(jax.random.fold_in(arg_keys[2], 2), own, number, SUB_DEV, N_UV, 1, CAP, 2))(owner_keys, owner_turns).reshape((NSUB, 1))
    w_plane = set_ends(jax.random.randint(arg_keys[3], (NSUB,), 0, W), jax.random.fold_in(arg_keys[3], 1), 0, W - 1).astype(jnp.int32)
    row_offset = set_ends(jax.random.randint(arg_keys[4], (NSUB,), 0, TU), jax.random.fold_in(arg_keys[4], 1), 0, TU - 1).astype(jnp.int32)
    col_offset = set_ends(jax.random.randint(arg_keys[5], (NSUB,), 0, NV - SUB + 1), jax.random.fold_in(arg_keys[5], 1), 0, NV - SUB).astype(jnp.int32)
    return {"visibilities": visibilities, "positions": positions, "owner": owner, "w_plane": w_plane, "row_offset": row_offset, "col_offset": col_offset}


def taper(offsets):
    scaled = offsets * (2.0 / TAPS)
    return jnp.square(jnp.maximum(0.0, 1.0 - scaled * scaled))


def group_grid(values, places):
    cell_index = jnp.arange(SUB, dtype=jnp.float32)
    row_taps = taper(cell_index - places[0][:, :, None]).astype(jnp.bfloat16)
    col_taps = taper(cell_index - places[1][:, :, None])
    weighted = (values.astype(jnp.float32)[:, :, :, None] * col_taps[None]).astype(jnp.bfloat16)
    product = jnp.einsum("gtu,cgtv->cguv", row_taps.astype(jnp.float32), weighted.astype(jnp.float32))
    return product.reshape(values.shape[0], values.shape[1], SUB * SUB)


def reference(visibilities, positions, owner, w_plane, row_offset, col_offset):
    span = math.gcd(TROWS, 4096)

    def one_group(group_index):
        sub_start = group_index * 4
        group_values = lax.dynamic_slice_in_dim(visibilities, sub_start, 4, 1)
        group_places = lax.dynamic_slice_in_dim(positions, sub_start, 4, 1)

        def add_span(step_index, running):
            row_start = step_index * span
            span_values = lax.dynamic_slice_in_dim(group_values, row_start, span, 2)
            span_places = lax.dynamic_slice_in_dim(group_places, row_start, span, 2)
            return running + group_grid(span_values, span_places)

        return lax.fori_loop(0, TROWS // span, add_span, jnp.zeros((C2, 4, SUB * SUB), jnp.float32))

    stacked = lax.map(one_group, jnp.arange(NSUB // 4, dtype=jnp.int32))
    subgrids = jnp.transpose(stacked, (1, 0, 2, 3)).reshape(C2, NSUB, SUB * SUB)
    within = jnp.arange(SUB * SUB, dtype=jnp.int32)
    global_rows = (owner[:, 0][:, None] * TU + row_offset[:, None] + (within // SUB)[None, :]) % NU
    flat = (w_plane[:, None] * NU + global_rows) * NV + col_offset[:, None] + (within % SUB)[None, :]
    grid = jnp.zeros((C2, W * NU * NV), jnp.float32).at[:, flat].add(subgrids)
    return grid.reshape(C2, W, NU, NV)
```

```python
import functools

import jax
import jax.numpy as jnp
from jax import lax
from jax.experimental import pallas as pl
from jax.experimental.pallas import tpu as pltpu
from jax.sharding import PartitionSpec as P

W = 8
SUB = 64
TAPS = 8
TU = 128
NV = 2048
LANES = 128
SUBLANES = 8


def taper(scaled):
    inner = jnp.maximum(0.0, 1.0 - scaled * scaled)
    return inner * inner


def grid_kernel(values_ref, places_ref, parts_ref, values_wide, *, peers):
    comp_count, sub_count, row_count = values_ref.shape
    kept = parts_ref.shape[3]
    for comp in range(comp_count):
        values_wide[comp * sub_count : (comp + 1) * sub_count, :] = values_ref[comp].astype(jnp.float32)
    cells = lax.broadcasted_iota(jnp.int32, (SUB, row_count), 0).astype(jnp.float32) * (2.0 / TAPS)

    def one_sub(sub, carry):
        row_taps = taper(cells - places_ref[0, pl.ds(sub, 1), :] * (2.0 / TAPS)).astype(jnp.bfloat16)
        col_taps = taper(cells - places_ref[1, pl.ds(sub, 1), :] * (2.0 / TAPS))
        weighted = jnp.concatenate(
            [
                (values_wide[pl.ds(comp * sub_count + sub, 1), :] * col_taps).astype(jnp.bfloat16)
                for comp in range(comp_count)
            ],
            axis=0,
        )
        cellsums = lax.dot_general(
            row_taps, weighted, (((1,), (1,)), ((), ())), preferred_element_type=jnp.float32
        ).astype(jnp.bfloat16)
        for peer in range(peers):
            parts_ref[peer, sub] = cellsums[:, peer * kept : (peer + 1) * kept]
        return carry

    lax.fori_loop(0, sub_count, one_sub, 0)


def grid_parts(values, places, peers):
    comp_count, sub_count, row_count = values.shape
    kept = comp_count // peers * SUB
    return pl.pallas_call(
        functools.partial(grid_kernel, peers=peers),
        out_shape=jax.ShapeDtypeStruct((peers, sub_count, SUB, kept), jnp.bfloat16),
        in_specs=[pl.BlockSpec(memory_space=pltpu.VMEM)] * 2,
        out_specs=pl.BlockSpec(memory_space=pltpu.VMEM),
        scratch_shapes=[pltpu.VMEM((comp_count * sub_count, row_count), jnp.float32)],
        compiler_params=pltpu.CompilerParams(vmem_limit_bytes=48 << 20),
        cost_estimate=pl.CostEstimate(
            flops=2 * sub_count * row_count * SUB * SUB * comp_count,
            bytes_accessed=4 << 20,
            transcendentals=0,
        ),
    )(values, places)


def place_kernel(start_ref, plane_ref, col_ref, patches_ref, out_ref, canvas, sem, count, listed):
    total = start_ref.shape[0]
    comp_count = canvas.shape[1]
    for plane in range(W):
        count[plane] = 0

    def enlist(sub, carry):
        @pl.when(start_ref[sub] >= 0)
        def _():
            plane = plane_ref[sub]
            at = count[plane]
            listed[plane, at] = sub
            count[plane] = at + 1

        return carry

    lax.fori_loop(0, total, enlist, 0)
    lane = lax.broadcasted_iota(jnp.int32, (SUB + SUBLANES, LANES), 1)

    def out_copy(slot, plane):
        return pltpu.make_async_copy(
            canvas.at[slot, :, pl.ds(SUB, TU), :], out_ref.at[:, plane], sem.at[slot]
        )

    def one_plane(plane, slot):
        canvas[slot] = jnp.zeros(canvas.shape[1:], jnp.float32)

        def add_patch(index, carry):
            sub = listed[plane, index]
            start = start_ref[sub]
            col = col_ref[sub]
            block = pl.multiple_of(col // LANES * LANES, LANES)
            shift = col % LANES
            patch = patches_ref[sub].astype(jnp.float32)
            if patch.shape[1] < LANES:
                patch = jnp.concatenate([patch] * (LANES // patch.shape[1]), axis=1)
            patch = jnp.concatenate([patch, jnp.zeros((SUBLANES, patch.shape[1]), jnp.float32)], axis=0)
            patch = pltpu.roll(patch, start % SUBLANES, 0)
            rows = pl.ds(pl.multiple_of(start // SUBLANES * SUBLANES, SUBLANES), SUB + SUBLANES)
            for comp in range(comp_count):
                source = patch[:, comp // 2 * LANES : (comp // 2 + 1) * LANES]
                turned = pltpu.roll(source, (shift + comp % 2 * SUB) % LANES, 1)
                here = (lane >= shift) & (lane < shift + SUB)
                canvas[slot, comp, rows, pl.ds(block, LANES)] += jnp.where(here, turned, 0.0)

                @pl.when(shift > LANES - SUB)
                def _():
                    canvas[slot, comp, rows, pl.ds(block + LANES, LANES)] += jnp.where(
                        lane < shift + SUB - LANES, turned, 0.0
                    )

            return carry

        lax.fori_loop(0, count[plane], add_patch, 0)
        out_copy(slot, plane).start()

    for plane in range(W):
        slot = plane % 2
        if plane >= 2:
            out_copy(slot, plane - 2).wait()
        one_plane(plane, slot)
    for plane in range(W - 2, W):
        out_copy(plane % 2, plane).wait()


def place_all(patches, starts, planes, cols, comp_count):
    total = patches.shape[0]
    smem = pl.BlockSpec(memory_space=pltpu.SMEM)
    return pl.pallas_call(
        place_kernel,
        out_shape=jax.ShapeDtypeStruct((comp_count, W, TU, NV), jnp.float32),
        in_specs=[smem, smem, smem, pl.BlockSpec(memory_space=pltpu.VMEM)],
        out_specs=pl.BlockSpec(memory_space=pl.ANY),
        scratch_shapes=[
            pltpu.VMEM((2, comp_count, TU + 2 * SUB, NV), jnp.float32),
            pltpu.SemaphoreType.DMA((2,)),
            pltpu.SMEM((W,), jnp.int32),
            pltpu.SMEM((W, total), jnp.int32),
        ],
        compiler_params=pltpu.CompilerParams(vmem_limit_bytes=32 << 20),
        cost_estimate=pl.CostEstimate(
            flops=0, bytes_accessed=comp_count * W * TU * NV * 4, transcendentals=0
        ),
    )(starts, planes, cols, patches)


def gather_around(array, axis):
    size = lax.axis_size(axis)
    hops = [array] + [
        lax.ppermute(array, axis, [((i + by) % size, i) for i in range(size)]) for by in range(1, size)
    ]
    return jnp.stack(hops, axis=0)


def body(visibilities, positions, owner, w_plane, row_offset, col_offset):
    peers = lax.axis_size("tm")
    tiles = lax.axis_size("uv")
    comp_count = visibilities.shape[0] // peers
    tile = lax.axis_index("uv")
    parts = grid_parts(visibilities, positions, peers)
    swapped = lax.all_to_all(parts, "tm", split_axis=0, concat_axis=0, tiled=True)
    summed = jnp.sum(swapped.astype(jnp.float32), axis=0).astype(jnp.bfloat16)
    patches = gather_around(summed, "uv")
    patches = patches.reshape((-1,) + patches.shape[2:])
    placing = gather_around(jnp.stack([owner[:, 0], row_offset, w_plane, col_offset], axis=0), "uv")
    placing = jnp.transpose(placing, (1, 0, 2)).reshape(4, -1)
    ahead = (placing[0] - tile) % tiles
    starts = jnp.where(ahead == 0, placing[1] + SUB, jnp.where(ahead == tiles - 1, placing[1] + SUB - TU, -1))
    return place_all(patches, starts, placing[2], placing[3], comp_count)


def solution(mesh):
    placed = (P(None, "uv", "tm"), P(None, "uv", "tm"), P("uv", None), P("uv"), P("uv"), P("uv"))
    return jax.shard_map(
        body, mesh=mesh, in_specs=placed, out_specs=P("tm", None, "uv", None), check_vma=False
    )
```

```python
import functools

import jax
import jax.numpy as jnp
from jax import lax
from jax.experimental import pallas as pl
from jax.experimental.pallas import tpu as pltpu
from jax.sharding import PartitionSpec as P

W = 8
SUB = 64
TAPS = 8
TU = 128
NV = 2048
LANES = 128
SUBLANES = 8
BLOCKS = NV // LANES
META = 16
STEP = 4

VMEM = pl.BlockSpec(memory_space=pltpu.VMEM)
SMEM = pl.BlockSpec(memory_space=pltpu.SMEM)
ANY = pl.BlockSpec(memory_space=pl.ANY)


def taper(scaled):
    inner = jnp.maximum(0.0, 1.0 - scaled * scaled)
    return inner * inner


def grid_kernel(me_ref, values_ref, places_ref, *rest):
    parts_refs, values_wide, pair_sums = rest[:-2], rest[-2], rest[-1]
    comp_count, sub_count, row_count = values_ref.shape
    peers = len(parts_refs)
    kept = comp_count // peers * SUB
    for comp in range(comp_count):
        values_wide[comp * sub_count : (comp + 1) * sub_count, :] = values_ref[comp].astype(jnp.float32)
    cells = lax.broadcasted_iota(jnp.int32, (SUB, row_count), 0).astype(jnp.float32) * (2.0 / TAPS)

    def one_sub(sub):
        row_taps = taper(cells - places_ref[0, pl.ds(sub, 1), :] * (2.0 / TAPS)).astype(jnp.bfloat16)
        col_taps = taper(cells - places_ref[1, pl.ds(sub, 1), :] * (2.0 / TAPS))
        weighted = jnp.concatenate(
            [
                (values_wide[pl.ds(comp * sub_count + sub, 1), :] * col_taps).astype(jnp.bfloat16)
                for comp in range(comp_count)
            ],
            axis=0,
        )
        return lax.dot_general(
            weighted, row_taps, (((1,), (1,)), ((), ())), preferred_element_type=jnp.float32
        )

    def some_subs(turn, carry):
        for pair in range(STEP // 2):
            sub = turn * STEP + pair * 2
            pair_sums[pair] = jnp.concatenate([one_sub(sub), one_sub(sub + 1)], axis=1).astype(jnp.bfloat16)
        for pair in range(STEP // 2):
            for ahead, parts_ref in enumerate(parts_refs):
                peer = lax.rem(me_ref[0] + ahead, peers)
                rows = pl.ds(pl.multiple_of(peer * kept, kept), kept)
                parts_ref[turn * (STEP // 2) + pair] = pair_sums[pair, rows, :]
        return carry

    lax.fori_loop(0, sub_count // STEP, some_subs, 0)


def grid_parts(values, places, peers, chunk, sub_count):
    comp_count, _, row_count = values.shape
    kept = comp_count // peers * SUB
    me = lax.axis_index("tm").astype(jnp.int32).reshape(1)
    return pl.pallas_call(
        grid_kernel,
        grid=(1,),
        out_shape=[jax.ShapeDtypeStruct((sub_count // 2, kept, LANES), jnp.bfloat16)] * peers,
        in_specs=[
            SMEM,
            pl.BlockSpec((comp_count, sub_count, row_count), lambda i: (0, chunk, 0)),
            pl.BlockSpec((2, sub_count, row_count), lambda i: (0, chunk, 0)),
        ],
        out_specs=[pl.BlockSpec((sub_count // 2, kept, LANES), lambda i: (0, 0, 0))] * peers,
        scratch_shapes=[
            pltpu.VMEM((comp_count * sub_count, row_count), jnp.float32),
            pltpu.VMEM((STEP // 2, comp_count * SUB, LANES), jnp.bfloat16),
        ],
        compiler_params=pltpu.CompilerParams(vmem_limit_bytes=48 << 20),
        cost_estimate=pl.CostEstimate(
            flops=8 * sub_count * row_count * SUB * SUB * comp_count,
            bytes_accessed=2 << 20,
            transcendentals=0,
        ),
    )(me, values, places)


def sum_kernel(*refs):
    numbers_ref, parts_refs, out_ref = refs[0], refs[1:-1], refs[-1]
    pairs = parts_refs[0].shape[0]
    for pair in range(pairs):
        total = parts_refs[0][pair].astype(jnp.float32)
        for parts_ref in parts_refs[1:]:
            total = total + parts_ref[pair].astype(jnp.float32)
        out_ref[pair * 2 * SUB : (pair + 1) * 2 * SUB, :] = total.T.astype(jnp.bfloat16)
    out_ref[pairs * 2 * SUB :, :] = numbers_ref[...].astype(jnp.bfloat16)


def sum_parts(parts, numbers):
    pairs, kept, _ = parts[0].shape
    return pl.pallas_call(
        sum_kernel,
        out_shape=jax.ShapeDtypeStruct((pairs * 2 * SUB + META, kept), jnp.bfloat16),
        in_specs=[VMEM] * (1 + len(parts)),
        out_specs=VMEM,
        compiler_params=pltpu.CompilerParams(vmem_limit_bytes=8 << 20),
        cost_estimate=pl.CostEstimate(flops=1 << 20, bytes_accessed=2 << 20, transcendentals=0),
    )(numbers, *parts)


def exchange(parts, axis):
    size = lax.axis_size(axis)
    return [parts[0]] + [
        lax.ppermute(parts[by], axis, [(i, (i + by) % size) for i in range(size)]) for by in range(1, size)
    ]


def gather_all(array, axis):
    size = lax.axis_size(axis)
    near = [array] + [
        lax.ppermute(array, axis, [(i, i ^ mask) for i in range(size)]) for mask in range(2, size, 2)
    ]
    near = jnp.stack(near, axis=0)
    other = lax.ppermute(near, axis, [(i, i ^ 1) for i in range(size)])
    return [near, other]


def zero_kernel(token_ref, out_ref, blank, sem):
    blank[...] = jnp.zeros(blank.shape, jnp.float32)
    copies = [pltpu.make_async_copy(blank, out_ref.at[:, plane], sem.at[plane]) for plane in range(W)]
    for copy in copies:
        copy.start()
    for copy in copies:
        copy.wait()


def blank_tile(token, comp_count):
    return pl.pallas_call(
        zero_kernel,
        out_shape=jax.ShapeDtypeStruct((comp_count, W, TU, NV), jnp.float32),
        in_specs=[ANY],
        out_specs=ANY,
        scratch_shapes=[pltpu.VMEM((comp_count, TU, NV), jnp.float32), pltpu.SemaphoreType.DMA((W,))],
        compiler_params=pltpu.CompilerParams(vmem_limit_bytes=8 << 20),
        cost_estimate=pl.CostEstimate(
            flops=0, bytes_accessed=comp_count * W * TU * NV * 4, transcendentals=0
        ),
    )(token)


def plan_kernel(placing_ref, count_ref, listed_ref, used_count_ref, used_ref, touched):
    sources, _, per_source = placing_ref.shape

    def clear(index, carry):
        touched[index] = 0
        return carry

    lax.fori_loop(0, W * BLOCKS, clear, 0)
    for plane in range(W):
        used_count_ref[plane] = 0
        for source in range(sources):
            count_ref[source, plane] = 0
    for source in range(sources):

        def enlist(sub, carry, source=source):
            @pl.when(placing_ref[source, 0, sub] >= 0)
            def _():
                plane = placing_ref[source, 1, sub]
                col = placing_ref[source, 2, sub]
                at = count_ref[source, plane]
                listed_ref[source, plane, at] = sub
                count_ref[source, plane] = at + 1

                def use(block):
                    @pl.when(touched[plane * BLOCKS + block] == 0)
                    def _():
                        touched[plane * BLOCKS + block] = 1
                        used_at = used_count_ref[plane]
                        used_ref[plane, used_at] = block
                        used_count_ref[plane] = used_at + 1

                use(col // LANES)

                @pl.when(col % LANES > LANES - SUB)
                def _():
                    use(col // LANES + 1)

            return carry

        lax.fori_loop(0, per_source, enlist, 0)


def plan(placing):
    sources, _, per_source = placing.shape
    return pl.pallas_call(
        plan_kernel,
        out_shape=[
            jax.ShapeDtypeStruct((sources, W), jnp.int32),
            jax.ShapeDtypeStruct((sources, W, per_source), jnp.int32),
            jax.ShapeDtypeStruct((W,), jnp.int32),
            jax.ShapeDtypeStruct((W, BLOCKS), jnp.int32),
        ],
        in_specs=[SMEM],
        out_specs=[SMEM] * 4,
        scratch_shapes=[pltpu.SMEM((W * BLOCKS,), jnp.int32)],
        cost_estimate=pl.CostEstimate(flops=0, bytes_accessed=4 << 20, transcendentals=0),
    )(placing)


def place_kernel(placing_ref, count_ref, listed_ref, used_count_ref, used_ref, *rest):
    sources = count_ref.shape[0]
    arrays, out_ref, canvas, sem = rest[:sources], rest[sources + 1], rest[-2], rest[-1]
    comp_count = canvas.shape[1]
    per_array = listed_ref.shape[2] // arrays[0].shape[0]
    lane = lax.broadcasted_iota(jnp.int32, (SUB + SUBLANES, LANES), 1)

    def lanes_of(block):
        return pl.ds(pl.multiple_of(block * LANES, LANES), LANES)

    def out_copy(plane, block):
        return pltpu.make_async_copy(
            canvas.at[plane, :, pl.ds(SUB, TU), lanes_of(block)],
            out_ref.at[:, plane, :, lanes_of(block)],
            sem.at[plane, block],
        )

    def add_patch(source, plane, index):
        sub = listed_ref[source, plane, index]
        start = placing_ref[source, 0, sub]
        col = placing_ref[source, 2, sub]
        block = col // LANES
        shift = col % LANES
        at = pl.ds(pl.multiple_of(sub % per_array * SUB, SUB), SUB)
        patch = arrays[source][sub // per_array, at, :].astype(jnp.float32)
        if patch.shape[1] < LANES:
            patch = jnp.concatenate([patch] * (LANES // patch.shape[1]), axis=1)
        patch = jnp.concatenate([patch, jnp.zeros((SUBLANES, patch.shape[1]), jnp.float32)], axis=0)
        patch = pltpu.roll(patch, start % SUBLANES, 0)
        rows = pl.ds(pl.multiple_of(start // SUBLANES * SUBLANES, SUBLANES), SUB + SUBLANES)
        for comp in range(comp_count):
            turned = patch[:, comp // 2 * LANES : (comp // 2 + 1) * LANES]
            turned = pltpu.roll(turned, (shift + comp % 2 * SUB) % LANES, 1)
            here = (lane >= shift) & (lane < shift + SUB)
            canvas[plane, comp, rows, lanes_of(block)] += jnp.where(here, turned, 0.0)

            @pl.when(shift > LANES - SUB)
            def _():
                canvas[plane, comp, rows, lanes_of(block + 1)] += jnp.where(
                    lane < shift + SUB - LANES, turned, 0.0
                )

    for plane in range(W):

        def clear(index, carry, plane=plane):
            block = used_ref[plane, index]
            canvas[plane, :, pl.ds(SUB, TU), lanes_of(block)] = jnp.zeros((comp_count, TU, LANES), jnp.float32)
            return carry

        lax.fori_loop(0, used_count_ref[plane], clear, 0)
        for source in range(sources):

            def add(index, carry, plane=plane, source=source):
                add_patch(source, plane, index)
                return carry

            lax.fori_loop(0, count_ref[source, plane], add, 0)

        def send(index, carry, plane=plane):
            out_copy(plane, used_ref[plane, index]).start()
            return carry

        lax.fori_loop(0, used_count_ref[plane], send, 0)
    for plane in range(W):

        def finish(index, carry, plane=plane):
            out_copy(plane, used_ref[plane, index]).wait()
            return carry

        lax.fori_loop(0, used_count_ref[plane], finish, 0)


def place_all(arrays, placing, plans, tile_grid):
    comp_count = tile_grid.shape[0]
    return pl.pallas_call(
        place_kernel,
        out_shape=jax.ShapeDtypeStruct(tile_grid.shape, jnp.float32),
        in_specs=[SMEM] * 5 + [VMEM] * len(arrays) + [ANY],
        out_specs=ANY,
        scratch_shapes=[
            pltpu.VMEM((W, comp_count, TU + 2 * SUB, NV), jnp.float32),
            pltpu.SemaphoreType.DMA((W, BLOCKS)),
        ],
        input_output_aliases={5 + len(arrays): 0},
        compiler_params=pltpu.CompilerParams(vmem_limit_bytes=44 << 20),
        cost_estimate=pl.CostEstimate(flops=0, bytes_accessed=16 << 20, transcendentals=0),
    )(placing, *plans, *arrays, tile_grid)


def body(visibilities, positions, owner, w_plane, row_offset, col_offset):
    peers = lax.axis_size("tm")
    tiles = lax.axis_size("uv")
    sub_count = visibilities.shape[1]
    comp_count = visibilities.shape[0] // peers
    kept = comp_count * SUB
    tile = lax.axis_index("uv")
    half = sub_count // 2

    numbers = jnp.stack(
        [owner[:, 0], row_offset, w_plane, col_offset // LANES, col_offset % LANES], axis=0
    ).astype(jnp.float32)
    numbers = jnp.pad(numbers, ((0, META - 5), (0, kept - sub_count)))

    sent_a = grid_parts(visibilities, positions, peers, 0, half)
    parts_a = exchange(sent_a, "tm")
    sent_b = grid_parts(visibilities, positions, peers, 1, half)
    parts_b = exchange(sent_b, "tm")
    arrays_a = gather_all(sum_parts(parts_a, numbers), "uv")
    tile_grid = blank_tile(sent_b[0], comp_count)

    told = jnp.stack(arrays_a, axis=0)[:, :, half * SUB :, :sub_count].astype(jnp.float32).astype(jnp.int32)
    told = jnp.transpose(told, (2, 0, 1, 3))
    ahead = (told[0] - tile) % tiles
    starts = jnp.where(ahead == 0, told[1] + SUB, jnp.where(ahead == tiles - 1, told[1] + SUB - TU, -1))
    placing = jnp.stack([starts, told[2], told[3] * LANES + told[4]], axis=0)
    placing = jnp.transpose(placing, (1, 0, 2, 3))
    placing = jnp.concatenate(
        [
            placing[:, :, :, :half].reshape(2, 3, -1),
            placing[:, :, :, half:].reshape(2, 3, -1),
        ],
        axis=0,
    )
    plans = plan(placing)
    arrays_b = gather_all(sum_parts(parts_b, numbers), "uv")
    return place_all(arrays_a + arrays_b, placing, plans, tile_grid)


def solution(mesh):
    placed = (P(None, "uv", "tm"), P(None, "uv", "tm"), P("uv", None), P("uv"), P("uv"), P("uv"))
    return jax.shard_map(
        body, mesh=mesh, in_specs=placed, out_specs=P("tm", None, "uv", None), check_vma=False
    )
```

```python
import functools

import jax
import jax.numpy as jnp
from jax import lax
from jax.experimental import pallas as pl
from jax.experimental.pallas import tpu as pltpu
from jax.sharding import PartitionSpec as P

W = 8
SUB = 64
TAPS = 8
TU = 128
NV = 2048
LANES = 128
SUBLANES = 8
BLOCKS = NV // LANES
META = 16
STEP = 4

VMEM = pl.BlockSpec(memory_space=pltpu.VMEM)
SMEM = pl.BlockSpec(memory_space=pltpu.SMEM)
ANY = pl.BlockSpec(memory_space=pl.ANY)


def taper(scaled):
    inner = jnp.maximum(0.0, 1.0 - scaled * scaled)
    return inner * inner


def grid_kernel(values_ref, places_ref, *rest, blanks, orders):
    parts_ref, rest = rest[orders], rest[orders + 1 :]
    zero_copies = []
    if blanks:
        out_ref, values_wide, blank, sem = rest
        blank[...] = jnp.zeros(blank.shape, jnp.float32)
        zero_copies = [pltpu.make_async_copy(blank, out_ref.at[:, plane], sem.at[plane]) for plane in range(W)]
    else:
        (values_wide,) = rest
    for copy in zero_copies:
        copy.start()
    comp_count, sub_count, row_count = values_ref.shape
    peers, _, kept, _ = parts_ref.shape
    for comp in range(comp_count):
        values_wide[comp * sub_count : (comp + 1) * sub_count, :] = values_ref[comp].astype(jnp.float32)
    cells = lax.broadcasted_iota(jnp.int32, (SUB, row_count), 0).astype(jnp.float32) * (2.0 / TAPS)

    def one_sub(sub):
        row_taps = taper(cells - places_ref[0, pl.ds(sub, 1), :] * (2.0 / TAPS)).astype(jnp.bfloat16)
        col_taps = taper(cells - places_ref[1, pl.ds(sub, 1), :] * (2.0 / TAPS))
        weighted = jnp.concatenate(
            [
                (values_wide[pl.ds(comp * sub_count + sub, 1), :] * col_taps).astype(jnp.bfloat16)
                for comp in range(comp_count)
            ],
            axis=0,
        )
        return lax.dot_general(
            weighted, row_taps, (((1,), (1,)), ((), ())), preferred_element_type=jnp.float32
        )

    def some_subs(turn, carry):
        for pair in range(STEP // 2):
            sub = turn * STEP + pair * 2
            sums = jnp.concatenate([one_sub(sub), one_sub(sub + 1)], axis=1).astype(jnp.bfloat16)
            for peer in range(peers):
                parts_ref[peer, turn * (STEP // 2) + pair] = sums[peer * kept : (peer + 1) * kept]
        return carry

    lax.fori_loop(0, sub_count // STEP, some_subs, 0)
    for copy in zero_copies:
        copy.wait()


def grid_parts(values, places, peers, chunk, sub_count, blanks, *order):
    comp_count, _, row_count = values.shape
    kept = comp_count // peers * SUB
    parts_shape = (peers, sub_count // 2, kept, LANES)
    return pl.pallas_call(
        functools.partial(grid_kernel, blanks=blanks, orders=len(order)),
        grid=(1,),
        out_shape=[jax.ShapeDtypeStruct(parts_shape, jnp.bfloat16)]
        + [jax.ShapeDtypeStruct((kept // SUB, W, TU, NV), jnp.float32)] * blanks,
        in_specs=[
            pl.BlockSpec((comp_count, sub_count, row_count), lambda i: (0, chunk, 0)),
            pl.BlockSpec((2, sub_count, row_count), lambda i: (0, chunk, 0)),
        ]
        + [ANY] * len(order),
        out_specs=[pl.BlockSpec(parts_shape, lambda i: (0, 0, 0, 0))] + [ANY] * blanks,
        scratch_shapes=[pltpu.VMEM((comp_count * sub_count, row_count), jnp.float32)]
        + [pltpu.VMEM((kept // SUB, TU, NV), jnp.float32), pltpu.SemaphoreType.DMA((W,))] * blanks,
        compiler_params=pltpu.CompilerParams(vmem_limit_bytes=60 << 20),
        cost_estimate=pl.CostEstimate(
            flops=8 * sub_count * row_count * SUB * SUB * comp_count,
            bytes_accessed=2 << 20,
            transcendentals=0,
        ),
    )(values, places, *order)


def sum_kernel(parts_ref, order_ref, *rest):
    numbers_refs, out_ref = rest[:-1], rest[-1]
    peers, pairs, _, _ = parts_ref.shape
    for pair in range(pairs):
        total = parts_ref[0, pair].astype(jnp.float32)
        for peer in range(1, peers):
            total = total + parts_ref[peer, pair].astype(jnp.float32)
        out_ref[pair * 2 * SUB : (pair + 1) * 2 * SUB, :] = total.T.astype(jnp.bfloat16)
    for numbers_ref in numbers_refs:
        out_ref[pairs * 2 * SUB :, :] = numbers_ref[...].astype(jnp.bfloat16)


def sum_parts(parts, order, *numbers):
    _, pairs, kept, _ = parts.shape
    return pl.pallas_call(
        sum_kernel,
        out_shape=jax.ShapeDtypeStruct((pairs * 2 * SUB + META * len(numbers), kept), jnp.bfloat16),
        in_specs=[VMEM, ANY] + [VMEM] * len(numbers),
        out_specs=VMEM,
        compiler_params=pltpu.CompilerParams(vmem_limit_bytes=8 << 20),
        cost_estimate=pl.CostEstimate(flops=1 << 20, bytes_accessed=2 << 20, transcendentals=0),
    )(parts, order, *numbers)


def gather_all(array, axis):
    size = lax.axis_size(axis)
    near = [array] + [
        lax.ppermute(array, axis, [(i, i ^ mask) for i in range(size)]) for mask in range(2, size, 2)
    ]
    near = jnp.stack(near, axis=0)
    other = lax.ppermute(near, axis, [(i, i ^ 1) for i in range(size)])
    return [near, other]


def touch_plan(starts, planes, cols):
    total = starts.shape[0]
    ids = jnp.arange(total, dtype=jnp.int32)
    taken = starts >= 0
    keys = jnp.where(taken, planes, W) * total + ids
    left = jnp.where(taken, planes * BLOCKS + cols // LANES, -1)
    right = jnp.where(taken & (cols % LANES > LANES - SUB), left + 1, -2)
    before = keys[None, :] < keys[:, None]
    after = keys[None, :] > keys[:, None]
    rank = jnp.sum(before.astype(jnp.int32), axis=1)

    def edges(units):
        same = (left[None, :] == units[:, None]) | (right[None, :] == units[:, None])
        first = ~jnp.any(same & before, axis=1)
        last = ~jnp.any(same & after, axis=1)
        return first.astype(jnp.int32) + 2 * last.astype(jnp.int32)

    flags = edges(left) + jnp.where(right >= 0, 4 * edges(right), 0)
    fields = jnp.stack([starts, cols, planes, ids, flags], axis=0)
    moved = jnp.where(rank[None, None, :] == ids[None, :, None], fields[:, None, :], 0)
    table = jnp.sum(moved, axis=2)
    number = jnp.sum(taken.astype(jnp.int32))
    return jnp.concatenate([table, jnp.full((1, total), number, jnp.int32)], axis=0)


def place_kernel(table_ref, *rest):
    arrays, out_ref, canvas, sem = rest[:-4], rest[-3], rest[-2], rest[-1]
    comp_count = canvas.shape[1]
    blocks = arrays[0].shape[0]
    half = arrays[2].shape[1] // SUB
    sub_count = 2 * half
    lane = lax.broadcasted_iota(jnp.int32, (SUB + SUBLANES, LANES), 1)

    def lanes_of(block):
        return pl.ds(pl.multiple_of(block * LANES, LANES), LANES)

    def out_copy(plane, block):
        return pltpu.make_async_copy(
            canvas.at[plane, :, pl.ds(SUB, TU), lanes_of(block)],
            out_ref.at[:, plane, :, lanes_of(block)],
            sem.at[plane, block],
        )

    def clear(plane, block):
        canvas[plane, :, pl.ds(SUB, TU), lanes_of(block)] = jnp.zeros((comp_count, TU, LANES), jnp.float32)

    def when_set(flags, bit, act):
        @pl.when((flags & bit) != 0)
        def _():
            act()

    def add_patch(index, carry):
        start = table_ref[0, index]
        col = table_ref[1, index]
        plane = table_ref[2, index]
        sub = table_ref[3, index]
        flags = table_ref[4, index]
        block = col // LANES
        shift = col % LANES
        holder = sub // sub_count
        local = sub % sub_count
        source = local // half * 2 + holder // blocks
        at = pl.ds(pl.multiple_of(local % half * SUB, SUB), SUB)

        def from_array(array):
            return lambda: array[holder % blocks, at, :].astype(jnp.float32)

        patch = lax.switch(source, [from_array(array) for array in arrays])
        if patch.shape[1] < LANES:
            patch = jnp.concatenate([patch] * (LANES // patch.shape[1]), axis=1)
        patch = jnp.concatenate([patch, jnp.zeros((SUBLANES, patch.shape[1]), jnp.float32)], axis=0)
        patch = pltpu.roll(patch, start % SUBLANES, 0)
        rows = pl.ds(pl.multiple_of(start // SUBLANES * SUBLANES, SUBLANES), SUB + SUBLANES)
        turned = [
            pltpu.roll(
                patch[:, comp // 2 * LANES : (comp // 2 + 1) * LANES], (shift + comp % 2 * SUB) % LANES, 1
            )
            for comp in range(comp_count)
        ]
        when_set(flags, 1, lambda: clear(plane, block))
        here = (lane >= shift) & (lane < shift + SUB)
        for comp in range(comp_count):
            canvas[plane, comp, rows, lanes_of(block)] += jnp.where(here, turned[comp], 0.0)
        when_set(flags, 2, lambda: out_copy(plane, block).start())

        @pl.when(shift > LANES - SUB)
        def _():
            when_set(flags, 4, lambda: clear(plane, block + 1))
            for comp in range(comp_count):
                canvas[plane, comp, rows, lanes_of(block + 1)] += jnp.where(
                    lane < shift + SUB - LANES, turned[comp], 0.0
                )
            when_set(flags, 8, lambda: out_copy(plane, block + 1).start())

        return carry

    def finish(index, carry):
        block = table_ref[1, index] // LANES
        plane = table_ref[2, index]
        flags = table_ref[4, index]
        when_set(flags, 2, lambda: out_copy(plane, block).wait())
        when_set(flags, 8, lambda: out_copy(plane, block + 1).wait())
        return carry

    lax.fori_loop(0, table_ref[5, 0], add_patch, 0)
    lax.fori_loop(0, table_ref[5, 0], finish, 0)


def place_all(arrays, table, tile_grid):
    comp_count = tile_grid.shape[0]
    return pl.pallas_call(
        place_kernel,
        out_shape=jax.ShapeDtypeStruct(tile_grid.shape, jnp.float32),
        in_specs=[SMEM] + [VMEM] * len(arrays) + [ANY],
        out_specs=ANY,
        scratch_shapes=[
            pltpu.VMEM((W, comp_count, TU + 2 * SUB, NV), jnp.float32),
            pltpu.SemaphoreType.DMA((W, BLOCKS)),
        ],
        input_output_aliases={1 + len(arrays): 0},
        compiler_params=pltpu.CompilerParams(vmem_limit_bytes=44 << 20),
        cost_estimate=pl.CostEstimate(flops=0, bytes_accessed=16 << 20, transcendentals=0),
    )(table, *arrays, tile_grid)


def body(visibilities, positions, owner, w_plane, row_offset, col_offset):
    peers = lax.axis_size("tm")
    tiles = lax.axis_size("uv")
    sub_count = visibilities.shape[1]
    comp_count = visibilities.shape[0] // peers
    kept = comp_count * SUB
    tile = lax.axis_index("uv")
    half = sub_count // 2

    numbers = jnp.stack(
        [owner[:, 0], row_offset, w_plane, col_offset // LANES, col_offset % LANES], axis=0
    ).astype(jnp.float32)
    numbers = jnp.pad(numbers, ((0, META - 5), (0, kept - sub_count)))

    sent_a, tile_grid = grid_parts(visibilities, positions, peers, 0, half, True)
    parts_a = lax.all_to_all(sent_a, "tm", split_axis=0, concat_axis=0, tiled=True)
    (sent_b,) = grid_parts(visibilities, positions, peers, 1, half, False, sent_a)
    parts_b = lax.all_to_all(sent_b, "tm", split_axis=0, concat_axis=0, tiled=True)
    arrays_a = gather_all(sum_parts(parts_a, sent_b, numbers), "uv")

    told = jnp.stack(arrays_a, axis=0)[:, :, half * SUB :, :sub_count].astype(jnp.float32).astype(jnp.int32)
    told = jnp.transpose(told, (2, 0, 1, 3)).reshape(META, -1)
    ahead = (told[0] - tile) % tiles
    starts = jnp.where(ahead == 0, told[1] + SUB, jnp.where(ahead == tiles - 1, told[1] + SUB - TU, -1))
    table = touch_plan(starts, told[2], told[3] * LANES + told[4])
    arrays_b = gather_all(sum_parts(parts_b, arrays_a[1]), "uv")
    return place_all(arrays_a + arrays_b, table, tile_grid)


def solution(mesh):
    placed = (P(None, "uv", "tm"), P(None, "uv", "tm"), P("uv", None), P("uv"), P("uv"), P("uv"))
    return jax.shard_map(
        body, mesh=mesh, in_specs=placed, out_specs=P("tm", None, "uv", None), check_vma=False
    )
```

```python
import functools

import jax
import jax.numpy as jnp
from jax import lax
from jax.experimental import pallas as pl
from jax.experimental.pallas import tpu as pltpu
from jax.sharding import PartitionSpec as P

W = 8
SUB = 64
TAPS = 8
TU = 128
NV = 2048
LANES = 128
SUBLANES = 8
BLOCKS = NV // LANES
META = 16
STEP = 4

VMEM = pl.BlockSpec(memory_space=pltpu.VMEM)
SMEM = pl.BlockSpec(memory_space=pltpu.SMEM)
ANY = pl.BlockSpec(memory_space=pl.ANY)


def taper(scaled):
    inner = jnp.maximum(0.0, 1.0 - scaled * scaled)
    return inner * inner


def grid_kernel(me_ref, values_ref, places_ref, *rest, peers, blanks, orders):
    parts_refs, rest = rest[orders : orders + peers], rest[orders + peers :]
    zero_copies = []
    if blanks:
        out_ref, values_wide, sums, blank, sem, values, places, in_sem = rest
        _, sub_count, row_count = values.shape
        in_copies = [
            pltpu.make_async_copy(values_ref.at[:, pl.ds(0, sub_count), :], values, in_sem.at[0]),
            pltpu.make_async_copy(places_ref.at[:, pl.ds(0, sub_count), :], places, in_sem.at[1]),
        ]
        for copy in in_copies:
            copy.start()
        blank[...] = jnp.zeros(blank.shape, jnp.float32)
        zero_copies = [pltpu.make_async_copy(blank, out_ref.at[:, plane], sem.at[plane]) for plane in range(W)]
        for copy in in_copies:
            copy.wait()
        values_ref, places_ref = values, places
    else:
        values_wide, sums = rest
    for copy in zero_copies:
        copy.start()
    comp_count, sub_count, row_count = values_ref.shape
    kept = comp_count // peers * SUB
    for comp in range(comp_count):
        values_wide[comp * sub_count : (comp + 1) * sub_count, :] = values_ref[comp].astype(jnp.float32)
    cells = lax.broadcasted_iota(jnp.int32, (SUB, row_count), 0).astype(jnp.float32) * (2.0 / TAPS)

    def one_sub(sub):
        row_taps = taper(cells - places_ref[0, pl.ds(sub, 1), :] * (2.0 / TAPS)).astype(jnp.bfloat16)
        col_taps = taper(cells - places_ref[1, pl.ds(sub, 1), :] * (2.0 / TAPS))
        weighted = jnp.concatenate(
            [
                (values_wide[pl.ds(comp * sub_count + sub, 1), :] * col_taps).astype(jnp.bfloat16)
                for comp in range(comp_count)
            ],
            axis=0,
        )
        return lax.dot_general(
            weighted, row_taps, (((1,), (1,)), ((), ())), preferred_element_type=jnp.float32
        )

    def some_subs(turn, carry):
        for pair in range(STEP // 2):
            sub = turn * STEP + pair * 2
            sums[pair] = jnp.concatenate([one_sub(sub), one_sub(sub + 1)], axis=1).astype(jnp.bfloat16)
        for pair in range(STEP // 2):
            for mask, parts_ref in enumerate(parts_refs):
                rows = pl.ds(pl.multiple_of((me_ref[0] ^ mask) * kept, kept), kept)
                parts_ref[turn * (STEP // 2) + pair] = sums[pair, rows, :]
        return carry

    lax.fori_loop(0, sub_count // STEP, some_subs, 0)
    for copy in zero_copies:
        copy.wait()


def grid_parts(values, places, peers, chunk, sub_count, blanks, *order):
    comp_count, _, row_count = values.shape
    kept = comp_count // peers * SUB
    me = lax.axis_index("tm").astype(jnp.int32).reshape(1)
    parts_shape = (sub_count // 2, kept, LANES)
    values_block, places_block = (comp_count, sub_count, row_count), (2, sub_count, row_count)
    if blanks:
        in_specs = [ANY] * 2
    else:
        in_specs = [pl.BlockSpec(block, lambda i: (0, chunk, 0)) for block in (values_block, places_block)]
    scratch = [
        pltpu.VMEM((comp_count * sub_count, row_count), jnp.float32),
        pltpu.VMEM((STEP // 2, comp_count * SUB, LANES), jnp.bfloat16),
    ]
    if blanks:
        scratch += [
            pltpu.VMEM((kept // SUB, TU, NV), jnp.float32),
            pltpu.SemaphoreType.DMA((W,)),
            pltpu.VMEM(values_block, values.dtype),
            pltpu.VMEM(places_block, places.dtype),
            pltpu.SemaphoreType.DMA((2,)),
        ]
    return pl.pallas_call(
        functools.partial(grid_kernel, peers=peers, blanks=blanks, orders=len(order)),
        grid=(1,),
        out_shape=[jax.ShapeDtypeStruct(parts_shape, jnp.bfloat16)] * peers
        + [jax.ShapeDtypeStruct((kept // SUB, W, TU, NV), jnp.float32)] * blanks,
        in_specs=[SMEM] + in_specs + [ANY] * len(order),
        out_specs=[pl.BlockSpec(parts_shape, lambda i: (0, 0, 0))] * peers + [ANY] * blanks,
        scratch_shapes=scratch,
        compiler_params=pltpu.CompilerParams(vmem_limit_bytes=(60 if blanks else 48) << 20),
        cost_estimate=pl.CostEstimate(
            flops=8 * sub_count * row_count * SUB * SUB * comp_count,
            bytes_accessed=2 << 20,
            transcendentals=0,
        ),
    )(me, values, places, *order)


def sum_kernel(*refs, peers, hops, orders):
    parts_refs, hops_refs, rest = refs[:peers], refs[peers : peers + hops], refs[peers + hops + orders :]
    pairs = parts_refs[0].shape[0]
    out_ref = rest[0] if hops else rest[1]
    for pair in range(pairs):
        total = parts_refs[0][pair].astype(jnp.float32)
        for parts_ref in parts_refs[1:]:
            total = total + parts_ref[pair].astype(jnp.float32)
        out_ref[pair * 2 * SUB : (pair + 1) * 2 * SUB, :] = total.T.astype(jnp.bfloat16)
    if hops:
        for at, hop_ref in enumerate(hops_refs):
            rest[1][at] = hop_ref[...]
    else:
        out_ref[pairs * 2 * SUB :, :] = rest[0][...].astype(jnp.bfloat16)


def sum_parts(parts, hops, order, *numbers):
    pairs, kept, _ = parts[0].shape
    rows = pairs * 2 * SUB + META * len(numbers)
    return pl.pallas_call(
        functools.partial(sum_kernel, peers=len(parts), hops=len(hops), orders=len(order)),
        out_shape=[jax.ShapeDtypeStruct((rows, kept), jnp.bfloat16)]
        + [jax.ShapeDtypeStruct((len(hops),) + hop.shape, hop.dtype) for hop in hops[:1]],
        in_specs=[VMEM] * (len(parts) + len(hops)) + [ANY] * len(order) + [VMEM] * len(numbers),
        out_specs=[VMEM] * (1 + len(hops[:1])),
        compiler_params=pltpu.CompilerParams(vmem_limit_bytes=8 << 20),
        cost_estimate=pl.CostEstimate(flops=1 << 20, bytes_accessed=2 << 20, transcendentals=0),
    )(*parts, *hops, *order, *numbers)


def exchange(parts, axis):
    size = lax.axis_size(axis)
    far_first = [
        lax.ppermute(parts[mask], axis, [(i, i ^ mask) for i in range(size)]) for mask in range(size - 1, 0, -1)
    ]
    return [parts[0]] + far_first


def across(array, axis):
    size = lax.axis_size(axis)
    return [array] + [lax.ppermute(array, axis, [(i, i ^ mask) for i in range(size)]) for mask in range(2, size, 2)]


def beside(array, axis):
    size = lax.axis_size(axis)
    return lax.ppermute(array, axis, [(i, i ^ 1) for i in range(size)])


def touch_plan(starts, planes, cols):
    total = starts.shape[0]
    ids = jnp.arange(total, dtype=jnp.int32)
    taken = starts >= 0
    keys = jnp.where(taken, planes, W) * total + ids
    left = jnp.where(taken, planes * BLOCKS + cols // LANES, -1)
    right = jnp.where(taken & (cols % LANES > LANES - SUB), left + 1, -2)
    before = keys[None, :] < keys[:, None]
    after = keys[None, :] > keys[:, None]
    rank = jnp.sum(before.astype(jnp.int32), axis=1)

    def edges(units):
        same = (left[None, :] == units[:, None]) | (right[None, :] == units[:, None])
        first = ~jnp.any(same & before, axis=1)
        last = ~jnp.any(same & after, axis=1)
        return first.astype(jnp.int32) + 2 * last.astype(jnp.int32)

    flags = edges(left) + jnp.where(right >= 0, 4 * edges(right), 0)
    fields = jnp.stack([starts, cols, planes, ids, flags], axis=0)
    moved = jnp.where(rank[None, None, :] == ids[None, :, None], fields[:, None, :], 0)
    table = jnp.sum(moved, axis=2)
    number = jnp.sum(taken.astype(jnp.int32))
    return jnp.concatenate([table, jnp.full((1, total), number, jnp.int32)], axis=0)


def place_kernel(table_ref, *rest):
    arrays, out_ref, canvas, sem = rest[:-4], rest[-3], rest[-2], rest[-1]
    comp_count = canvas.shape[1]
    blocks = arrays[0].shape[0]
    half = arrays[2].shape[1] // SUB
    sub_count = 2 * half
    lane = lax.broadcasted_iota(jnp.int32, (SUB + SUBLANES, LANES), 1)

    def lanes_of(block):
        return pl.ds(pl.multiple_of(block * LANES, LANES), LANES)

    def out_copy(plane, block):
        return pltpu.make_async_copy(
            canvas.at[plane, :, pl.ds(SUB, TU), lanes_of(block)],
            out_ref.at[:, plane, :, lanes_of(block)],
            sem.at[plane, block],
        )

    def clear(plane, block):
        canvas[plane, :, pl.ds(SUB, TU), lanes_of(block)] = jnp.zeros((comp_count, TU, LANES), jnp.float32)

    def when_set(flags, bit, act):
        @pl.when((flags & bit) != 0)
        def _():
            act()

    def add_patch(index, carry):
        start = table_ref[0, index]
        col = table_ref[1, index]
        plane = table_ref[2, index]
        sub = table_ref[3, index]
        flags = table_ref[4, index]
        block = col // LANES
        shift = col % LANES
        holder = sub // sub_count
        local = sub % sub_count
        source = local // half * 2 + holder // blocks
        at = pl.ds(pl.multiple_of(local % half * SUB, SUB), SUB)

        def from_array(array):
            return lambda: array[holder % blocks, at, :].astype(jnp.float32)

        patch = lax.switch(source, [from_array(array) for array in arrays])
        if patch.shape[1] < LANES:
            patch = jnp.concatenate([patch] * (LANES // patch.shape[1]), axis=1)
        patch = jnp.concatenate([patch, jnp.zeros((SUBLANES, patch.shape[1]), jnp.float32)], axis=0)
        patch = pltpu.roll(patch, start % SUBLANES, 0)
        rows = pl.ds(pl.multiple_of(start // SUBLANES * SUBLANES, SUBLANES), SUB + SUBLANES)
        turned = [
            pltpu.roll(
                patch[:, comp // 2 * LANES : (comp // 2 + 1) * LANES], (shift + comp % 2 * SUB) % LANES, 1
            )
            for comp in range(comp_count)
        ]
        when_set(flags, 1, lambda: clear(plane, block))
        here = (lane >= shift) & (lane < shift + SUB)
        for comp in range(comp_count):
            canvas[plane, comp, rows, lanes_of(block)] += jnp.where(here, turned[comp], 0.0)
        when_set(flags, 2, lambda: out_copy(plane, block).start())

        @pl.when(shift > LANES - SUB)
        def _():
            when_set(flags, 4, lambda: clear(plane, block + 1))
            for comp in range(comp_count):
                canvas[plane, comp, rows, lanes_of(block + 1)] += jnp.where(
                    lane < shift + SUB - LANES, turned[comp], 0.0
                )
            when_set(flags, 8, lambda: out_copy(plane, block + 1).start())

        return carry

    def finish(index, carry):
        block = table_ref[1, index] // LANES
        plane = table_ref[2, index]
        flags = table_ref[4, index]
        when_set(flags, 2, lambda: out_copy(plane, block).wait())
        when_set(flags, 8, lambda: out_copy(plane, block + 1).wait())
        return carry

    lax.fori_loop(0, table_ref[5, 0], add_patch, 0)
    lax.fori_loop(0, table_ref[5, 0], finish, 0)


def place_all(arrays, table, tile_grid):
    comp_count = tile_grid.shape[0]
    return pl.pallas_call(
        place_kernel,
        out_shape=jax.ShapeDtypeStruct(tile_grid.shape, jnp.float32),
        in_specs=[SMEM] + [VMEM] * len(arrays) + [ANY],
        out_specs=ANY,
        scratch_shapes=[
            pltpu.VMEM((W, comp_count, TU + 2 * SUB, NV), jnp.float32),
            pltpu.SemaphoreType.DMA((W, BLOCKS)),
        ],
        input_output_aliases={1 + len(arrays): 0},
        compiler_params=pltpu.CompilerParams(vmem_limit_bytes=44 << 20),
        cost_estimate=pl.CostEstimate(flops=0, bytes_accessed=16 << 20, transcendentals=0),
    )(table, *arrays, tile_grid)


def body(visibilities, positions, owner, w_plane, row_offset, col_offset):
    peers = lax.axis_size("tm")
    tiles = lax.axis_size("uv")
    sub_count = visibilities.shape[1]
    comp_count = visibilities.shape[0] // peers
    kept = comp_count * SUB
    tile = lax.axis_index("uv")
    half = sub_count // 2

    numbers = jnp.stack(
        [owner[:, 0], row_offset, w_plane, col_offset // LANES, col_offset % LANES], axis=0
    ).astype(jnp.float32)
    numbers = jnp.pad(numbers, ((0, META - 5), (0, kept - sub_count)))

    *sent_a, tile_grid = grid_parts(visibilities, positions, peers, 0, half, True)
    parts_a = exchange(sent_a, "tm")
    sent_b = grid_parts(visibilities, positions, peers, 1, half, False, sent_a[0])
    parts_b = exchange(sent_b, "tm")
    (sum_a,) = sum_parts(parts_a, [], sent_b[:1], numbers)
    hops_a = across(sum_a, "uv")
    sum_b, near_a = sum_parts(parts_b, hops_a, [])
    other_a = beside(near_a, "uv")

    told = jnp.stack([near_a, other_a], axis=0)[:, :, half * SUB :, :sub_count].astype(jnp.float32).astype(jnp.int32)
    told = jnp.transpose(told, (2, 0, 1, 3)).reshape(META, -1)
    ahead = (told[0] - tile) % tiles
    starts = jnp.where(ahead == 0, told[1] + SUB, jnp.where(ahead == tiles - 1, told[1] + SUB - TU, -1))
    table = touch_plan(starts, told[2], told[3] * LANES + told[4])
    near_b = jnp.stack(across(sum_b, "uv"), axis=0)
    other_b = beside(near_b, "uv")
    return place_all([near_a, other_a, near_b, other_b], table, tile_grid)


def solution(mesh):
    placed = (P(None, "uv", "tm"), P(None, "uv", "tm"), P("uv", None), P("uv"), P("uv"), P("uv"))
    return jax.shard_map(
        body, mesh=mesh, in_specs=placed, out_specs=P("tm", None, "uv", None), check_vma=False
    )
```

```python
import functools

import jax
import jax.numpy as jnp
from jax import lax
from jax.experimental import pallas as pl
from jax.experimental.pallas import tpu as pltpu
from jax.sharding import PartitionSpec as P

W = 8
SUB = 64
TAPS = 8
TU = 128
NV = 2048
LANES = 128
SUBLANES = 8
BLOCKS = NV // LANES
META = 16
STEP = 4

VMEM = pl.BlockSpec(memory_space=pltpu.VMEM)
SMEM = pl.BlockSpec(memory_space=pltpu.SMEM)
ANY = pl.BlockSpec(memory_space=pl.ANY)


def taper(scaled):
    inner = jnp.maximum(0.0, 1.0 - scaled * scaled)
    return inner * inner


def grid_kernel(me_ref, values_ref, places_ref, *rest, peers, blanks, orders):
    parts_refs, rest = rest[orders : orders + peers], rest[orders + peers :]
    zero_copies = []
    if blanks:
        out_ref, values_wide, sums, blank, sem, values, places, in_sem = rest
        _, sub_count, row_count = values.shape
        in_copies = [
            pltpu.make_async_copy(values_ref.at[:, pl.ds(0, sub_count), :], values, in_sem.at[0]),
            pltpu.make_async_copy(places_ref.at[:, pl.ds(0, sub_count), :], places, in_sem.at[1]),
        ]
        for copy in in_copies:
            copy.start()
        blank[...] = jnp.zeros(blank.shape, jnp.float32)
        zero_copies = [pltpu.make_async_copy(blank, out_ref.at[:, plane], sem.at[plane]) for plane in range(W)]
        for copy in in_copies:
            copy.wait()
        values_ref, places_ref = values, places
    else:
        values_wide, sums = rest
    for copy in zero_copies:
        copy.start()
    comp_count, sub_count, row_count = values_ref.shape
    kept = comp_count // peers * SUB
    for comp in range(comp_count):
        values_wide[comp * sub_count : (comp + 1) * sub_count, :] = values_ref[comp].astype(jnp.float32)
    cells = lax.broadcasted_iota(jnp.int32, (SUB, row_count), 0).astype(jnp.float32) * (2.0 / TAPS)

    def one_sub(sub):
        row_taps = taper(cells - places_ref[0, pl.ds(sub, 1), :] * (2.0 / TAPS)).astype(jnp.bfloat16)
        col_taps = taper(cells - places_ref[1, pl.ds(sub, 1), :] * (2.0 / TAPS))
        weighted = jnp.concatenate(
            [
                (values_wide[pl.ds(comp * sub_count + sub, 1), :] * col_taps).astype(jnp.bfloat16)
                for comp in range(comp_count)
            ],
            axis=0,
        )
        return lax.dot_general(
            weighted, row_taps, (((1,), (1,)), ((), ())), preferred_element_type=jnp.float32
        )

    def some_subs(turn, carry):
        for pair in range(STEP // 2):
            sub = turn * STEP + pair * 2
            sums[pair] = jnp.concatenate([one_sub(sub), one_sub(sub + 1)], axis=1).astype(jnp.bfloat16)
        for pair in range(STEP // 2):
            for mask, parts_ref in enumerate(parts_refs):
                rows = pl.ds(pl.multiple_of((me_ref[0] ^ mask) * kept, kept), kept)
                parts_ref[turn * (STEP // 2) + pair] = sums[pair, rows, :]
        return carry

    lax.fori_loop(0, sub_count // STEP, some_subs, 0)
    for copy in zero_copies:
        copy.wait()


def grid_parts(values, places, peers, chunk, sub_count, blanks, *order):
    comp_count, _, row_count = values.shape
    kept = comp_count // peers * SUB
    me = lax.axis_index("tm").astype(jnp.int32).reshape(1)
    parts_shape = (sub_count // 2, kept, LANES)
    values_block, places_block = (comp_count, sub_count, row_count), (2, sub_count, row_count)
    if blanks:
        in_specs = [ANY] * 2
    else:
        in_specs = [pl.BlockSpec(block, lambda i: (0, chunk, 0)) for block in (values_block, places_block)]
    scratch = [
        pltpu.VMEM((comp_count * sub_count, row_count), jnp.float32),
        pltpu.VMEM((STEP // 2, comp_count * SUB, LANES), jnp.bfloat16),
    ]
    if blanks:
        scratch += [
            pltpu.VMEM((kept // SUB, TU, NV), jnp.float32),
            pltpu.SemaphoreType.DMA((W,)),
            pltpu.VMEM(values_block, values.dtype),
            pltpu.VMEM(places_block, places.dtype),
            pltpu.SemaphoreType.DMA((2,)),
        ]
    return pl.pallas_call(
        functools.partial(grid_kernel, peers=peers, blanks=blanks, orders=len(order)),
        grid=(1,),
        out_shape=[jax.ShapeDtypeStruct(parts_shape, jnp.bfloat16)] * peers
        + [jax.ShapeDtypeStruct((kept // SUB, W, TU, NV), jnp.float32)] * blanks,
        in_specs=[SMEM] + in_specs + [ANY] * len(order),
        out_specs=[pl.BlockSpec(parts_shape, lambda i: (0, 0, 0))] * peers + [ANY] * blanks,
        scratch_shapes=scratch,
        compiler_params=pltpu.CompilerParams(vmem_limit_bytes=(60 if blanks else 48) << 20),
        cost_estimate=pl.CostEstimate(
            flops=8 * sub_count * row_count * SUB * SUB * comp_count,
            bytes_accessed=2 << 20,
            transcendentals=0,
        ),
    )(me, values, places, *order)


def sum_kernel(*refs, peers, hops, orders):
    parts_refs, hops_refs, rest = refs[:peers], refs[peers : peers + hops], refs[peers + hops + orders :]
    pairs = parts_refs[0].shape[0]
    out_ref = rest[0] if hops else rest[1]
    for pair in range(pairs):
        total = parts_refs[0][pair].astype(jnp.float32)
        for parts_ref in parts_refs[1:]:
            total = total + parts_ref[pair].astype(jnp.float32)
        out_ref[pair * 2 * SUB : (pair + 1) * 2 * SUB, :] = total.T.astype(jnp.bfloat16)
    if hops:
        for at, hop_ref in enumerate(hops_refs):
            rest[1][at] = hop_ref[: rest[1].shape[1], :]
    else:
        out_ref[pairs * 2 * SUB :, :] = rest[0][...].astype(jnp.bfloat16)


def sum_parts(parts, hops, order, *numbers):
    pairs, kept, _ = parts[0].shape
    rows = pairs * 2 * SUB + META * len(numbers)
    return pl.pallas_call(
        functools.partial(sum_kernel, peers=len(parts), hops=len(hops), orders=len(order)),
        out_shape=[jax.ShapeDtypeStruct((rows, kept), jnp.bfloat16)]
        + [jax.ShapeDtypeStruct((len(hops), rows, kept), jnp.bfloat16)] * len(hops[:1]),
        in_specs=[VMEM] * (len(parts) + len(hops)) + [ANY] * len(order) + [VMEM] * len(numbers),
        out_specs=[VMEM] * (1 + len(hops[:1])),
        compiler_params=pltpu.CompilerParams(vmem_limit_bytes=8 << 20),
        cost_estimate=pl.CostEstimate(flops=1 << 20, bytes_accessed=2 << 20, transcendentals=0),
    )(*parts, *hops, *order, *numbers)


def exchange(parts, axis):
    size = lax.axis_size(axis)
    far_first = [
        lax.ppermute(parts[mask], axis, [(i, i ^ mask) for i in range(size)]) for mask in range(size - 1, 0, -1)
    ]
    return [parts[0]] + far_first


def across(array, axis):
    size = lax.axis_size(axis)
    return [array] + [lax.ppermute(array, axis, [(i, i ^ mask) for i in range(size)]) for mask in range(2, size, 2)]


def beside(array, axis):
    size = lax.axis_size(axis)
    return lax.ppermute(array, axis, [(i, i ^ 1) for i in range(size)])


def touch_plan(starts, planes, cols, spots, others):
    total = starts.shape[0]
    ids = jnp.arange(total, dtype=jnp.int32)
    taken = starts >= 0
    keys = jnp.where(taken, planes, W) * total + ids
    left = jnp.where(taken, planes * BLOCKS + cols // LANES, -1)
    right = jnp.where(taken & (cols % LANES > LANES - SUB), left + 1, -2)
    before = keys[None, :] < keys[:, None]
    after = keys[None, :] > keys[:, None]
    rank = jnp.sum(before.astype(jnp.int32), axis=1)

    def edges(units):
        same = (left[None, :] == units[:, None]) | (right[None, :] == units[:, None])
        first = ~jnp.any(same & before, axis=1)
        last = ~jnp.any(same & after, axis=1)
        return first.astype(jnp.int32) + 2 * last.astype(jnp.int32)

    flags = edges(left) + jnp.where(right >= 0, 4 * edges(right), 0) + 16 * others
    fields = jnp.stack([starts, cols, planes, spots, flags], axis=0)
    moved = jnp.where(rank[None, None, :] == ids[None, :, None], fields[:, None, :], 0)
    table = jnp.sum(moved, axis=2)
    number = jnp.sum(taken.astype(jnp.int32))
    return jnp.concatenate([table, jnp.full((1, total), number, jnp.int32)], axis=0)


def place_kernel(table_ref, near_ref, other_ref, _, out_ref, canvas, sem):
    comp_count = canvas.shape[1]
    number = table_ref[5, 0]
    lane = lax.broadcasted_iota(jnp.int32, (SUB + SUBLANES, LANES), 1)

    def lanes_of(block):
        return pl.ds(pl.multiple_of(block * LANES, LANES), LANES)

    def out_copy(plane, block):
        return pltpu.make_async_copy(
            canvas.at[plane, :, pl.ds(SUB, TU), lanes_of(block)],
            out_ref.at[:, plane, :, lanes_of(block)],
            sem.at[plane, block],
        )

    def clear(plane, block):
        canvas[plane, :, pl.ds(SUB, TU), lanes_of(block)] = jnp.zeros((comp_count, TU, LANES), jnp.float32)

    def when_set(flags, bit, act):
        @pl.when((flags & bit) != 0)
        def _():
            act()

    def turn(index):
        start = table_ref[0, index]
        col = table_ref[1, index]
        block = table_ref[3, index] // (1 << 16)
        at = pl.ds(pl.multiple_of(table_ref[3, index] % (1 << 16), SUB), SUB)
        shift = col % LANES
        patch = jnp.where((table_ref[4, index] & 16) != 0, other_ref[block, at, :], near_ref[block, at, :])
        patch = patch.astype(jnp.float32)
        if patch.shape[1] < LANES:
            patch = jnp.concatenate([patch] * (LANES // patch.shape[1]), axis=1)
        patch = jnp.concatenate([patch, jnp.zeros((SUBLANES, patch.shape[1]), jnp.float32)], axis=0)
        patch = pltpu.roll(patch, start % SUBLANES, 0)
        return [
            pltpu.roll(
                patch[:, comp // 2 * LANES : (comp // 2 + 1) * LANES], (shift + comp % 2 * SUB) % LANES, 1
            )
            for comp in range(comp_count)
        ]

    def add_patch(index, turned):
        start = table_ref[0, index]
        col = table_ref[1, index]
        plane = table_ref[2, index]
        flags = table_ref[4, index]
        block = col // LANES
        shift = col % LANES
        rows = pl.ds(pl.multiple_of(start // SUBLANES * SUBLANES, SUBLANES), SUB + SUBLANES)
        when_set(flags, 1, lambda: clear(plane, block))
        here = (lane >= shift) & (lane < shift + SUB)
        for comp in range(comp_count):
            canvas[plane, comp, rows, lanes_of(block)] += jnp.where(here, turned[comp], 0.0)
        when_set(flags, 2, lambda: out_copy(plane, block).start())

        @pl.when(shift > LANES - SUB)
        def _():
            when_set(flags, 4, lambda: clear(plane, block + 1))
            for comp in range(comp_count):
                canvas[plane, comp, rows, lanes_of(block + 1)] += jnp.where(
                    lane < shift + SUB - LANES, turned[comp], 0.0
                )
            when_set(flags, 8, lambda: out_copy(plane, block + 1).start())

    def add_two(turn_index, carry):
        index = turn_index * 2
        first, second = turn(index), turn(index + 1)
        add_patch(index, first)

        @pl.when(index + 1 < number)
        def _():
            add_patch(index + 1, second)

        return carry

    def finish(index, carry):
        block = table_ref[1, index] // LANES
        plane = table_ref[2, index]
        flags = table_ref[4, index]
        when_set(flags, 2, lambda: out_copy(plane, block).wait())
        when_set(flags, 8, lambda: out_copy(plane, block + 1).wait())
        return carry

    lax.fori_loop(0, (number + 1) // 2, add_two, 0)
    lax.fori_loop(0, number, finish, 0)


def place_all(near, other, table, tile_grid):
    comp_count = tile_grid.shape[0]
    return pl.pallas_call(
        place_kernel,
        out_shape=jax.ShapeDtypeStruct(tile_grid.shape, jnp.float32),
        in_specs=[SMEM, VMEM, VMEM, ANY],
        out_specs=ANY,
        scratch_shapes=[
            pltpu.VMEM((W, comp_count, TU + 2 * SUB, NV), jnp.float32),
            pltpu.SemaphoreType.DMA((W, BLOCKS)),
        ],
        input_output_aliases={3: 0},
        compiler_params=pltpu.CompilerParams(vmem_limit_bytes=44 << 20),
        cost_estimate=pl.CostEstimate(flops=0, bytes_accessed=16 << 20, transcendentals=0),
    )(table, near, other, tile_grid)


def body(visibilities, positions, owner, w_plane, row_offset, col_offset):
    peers = lax.axis_size("tm")
    tiles = lax.axis_size("uv")
    sub_count = visibilities.shape[1]
    comp_count = visibilities.shape[0] // peers
    kept = comp_count * SUB
    tile = lax.axis_index("uv")
    half = sub_count // 2

    numbers = jnp.stack(
        [owner[:, 0], row_offset, w_plane, col_offset // LANES, col_offset % LANES], axis=0
    ).astype(jnp.bfloat16)
    numbers = jnp.concatenate([numbers, beside(numbers, "uv")], axis=1).astype(jnp.float32)
    numbers = jnp.pad(numbers, ((0, META - 5), (0, kept - 2 * sub_count)))

    *sent_a, tile_grid = grid_parts(visibilities, positions, peers, 0, half, True)
    parts_a = exchange(sent_a, "tm")
    sent_b = grid_parts(visibilities, positions, peers, 1, half, False, sent_a[0])
    parts_b = exchange(sent_b, "tm")
    (sum_a,) = sum_parts(parts_a, [], sent_b[:1], numbers)
    hops_a = across(sum_a, "uv")
    sum_b, near_a = sum_parts(parts_b, hops_a, [])
    near = jnp.concatenate([near_a, jnp.stack(across(sum_b, "uv"), axis=0)], axis=0)
    other = beside(near, "uv")

    told = jnp.stack([hop[half * SUB :, : 2 * sub_count] for hop in hops_a], axis=1).astype(jnp.float32).astype(jnp.int32)
    chips = told.shape[1]
    told = told.reshape(META, -1)
    entry = jnp.arange(told.shape[1], dtype=jnp.int32)
    chip, sub = entry // (2 * sub_count), entry % sub_count
    others = entry // sub_count % 2
    spots = ((sub // half * chips + chip) << 16) + sub % half * SUB
    ahead = (told[0] - tile) % tiles
    starts = jnp.where(ahead == 0, told[1] + SUB, jnp.where(ahead == tiles - 1, told[1] + SUB - TU, -1))
    table = touch_plan(starts, told[2], told[3] * LANES + told[4], spots, others)
    return place_all(near, other, table, tile_grid)


def solution(mesh):
    placed = (P(None, "uv", "tm"), P(None, "uv", "tm"), P("uv", None), P("uv"), P("uv"), P("uv"))
    return jax.shard_map(
        body, mesh=mesh, in_specs=placed, out_specs=P("tm", None, "uv", None), check_vma=False
    )
```

```python
import functools

import jax
import jax.numpy as jnp
from jax import lax
from jax.experimental import pallas as pl
from jax.experimental.pallas import tpu as pltpu
from jax.sharding import PartitionSpec as P

W = 8
SUB = 64
TAPS = 8
TU = 128
NV = 2048
LANES = 128
SUBLANES = 8
BLOCKS = NV // LANES
META = 16
STEP = 4

VMEM = pl.BlockSpec(memory_space=pltpu.VMEM)
SMEM = pl.BlockSpec(memory_space=pltpu.SMEM)
ANY = pl.BlockSpec(memory_space=pl.ANY)


def taper(scaled):
    inner = jnp.maximum(0.0, 1.0 - scaled * scaled)
    return inner * inner


def number_rows(owner, row_offset, w_plane, col_offset):
    rows = [owner, row_offset, w_plane, col_offset // LANES, col_offset % LANES]
    blank = jnp.zeros((META - len(rows), owner.shape[1]), jnp.int32)
    return jnp.concatenate(rows + [blank], axis=0).astype(jnp.float32).astype(jnp.bfloat16)


def grid_kernel(me_ref, values_ref, places_ref, *rest, peers, first):
    if first:
        kept_ref, sent_ref, out_ref, values_wide, sums, blank, sem, values, places, in_sem = rest
        _, sub_count, row_count = values.shape
        in_copies = [
            pltpu.make_async_copy(values_ref.at[:, pl.ds(0, sub_count), :], values, in_sem.at[0]),
            pltpu.make_async_copy(places_ref.at[:, pl.ds(0, sub_count), :], places, in_sem.at[1]),
        ]
        for copy in in_copies:
            copy.start()
        blank[...] = jnp.zeros(blank.shape, jnp.float32)
        zero_copies = [pltpu.make_async_copy(blank, out_ref.at[:, plane], sem.at[plane]) for plane in range(W)]
        for copy in in_copies:
            copy.wait()
        for copy in zero_copies:
            copy.start()
        values_ref, places_ref = values, places
    else:
        _, owner_ref, row_ref, plane_ref, col_ref, kept_ref, sent_ref, numbers_ref, values_wide, sums = rest
        numbers_ref[...] = number_rows(owner_ref[...], row_ref[...], plane_ref[...], col_ref[...])
    comp_count, sub_count, row_count = values_ref.shape
    rows_each = comp_count // peers * SUB
    for comp in range(comp_count):
        values_wide[comp * sub_count : (comp + 1) * sub_count, :] = values_ref[comp].astype(jnp.float32)
    cells = lax.broadcasted_iota(jnp.int32, (SUB, row_count), 0).astype(jnp.float32) * (2.0 / TAPS)

    def one_sub(sub):
        row_taps = taper(cells - places_ref[0, pl.ds(sub, 1), :] * (2.0 / TAPS)).astype(jnp.bfloat16)
        col_taps = taper(cells - places_ref[1, pl.ds(sub, 1), :] * (2.0 / TAPS))
        weighted = jnp.concatenate(
            [
                (values_wide[pl.ds(comp * sub_count + sub, 1), :] * col_taps).astype(jnp.bfloat16)
                for comp in range(comp_count)
            ],
            axis=0,
        )
        return lax.dot_general(
            weighted, row_taps, (((1,), (1,)), ((), ())), preferred_element_type=jnp.float32
        )

    def some_subs(turn, carry):
        for pair in range(STEP // 2):
            sub = turn * STEP + pair * 2
            sums[pair] = jnp.concatenate([one_sub(sub), one_sub(sub + 1)], axis=1).astype(jnp.bfloat16)
        for pair in range(STEP // 2):
            for mask in range(peers):
                rows = pl.ds(pl.multiple_of((me_ref[0] ^ mask) * rows_each, rows_each), rows_each)
                target = sent_ref if mask % 2 else kept_ref
                target[mask // 2, turn * (STEP // 2) + pair] = sums[pair, rows, :]
        return carry

    lax.fori_loop(0, sub_count // STEP, some_subs, 0)
    if first:
        for copy in zero_copies:
            copy.wait()


def grid_parts(values, places, peers, chunk, sub_count, order=None, numbers=()):
    comp_count, all_subs, row_count = values.shape
    rows_each = comp_count // peers * SUB
    first = order is None
    me = lax.axis_index("tm").astype(jnp.int32).reshape(1)
    parts_shape = (peers // 2, sub_count // 2, rows_each, LANES)
    values_block, places_block = (comp_count, sub_count, row_count), (2, sub_count, row_count)
    out_shape = [jax.ShapeDtypeStruct(parts_shape, jnp.bfloat16)] * 2
    out_specs = [pl.BlockSpec(parts_shape, lambda i: (0, 0, 0, 0))] * 2
    scratch = [
        pltpu.VMEM((comp_count * sub_count, row_count), jnp.float32),
        pltpu.VMEM((STEP // 2, comp_count * SUB, LANES), jnp.bfloat16),
    ]
    if first:
        in_specs = [ANY] * 2
        out_shape.append(jax.ShapeDtypeStruct((rows_each // SUB, W, TU, NV), jnp.float32))
        out_specs.append(ANY)
        scratch += [
            pltpu.VMEM((rows_each // SUB, TU, NV), jnp.float32),
            pltpu.SemaphoreType.DMA((W,)),
            pltpu.VMEM(values_block, values.dtype),
            pltpu.VMEM(places_block, places.dtype),
            pltpu.SemaphoreType.DMA((2,)),
        ]
        more = []
    else:
        whole = pl.BlockSpec((1, all_subs), lambda i: (0, 0))
        in_specs = [pl.BlockSpec(block, lambda i: (0, chunk, 0)) for block in (values_block, places_block)]
        in_specs += [ANY] + [whole] * len(numbers)
        out_shape.append(jax.ShapeDtypeStruct((META, all_subs), jnp.bfloat16))
        out_specs.append(pl.BlockSpec((META, all_subs), lambda i: (0, 0)))
        more = [order, *numbers]
    return pl.pallas_call(
        functools.partial(grid_kernel, peers=peers, first=first),
        grid=(1,),
        out_shape=out_shape,
        in_specs=[SMEM] + in_specs,
        out_specs=out_specs,
        scratch_shapes=scratch,
        compiler_params=pltpu.CompilerParams(vmem_limit_bytes=(60 if first else 48) << 20),
        cost_estimate=pl.CostEstimate(
            flops=8 * sub_count * row_count * SUB * SUB * comp_count,
            bytes_accessed=2 << 20,
            transcendentals=0,
        ),
    )(me, values, places, *more)


def halve_kernel(kept_ref, arrived_ref, *rest):
    next_kept_ref, next_sent_ref = rest[-2:]
    for at in range(kept_ref.shape[0]):
        total = kept_ref[at].astype(jnp.float32) + arrived_ref[at].astype(jnp.float32)
        if at % 2:
            next_sent_ref[at // 2] = total.astype(jnp.bfloat16)
        else:
            next_kept_ref[at // 2] = total


def halve(kept, arrived, order):
    shape = (kept.shape[0] // 2,) + kept.shape[1:]
    return pl.pallas_call(
        halve_kernel,
        out_shape=[jax.ShapeDtypeStruct(shape, jnp.float32), jax.ShapeDtypeStruct(shape, jnp.bfloat16)],
        in_specs=[VMEM] * 2 + [ANY] * len(order),
        out_specs=[VMEM] * 2,
        compiler_params=pltpu.CompilerParams(vmem_limit_bytes=8 << 20),
        cost_estimate=pl.CostEstimate(flops=1 << 18, bytes_accessed=1 << 20, transcendentals=0),
    )(kept, arrived, *order)


def paired(array, axis, mask):
    return lax.ppermute(array, axis, [(i, i ^ mask) for i in range(lax.axis_size(axis))])


def reduce_over(kept, sent, axis, order):
    mask = 1
    arrived = paired(sent, axis, mask)
    while kept.shape[0] > 1:
        kept, sent = halve(kept, arrived, order)
        mask *= 2
        arrived = paired(sent, axis, mask)
    return kept, arrived


def sum_kernel(kept_ref, arrived_ref, *rest, hops):
    pairs = kept_ref.shape[1]
    out_ref = rest[hops or 2]
    for pair in range(pairs):
        total = kept_ref[0, pair].astype(jnp.float32) + arrived_ref[0, pair].astype(jnp.float32)
        out_ref[pair * 2 * SUB : (pair + 1) * 2 * SUB, :] = total.T.astype(jnp.bfloat16)
    if hops:
        near_ref = rest[hops + 1]
        for at in range(hops):
            near_ref[at] = rest[at][: near_ref.shape[1], :]
    else:
        numbers = [ref[...].astype(jnp.float32) for ref in rest[:2]]
        blank = jnp.zeros((META, out_ref.shape[1] - 2 * numbers[0].shape[1]), jnp.float32)
        out_ref[pairs * 2 * SUB :, :] = jnp.concatenate(numbers + [blank], axis=1).astype(jnp.bfloat16)


def sum_parts(kept, arrived, hops, numbers):
    _, pairs, lanes, _ = kept.shape
    rows = pairs * 2 * SUB
    out_shape = [jax.ShapeDtypeStruct((rows if hops else rows + META, lanes), jnp.bfloat16)]
    if hops:
        out_shape.append(jax.ShapeDtypeStruct((len(hops), rows, lanes), jnp.bfloat16))
    return pl.pallas_call(
        functools.partial(sum_kernel, hops=len(hops)),
        out_shape=out_shape,
        in_specs=[VMEM] * (2 + len(hops) + len(numbers)),
        out_specs=[VMEM] * len(out_shape),
        compiler_params=pltpu.CompilerParams(vmem_limit_bytes=8 << 20),
        cost_estimate=pl.CostEstimate(flops=1 << 20, bytes_accessed=2 << 20, transcendentals=0),
    )(kept, arrived, *hops, *numbers)


def across(array, axis):
    return [array] + [paired(array, axis, mask) for mask in range(2, lax.axis_size(axis), 2)]


def touch_plan(starts, planes, cols, spots, others):
    total = starts.shape[0]
    ids = jnp.arange(total, dtype=jnp.int32)
    taken = starts >= 0
    keys = jnp.where(taken, planes, W) * total + ids
    left = jnp.where(taken, planes * BLOCKS + cols // LANES, -1)
    right = jnp.where(taken & (cols % LANES > LANES - SUB), left + 1, -2)
    before = keys[None, :] < keys[:, None]
    after = keys[None, :] > keys[:, None]
    rank = jnp.sum(before.astype(jnp.int32), axis=1)

    def edges(units):
        same = (left[None, :] == units[:, None]) | (right[None, :] == units[:, None])
        first = ~jnp.any(same & before, axis=1)
        last = ~jnp.any(same & after, axis=1)
        return first.astype(jnp.int32) + 2 * last.astype(jnp.int32)

    flags = edges(left) + jnp.where(right >= 0, 4 * edges(right), 0) + 16 * others
    fields = jnp.stack([starts, cols, planes, spots, flags], axis=0)
    moved = jnp.where(rank[None, None, :] == ids[None, :, None], fields[:, None, :], 0)
    table = jnp.sum(moved, axis=2)
    number = jnp.sum(taken.astype(jnp.int32))
    return jnp.concatenate([table, jnp.full((1, total), number, jnp.int32)], axis=0)


def place_kernel(table_ref, near_ref, other_ref, _, out_ref, canvas, sem):
    comp_count = canvas.shape[1]
    number = table_ref[5, 0]
    lane = lax.broadcasted_iota(jnp.int32, (SUB + SUBLANES, LANES), 1)

    def lanes_of(block):
        return pl.ds(pl.multiple_of(block * LANES, LANES), LANES)

    def out_copy(plane, block):
        return pltpu.make_async_copy(
            canvas.at[plane, :, pl.ds(SUB, TU), lanes_of(block)],
            out_ref.at[:, plane, :, lanes_of(block)],
            sem.at[plane, block],
        )

    def clear(plane, block):
        canvas[plane, :, pl.ds(SUB, TU), lanes_of(block)] = jnp.zeros((comp_count, TU, LANES), jnp.float32)

    def when_set(flags, bit, act):
        @pl.when((flags & bit) != 0)
        def _():
            act()

    def turn(index):
        start = table_ref[0, index]
        col = table_ref[1, index]
        block = table_ref[3, index] // (1 << 16)
        at = pl.ds(pl.multiple_of(table_ref[3, index] % (1 << 16), SUB), SUB)
        shift = col % LANES
        patch = jnp.where((table_ref[4, index] & 16) != 0, other_ref[block, at, :], near_ref[block, at, :])
        patch = patch.astype(jnp.float32)
        if patch.shape[1] < LANES:
            patch = jnp.concatenate([patch] * (LANES // patch.shape[1]), axis=1)
        patch = jnp.concatenate([patch, jnp.zeros((SUBLANES, patch.shape[1]), jnp.float32)], axis=0)
        patch = pltpu.roll(patch, start % SUBLANES, 0)
        return [
            pltpu.roll(
                patch[:, comp // 2 * LANES : (comp // 2 + 1) * LANES], (shift + comp % 2 * SUB) % LANES, 1
            )
            for comp in range(comp_count)
        ]

    def add_patch(index, turned):
        start = table_ref[0, index]
        col = table_ref[1, index]
        plane = table_ref[2, index]
        flags = table_ref[4, index]
        block = col // LANES
        shift = col % LANES
        rows = pl.ds(pl.multiple_of(start // SUBLANES * SUBLANES, SUBLANES), SUB + SUBLANES)
        when_set(flags, 1, lambda: clear(plane, block))
        here = (lane >= shift) & (lane < shift + SUB)
        for comp in range(comp_count):
            canvas[plane, comp, rows, lanes_of(block)] += jnp.where(here, turned[comp], 0.0)
        when_set(flags, 2, lambda: out_copy(plane, block).start())

        @pl.when(shift > LANES - SUB)
        def _():
            when_set(flags, 4, lambda: clear(plane, block + 1))
            for comp in range(comp_count):
                canvas[plane, comp, rows, lanes_of(block + 1)] += jnp.where(
                    lane < shift + SUB - LANES, turned[comp], 0.0
                )
            when_set(flags, 8, lambda: out_copy(plane, block + 1).start())

    def add_two(turn_index, carry):
        index = turn_index * 2
        first, second = turn(index), turn(index + 1)
        add_patch(index, first)

        @pl.when(index + 1 < number)
        def _():
            add_patch(index + 1, second)

        return carry

    def finish(index, carry):
        block = table_ref[1, index] // LANES
        plane = table_ref[2, index]
        flags = table_ref[4, index]
        when_set(flags, 2, lambda: out_copy(plane, block).wait())
        when_set(flags, 8, lambda: out_copy(plane, block + 1).wait())
        return carry

    lax.fori_loop(0, (number + 1) // 2, add_two, 0)
    lax.fori_loop(0, number, finish, 0)


def place_all(near, other, table, tile_grid):
    comp_count = tile_grid.shape[0]
    return pl.pallas_call(
        place_kernel,
        out_shape=jax.ShapeDtypeStruct(tile_grid.shape, jnp.float32),
        in_specs=[SMEM, VMEM, VMEM, ANY],
        out_specs=ANY,
        scratch_shapes=[
            pltpu.VMEM((W, comp_count, TU + 2 * SUB, NV), jnp.float32),
            pltpu.SemaphoreType.DMA((W, BLOCKS)),
        ],
        input_output_aliases={3: 0},
        compiler_params=pltpu.CompilerParams(vmem_limit_bytes=44 << 20),
        cost_estimate=pl.CostEstimate(flops=0, bytes_accessed=16 << 20, transcendentals=0),
    )(table, near, other, tile_grid)


def body(visibilities, positions, owner, w_plane, row_offset, col_offset):
    peers = lax.axis_size("tm")
    tiles = lax.axis_size("uv")
    sub_count = visibilities.shape[1]
    comp_count = visibilities.shape[0] // peers
    tile = lax.axis_index("uv")
    half = sub_count // 2

    *parts_a, tile_grid = grid_parts(visibilities, positions, peers, 0, half)
    *parts_b, own_numbers = grid_parts(
        visibilities,
        positions,
        peers,
        1,
        half,
        tile_grid,
        (owner.T, row_offset[None], w_plane[None], col_offset[None]),
    )
    reduced_a = reduce_over(*parts_a, "tm", parts_b[:1])
    reduced_b = reduce_over(*parts_b, "tm", [])
    numbers = (own_numbers, paired(own_numbers, "uv", 1))
    (sum_a,) = sum_parts(*reduced_a, [], numbers)
    hops_a = across(sum_a, "uv")
    sum_b, near_a = sum_parts(*reduced_b, hops_a, ())
    near = jnp.concatenate([near_a, jnp.stack(across(sum_b, "uv"), axis=0)], axis=0)
    other = paired(near, "uv", 1)

    told = jnp.stack([hop[half * SUB :, : 2 * sub_count] for hop in hops_a], axis=1).astype(jnp.float32).astype(jnp.int32)
    chips = told.shape[1]
    told = told.reshape(META, -1)
    entry = jnp.arange(told.shape[1], dtype=jnp.int32)
    chip, sub = entry // (2 * sub_count), entry % sub_count
    others = entry // sub_count % 2
    spots = ((sub // half * chips + chip) << 16) + sub % half * SUB
    ahead = (told[0] - tile) % tiles
    starts = jnp.where(ahead == 0, told[1] + SUB, jnp.where(ahead == tiles - 1, told[1] + SUB - TU, -1))
    table = touch_plan(starts, told[2], told[3] * LANES + told[4], spots, others)
    return place_all(near, other, table, tile_grid)


def solution(mesh):
    placed = (P(None, "uv", "tm"), P(None, "uv", "tm"), P("uv", None), P("uv"), P("uv"), P("uv"))
    return jax.shard_map(
        body, mesh=mesh, in_specs=placed, out_specs=P("tm", None, "uv", None), check_vma=False
    )
```

```python
import functools

import jax
import jax.numpy as jnp
from jax import lax
from jax.experimental import pallas as pl
from jax.experimental.pallas import tpu as pltpu
from jax.sharding import PartitionSpec as P

W = 8
SUB = 64
TAPS = 8
TU = 128
NV = 2048
LANES = 128
SUBLANES = 8
BLOCKS = NV // LANES
META = 16
STEP = 4

VMEM = pl.BlockSpec(memory_space=pltpu.VMEM)
SMEM = pl.BlockSpec(memory_space=pltpu.SMEM)
ANY = pl.BlockSpec(memory_space=pl.ANY)


def taper(scaled):
    inner = jnp.maximum(0.0, 1.0 - scaled * scaled)
    return inner * inner


def number_rows(owner, row_offset, w_plane, col_offset):
    rows = [owner, row_offset, w_plane, col_offset // LANES, col_offset % LANES]
    blank = jnp.zeros((META - len(rows), owner.shape[1]), jnp.int32)
    return jnp.concatenate(rows + [blank], axis=0).astype(jnp.float32).astype(jnp.bfloat16)


def grid_kernel(me_ref, values_ref, places_ref, *rest, peers, first):
    if first:
        kept_ref, sent_ref, out_ref, values_wide, sums, blank, sem, values, places, in_sem = rest
        _, sub_count, row_count = values.shape
        in_copies = [
            pltpu.make_async_copy(values_ref.at[:, pl.ds(0, sub_count), :], values, in_sem.at[0]),
            pltpu.make_async_copy(places_ref.at[:, pl.ds(0, sub_count), :], places, in_sem.at[1]),
        ]
        for copy in in_copies:
            copy.start()
        blank[...] = jnp.zeros(blank.shape, jnp.float32)
        zero_copies = [pltpu.make_async_copy(blank, out_ref.at[:, plane], sem.at[plane]) for plane in range(W)]
        for copy in in_copies:
            copy.wait()
        for copy in zero_copies:
            copy.start()
        values_ref, places_ref = values, places
    else:
        _, owner_ref, row_ref, plane_ref, col_ref, kept_ref, sent_ref, numbers_ref, values_wide, sums = rest
        numbers_ref[...] = number_rows(owner_ref[...], row_ref[...], plane_ref[...], col_ref[...])
    comp_count, sub_count, row_count = values_ref.shape
    rows_each = comp_count // peers * SUB
    for comp in range(comp_count):
        values_wide[comp * sub_count : (comp + 1) * sub_count, :] = values_ref[comp].astype(jnp.float32)
    cells = lax.broadcasted_iota(jnp.int32, (SUB, row_count), 0).astype(jnp.float32) * (2.0 / TAPS)

    def one_sub(sub):
        row_taps = taper(cells - places_ref[0, pl.ds(sub, 1), :] * (2.0 / TAPS)).astype(jnp.bfloat16)
        col_taps = taper(cells - places_ref[1, pl.ds(sub, 1), :] * (2.0 / TAPS))
        weighted = jnp.concatenate(
            [
                (values_wide[pl.ds(comp * sub_count + sub, 1), :] * col_taps).astype(jnp.bfloat16)
                for comp in range(comp_count)
            ],
            axis=0,
        )
        return lax.dot_general(
            weighted, row_taps, (((1,), (1,)), ((), ())), preferred_element_type=jnp.float32
        )

    def some_subs(turn, carry):
        for pair in range(STEP // 2):
            sub = turn * STEP + pair * 2
            sums[pair] = jnp.concatenate([one_sub(sub), one_sub(sub + 1)], axis=1).astype(jnp.bfloat16)
        for pair in range(STEP // 2):
            for mask in range(peers):
                rows = pl.ds(pl.multiple_of((me_ref[0] ^ mask) * rows_each, rows_each), rows_each)
                target = sent_ref if mask % 2 else kept_ref
                target[mask // 2, turn * (STEP // 2) + pair] = sums[pair, rows, :]
        return carry

    lax.fori_loop(0, sub_count // STEP, some_subs, 0)
    if first:
        for copy in zero_copies:
            copy.wait()


def grid_parts(values, places, peers, chunk, sub_count, order=None, numbers=()):
    comp_count, all_subs, row_count = values.shape
    rows_each = comp_count // peers * SUB
    first = order is None
    me = lax.axis_index("tm").astype(jnp.int32).reshape(1)
    parts_shape = (peers // 2, sub_count // 2, rows_each, LANES)
    values_block, places_block = (comp_count, sub_count, row_count), (2, sub_count, row_count)
    out_shape = [jax.ShapeDtypeStruct(parts_shape, jnp.bfloat16)] * 2
    out_specs = [pl.BlockSpec(parts_shape, lambda i: (0, 0, 0, 0))] * 2
    scratch = [
        pltpu.VMEM((comp_count * sub_count, row_count), jnp.float32),
        pltpu.VMEM((STEP // 2, comp_count * SUB, LANES), jnp.bfloat16),
    ]
    if first:
        in_specs = [ANY] * 2
        out_shape.append(jax.ShapeDtypeStruct((rows_each // SUB, W, TU, NV), jnp.float32))
        out_specs.append(ANY)
        scratch += [
            pltpu.VMEM((rows_each // SUB, TU, NV), jnp.float32),
            pltpu.SemaphoreType.DMA((W,)),
            pltpu.VMEM(values_block, values.dtype),
            pltpu.VMEM(places_block, places.dtype),
            pltpu.SemaphoreType.DMA((2,)),
        ]
        more = []
    else:
        whole = pl.BlockSpec((1, all_subs), lambda i: (0, 0))
        in_specs = [pl.BlockSpec(block, lambda i: (0, chunk, 0)) for block in (values_block, places_block)]
        in_specs += [ANY] + [whole] * len(numbers)
        out_shape.append(jax.ShapeDtypeStruct((META, all_subs), jnp.bfloat16))
        out_specs.append(pl.BlockSpec((META, all_subs), lambda i: (0, 0)))
        more = [order, *numbers]
    return pl.pallas_call(
        functools.partial(grid_kernel, peers=peers, first=first),
        grid=(1,),
        out_shape=out_shape,
        in_specs=[SMEM] + in_specs,
        out_specs=out_specs,
        scratch_shapes=scratch,
        compiler_params=pltpu.CompilerParams(vmem_limit_bytes=(60 if first else 48) << 20),
        cost_estimate=pl.CostEstimate(
            flops=8 * sub_count * row_count * SUB * SUB * comp_count,
            bytes_accessed=2 << 20,
            transcendentals=0,
        ),
    )(me, values, places, *more)


def halve_kernel(kept_ref, arrived_ref, *rest):
    next_kept_ref, next_sent_ref = rest[-2:]
    for at in range(kept_ref.shape[0]):
        total = kept_ref[at].astype(jnp.float32) + arrived_ref[at].astype(jnp.float32)
        if at % 2:
            next_sent_ref[at // 2] = total.astype(jnp.bfloat16)
        else:
            next_kept_ref[at // 2] = total


def halve(kept, arrived, order):
    shape = (kept.shape[0] // 2,) + kept.shape[1:]
    return pl.pallas_call(
        halve_kernel,
        out_shape=[jax.ShapeDtypeStruct(shape, jnp.float32), jax.ShapeDtypeStruct(shape, jnp.bfloat16)],
        in_specs=[VMEM] * 2 + [ANY] * len(order),
        out_specs=[VMEM] * 2,
        compiler_params=pltpu.CompilerParams(vmem_limit_bytes=8 << 20),
        cost_estimate=pl.CostEstimate(flops=1 << 18, bytes_accessed=1 << 20, transcendentals=0),
    )(kept, arrived, *order)


def paired(array, axis, mask):
    return lax.ppermute(array, axis, [(i, i ^ mask) for i in range(lax.axis_size(axis))])


def reduce_over(kept, sent, axis, order):
    mask = 1
    arrived = paired(sent, axis, mask)
    while kept.shape[0] > 1:
        kept, sent = halve(kept, arrived, order)
        mask *= 2
        arrived = paired(sent, axis, mask)
    return kept, arrived


def turning(chunk_numbers, sub, lanes):
    row_offsets = chunk_numbers[1:2, sub : sub + 2]
    col_shifts = chunk_numbers[4:5, sub : sub + 2]
    to = lax.broadcasted_iota(jnp.int32, (2 * SUB, 2 * SUB), 0)
    of = lax.broadcasted_iota(jnp.int32, (2 * SUB, 2 * SUB), 1)
    turned = jnp.where(of < SUB, row_offsets[:, 0:1], row_offsets[:, 1:2]) & (SUBLANES - 1)
    rows = (to == (of & SUB) + ((of + turned) & (SUB - 1))).astype(jnp.bfloat16)
    to = lax.broadcasted_iota(jnp.int32, (lanes, LANES), 1)
    of = lax.broadcasted_iota(jnp.int32, (lanes, LANES), 0)
    cols = [
        (to == ((of + col_shifts[:, which : which + 1]) & (LANES - 1))).astype(jnp.bfloat16) for which in range(2)
    ]
    return rows, cols


def sum_kernel(kept_ref, arrived_ref, numbers_ref, *rest, hops, first_sub):
    pairs, lanes = kept_ref.shape[1:3]
    group = min(lanes, LANES)
    out_ref = rest[hops or 1]
    numbers = numbers_ref[...].astype(jnp.float32).astype(jnp.int32)
    for pair in range(pairs):
        total = kept_ref[0, pair].astype(jnp.float32) + arrived_ref[0, pair].astype(jnp.float32)
        rows, cols = turning(numbers, first_sub + 2 * pair, group)
        total = lax.dot_general(
            rows, total.astype(jnp.bfloat16), (((1,), (1,)), ((), ())), preferred_element_type=jnp.float32
        ).astype(jnp.bfloat16)
        for which in range(2):
            at = (pair * 2 + which) * SUB
            for left in range(0, lanes, group):
                out_ref[at : at + SUB, left : left + LANES] = jnp.dot(
                    total[which * SUB : (which + 1) * SUB, left : left + group],
                    cols[which],
                    preferred_element_type=jnp.float32,
                ).astype(jnp.bfloat16)
    if hops:
        near_ref = rest[hops + 1]
        for at in range(hops):
            near_ref[at] = rest[at][: near_ref.shape[1], :]
    else:
        both = [ref[...].astype(jnp.float32) for ref in (numbers_ref, rest[0])]
        blank = jnp.zeros((META, out_ref.shape[1] - 2 * both[0].shape[1]), jnp.float32)
        out_ref[pairs * 2 * SUB :, :] = jnp.concatenate(both + [blank], axis=1).astype(jnp.bfloat16)


def sum_parts(kept, arrived, first_sub, own_numbers, hops, other_numbers):
    _, pairs, lanes, _ = kept.shape
    rows = pairs * 2 * SUB
    lanes = max(lanes, LANES)
    out_shape = [jax.ShapeDtypeStruct((rows if hops else rows + META, lanes), jnp.bfloat16)]
    if hops:
        out_shape.append(jax.ShapeDtypeStruct((len(hops), rows, lanes), jnp.bfloat16))
    return pl.pallas_call(
        functools.partial(sum_kernel, hops=len(hops), first_sub=first_sub),
        out_shape=out_shape,
        in_specs=[VMEM] * (3 + len(hops) + len(other_numbers)),
        out_specs=[VMEM] * len(out_shape),
        compiler_params=pltpu.CompilerParams(vmem_limit_bytes=8 << 20),
        cost_estimate=pl.CostEstimate(flops=1 << 20, bytes_accessed=2 << 20, transcendentals=0),
    )(kept, arrived, own_numbers, *hops, *other_numbers)


def across(array, axis):
    return [array] + [paired(array, axis, mask) for mask in range(2, lax.axis_size(axis), 2)]


def touch_plan(starts, planes, cols, spots, others):
    total = starts.shape[0]
    ids = jnp.arange(total, dtype=jnp.int32)
    taken = starts >= 0
    keys = jnp.where(taken, planes, W) * total + ids
    left = jnp.where(taken, planes * BLOCKS + cols // LANES, -1)
    right = jnp.where(taken & (cols % LANES > LANES - SUB), left + 1, -2)
    before = keys[None, :] < keys[:, None]
    after = keys[None, :] > keys[:, None]
    rank = jnp.sum(before.astype(jnp.int32), axis=1)

    def edges(units):
        same = (left[None, :] == units[:, None]) | (right[None, :] == units[:, None])
        first = ~jnp.any(same & before, axis=1)
        last = ~jnp.any(same & after, axis=1)
        return first.astype(jnp.int32) + 2 * last.astype(jnp.int32)

    flags = edges(left) + jnp.where(right >= 0, 4 * edges(right), 0) + 16 * others
    fields = jnp.stack([starts, cols, planes, spots, flags], axis=0)
    moved = jnp.where(rank[None, None, :] == ids[None, :, None], fields[:, None, :], 0)
    table = jnp.sum(moved, axis=2)
    number = jnp.sum(taken.astype(jnp.int32))
    return jnp.concatenate([table, jnp.full((1, total), number, jnp.int32)], axis=0)


def place_kernel(table_ref, near_ref, other_ref, _, out_ref, canvas, sem):
    comp_count = canvas.shape[1]
    number = table_ref[5, 0]
    row = lax.broadcasted_iota(jnp.int32, (SUB + SUBLANES, LANES), 0)
    lane = lax.broadcasted_iota(jnp.int32, (SUB + SUBLANES, LANES), 1)

    def lanes_of(block):
        return pl.ds(pl.multiple_of(block * LANES, LANES), LANES)

    def out_copy(plane, block):
        return pltpu.make_async_copy(
            canvas.at[plane, :, pl.ds(SUB, TU), lanes_of(block)],
            out_ref.at[:, plane, :, lanes_of(block)],
            sem.at[plane, block],
        )

    def clear(plane, block):
        canvas[plane, :, pl.ds(SUB, TU), lanes_of(block)] = jnp.zeros((comp_count, TU, LANES), jnp.float32)

    def when_set(flags, bit, act):
        @pl.when((flags & bit) != 0)
        def _():
            act()

    def patch_of(index):
        spot = table_ref[3, index]
        block = spot >> 16
        at = pl.ds(pl.multiple_of(spot & 0xFFFF, SUB), SUB)
        patch = jnp.where((table_ref[4, index] & 16) != 0, other_ref[block, at, :], near_ref[block, at, :])
        patch = patch.astype(jnp.float32)
        patches = []
        for comp in range(comp_count):
            values = patch[:, comp // 2 * LANES : (comp // 2 + 1) * LANES]
            if comp % 2:
                values = pltpu.roll(values, SUB, 1)
            patches.append(jnp.concatenate([values, values[:SUBLANES]], axis=0))
        return patches

    def add_patch(index, patches):
        start = table_ref[0, index]
        col = table_ref[1, index]
        plane = table_ref[2, index]
        flags = table_ref[4, index]
        block = col >> 7
        shift = col & (LANES - 1)
        skip = start & (SUBLANES - 1)
        rows = pl.ds(pl.multiple_of(start - skip, SUBLANES), SUB + SUBLANES)
        inside = (row >= skip) & (row < skip + SUB)
        when_set(flags, 1, lambda: clear(plane, block))
        here = inside & (lane >= shift) & (lane < shift + SUB)
        for comp in range(comp_count):
            canvas[plane, comp, rows, lanes_of(block)] += jnp.where(here, patches[comp], 0.0)
        when_set(flags, 2, lambda: out_copy(plane, block).start())

        @pl.when(shift > LANES - SUB)
        def _():
            when_set(flags, 4, lambda: clear(plane, block + 1))
            there = inside & (lane < shift + SUB - LANES)
            for comp in range(comp_count):
                canvas[plane, comp, rows, lanes_of(block + 1)] += jnp.where(there, patches[comp], 0.0)
            when_set(flags, 8, lambda: out_copy(plane, block + 1).start())

    def add_two(turn_index, carry):
        index = turn_index * 2
        first, second = patch_of(index), patch_of(index + 1)
        add_patch(index, first)

        @pl.when(index + 1 < number)
        def _():
            add_patch(index + 1, second)

        return carry

    def finish(index, carry):
        block = table_ref[1, index] >> 7
        plane = table_ref[2, index]
        flags = table_ref[4, index]
        when_set(flags, 2, lambda: out_copy(plane, block).wait())
        when_set(flags, 8, lambda: out_copy(plane, block + 1).wait())
        return carry

    lax.fori_loop(0, (number + 1) // 2, add_two, 0)
    lax.fori_loop(0, number, finish, 0)


def place_all(near, other, table, tile_grid):
    comp_count = tile_grid.shape[0]
    return pl.pallas_call(
        place_kernel,
        out_shape=jax.ShapeDtypeStruct(tile_grid.shape, jnp.float32),
        in_specs=[SMEM, VMEM, VMEM, ANY],
        out_specs=ANY,
        scratch_shapes=[
            pltpu.VMEM((W, comp_count, TU + 2 * SUB, NV), jnp.float32),
            pltpu.SemaphoreType.DMA((W, BLOCKS)),
        ],
        input_output_aliases={3: 0},
        compiler_params=pltpu.CompilerParams(vmem_limit_bytes=44 << 20),
        cost_estimate=pl.CostEstimate(flops=0, bytes_accessed=16 << 20, transcendentals=0),
    )(table, near, other, tile_grid)


def body(visibilities, positions, owner, w_plane, row_offset, col_offset):
    peers = lax.axis_size("tm")
    tiles = lax.axis_size("uv")
    sub_count = visibilities.shape[1]
    comp_count = visibilities.shape[0] // peers
    tile = lax.axis_index("uv")
    half = sub_count // 2

    *parts_a, tile_grid = grid_parts(visibilities, positions, peers, 0, half)
    *parts_b, own_numbers = grid_parts(
        visibilities,
        positions,
        peers,
        1,
        half,
        tile_grid,
        (owner.T, row_offset[None], w_plane[None], col_offset[None]),
    )
    reduced_a = reduce_over(*parts_a, "tm", parts_b[:1])
    reduced_b = reduce_over(*parts_b, "tm", [])
    (sum_a,) = sum_parts(*reduced_a, 0, own_numbers, [], [paired(own_numbers, "uv", 1)])
    hops_a = across(sum_a, "uv")
    sum_b, near_a = sum_parts(*reduced_b, half, own_numbers, hops_a, [])
    near = jnp.concatenate([near_a, jnp.stack(across(sum_b, "uv"), axis=0)], axis=0)
    other = paired(near, "uv", 1)

    told = jnp.stack([hop[half * SUB :, : 2 * sub_count] for hop in hops_a], axis=1).astype(jnp.float32).astype(jnp.int32)
    chips = told.shape[1]
    told = told.reshape(META, -1)
    entry = jnp.arange(told.shape[1], dtype=jnp.int32)
    chip, sub = entry // (2 * sub_count), entry % sub_count
    others = entry // sub_count % 2
    spots = ((sub // half * chips + chip) << 16) + sub % half * SUB
    ahead = (told[0] - tile) % tiles
    starts = jnp.where(ahead == 0, told[1] + SUB, jnp.where(ahead == tiles - 1, told[1] + SUB - TU, -1))
    table = touch_plan(starts, told[2], told[3] * LANES + told[4], spots, others)
    return place_all(near, other, table, tile_grid)


def solution(mesh):
    placed = (P(None, "uv", "tm"), P(None, "uv", "tm"), P("uv", None), P("uv"), P("uv"), P("uv"))
    return jax.shard_map(
        body, mesh=mesh, in_specs=placed, out_specs=P("tm", None, "uv", None), check_vma=False
    )
```

```python
import functools

import jax
import jax.numpy as jnp
from jax import lax
from jax.experimental import pallas as pl
from jax.experimental.pallas import tpu as pltpu
from jax.sharding import PartitionSpec as P

W = 8
SUB = 64
TAPS = 8
TU = 128
NV = 2048
LANES = 128
SUBLANES = 8
BLOCKS = NV // LANES
META = 16
STEP = 4

VMEM = pl.BlockSpec(memory_space=pltpu.VMEM)
SMEM = pl.BlockSpec(memory_space=pltpu.SMEM)
ANY = pl.BlockSpec(memory_space=pl.ANY)


def taper(scaled):
    inner = jnp.maximum(0.0, 1.0 - scaled * scaled)
    return inner * inner


def number_rows(owner, row_offset, w_plane, col_offset):
    rows = [owner, row_offset, w_plane, col_offset // LANES, col_offset % LANES]
    blank = jnp.zeros((META - len(rows), owner.shape[1]), jnp.int32)
    return jnp.concatenate(rows + [blank], axis=0).astype(jnp.float32).astype(jnp.bfloat16)


def grid_kernel(me_ref, values_ref, places_ref, *rest, peers, first, turns, earlier):
    if first:
        kept_ref, sent_ref, out_ref, values_wide, sums, blank, sem, values, places, in_sem = rest
        _, sub_count, row_count = values.shape
        in_copies = [
            pltpu.make_async_copy(values_ref.at[:, pl.ds(0, sub_count), :], values, in_sem.at[0]),
            pltpu.make_async_copy(places_ref.at[:, pl.ds(0, sub_count), :], places, in_sem.at[1]),
        ]
        for copy in in_copies:
            copy.start()
        blank[...] = jnp.zeros(blank.shape, jnp.float32)
        zero_copies = [pltpu.make_async_copy(blank, out_ref.at[:, plane], sem.at[plane]) for plane in range(W)]
        for copy in in_copies:
            copy.wait()
        for copy in zero_copies:
            copy.start()
        values_ref, places_ref = values, places
    else:
        rest = rest[1:]
        if earlier:
            earlier_kept, earlier_sent, kept_ref, sent_ref, values_wide, sums = rest
            done = earlier_kept.shape[1]
            kept_ref[:, :done] = earlier_kept[...]
            sent_ref[:, :done] = earlier_sent[...]
        else:
            owner_ref, row_ref, plane_ref, col_ref, kept_ref, sent_ref, numbers_ref, values_wide, sums = rest
            numbers_ref[...] = number_rows(owner_ref[...], row_ref[...], plane_ref[...], col_ref[...])
    comp_count, sub_count, row_count = values_ref.shape
    rows_each = comp_count // peers * SUB
    for comp in range(comp_count):
        values_wide[comp * sub_count : (comp + 1) * sub_count, :] = values_ref[comp].astype(jnp.float32)
    cells = lax.broadcasted_iota(jnp.int32, (SUB, row_count), 0).astype(jnp.float32) * (2.0 / TAPS)

    def one_sub(sub):
        row_taps = taper(cells - places_ref[0, pl.ds(sub, 1), :] * (2.0 / TAPS)).astype(jnp.bfloat16)
        col_taps = taper(cells - places_ref[1, pl.ds(sub, 1), :] * (2.0 / TAPS))
        weighted = jnp.concatenate(
            [
                (values_wide[pl.ds(comp * sub_count + sub, 1), :] * col_taps).astype(jnp.bfloat16)
                for comp in range(comp_count)
            ],
            axis=0,
        )
        return lax.dot_general(
            weighted, row_taps, (((1,), (1,)), ((), ())), preferred_element_type=jnp.float32
        )

    def some_subs(turn, carry):
        for pair in range(STEP // 2):
            sub = turn * STEP + pair * 2
            sums[pair] = jnp.concatenate([one_sub(sub), one_sub(sub + 1)], axis=1).astype(jnp.bfloat16)
        for pair in range(STEP // 2):
            for mask in range(peers):
                rows = pl.ds(pl.multiple_of((me_ref[0] ^ mask) * rows_each, rows_each), rows_each)
                target = sent_ref if mask % 2 else kept_ref
                target[mask // 2, turn * (STEP // 2) + pair] = sums[pair, rows, :]
        return carry

    lax.fori_loop(*turns, some_subs, 0)
    if first:
        for copy in zero_copies:
            copy.wait()


def grid_parts(values, places, peers, chunk, turns, order=None, numbers=(), earlier=()):
    comp_count, all_subs, row_count = values.shape
    sub_count = all_subs // 2
    rows_each = comp_count // peers * SUB
    first = order is None
    me = lax.axis_index("tm").astype(jnp.int32).reshape(1)
    parts_shape = (peers // 2, turns[1] * STEP // 2, rows_each, LANES)
    values_block, places_block = (comp_count, sub_count, row_count), (2, sub_count, row_count)
    out_shape = [jax.ShapeDtypeStruct(parts_shape, jnp.bfloat16)] * 2
    out_specs = [pl.BlockSpec(parts_shape, lambda i: (0, 0, 0, 0))] * 2
    scratch = [
        pltpu.VMEM((comp_count * sub_count, row_count), jnp.float32),
        pltpu.VMEM((STEP // 2, comp_count * SUB, LANES), jnp.bfloat16),
    ]
    if first:
        in_specs = [ANY] * 2
        out_shape.append(jax.ShapeDtypeStruct((rows_each // SUB, W, TU, NV), jnp.float32))
        out_specs.append(ANY)
        scratch += [
            pltpu.VMEM((rows_each // SUB, TU, NV), jnp.float32),
            pltpu.SemaphoreType.DMA((W,)),
            pltpu.VMEM(values_block, values.dtype),
            pltpu.VMEM(places_block, places.dtype),
            pltpu.SemaphoreType.DMA((2,)),
        ]
        more = []
    else:
        in_specs = [pl.BlockSpec(block, lambda i: (0, chunk, 0)) for block in (values_block, places_block)]
        in_specs += [ANY] + [pl.BlockSpec((1, all_subs), lambda i: (0, 0))] * len(numbers)
        in_specs += [pl.BlockSpec(array.shape, lambda i: (0, 0, 0, 0)) for array in earlier]
        more = [order, *numbers, *earlier]
        if numbers:
            out_shape.append(jax.ShapeDtypeStruct((META, all_subs), jnp.bfloat16))
            out_specs.append(pl.BlockSpec((META, all_subs), lambda i: (0, 0)))
    return pl.pallas_call(
        functools.partial(grid_kernel, peers=peers, first=first, turns=turns, earlier=bool(earlier)),
        grid=(1,),
        out_shape=out_shape,
        in_specs=[SMEM] + in_specs,
        out_specs=out_specs,
        scratch_shapes=scratch,
        compiler_params=pltpu.CompilerParams(vmem_limit_bytes=(60 if first else 48) << 20),
        cost_estimate=pl.CostEstimate(
            flops=8 * (turns[1] - turns[0]) * STEP * row_count * SUB * SUB * comp_count,
            bytes_accessed=2 << 20,
            transcendentals=0,
        ),
    )(me, values, places, *more)


def halve_kernel(kept_ref, arrived_ref, *rest):
    next_kept_ref, next_sent_ref = rest[-2:]
    for at in range(kept_ref.shape[0]):
        total = kept_ref[at].astype(jnp.float32) + arrived_ref[at].astype(jnp.float32)
        if at % 2:
            next_sent_ref[at // 2] = total.astype(jnp.bfloat16)
        else:
            next_kept_ref[at // 2] = total


def halve(kept, arrived, order):
    shape = (kept.shape[0] // 2,) + kept.shape[1:]
    return pl.pallas_call(
        halve_kernel,
        out_shape=[jax.ShapeDtypeStruct(shape, jnp.float32), jax.ShapeDtypeStruct(shape, jnp.bfloat16)],
        in_specs=[VMEM] * 2 + [ANY] * len(order),
        out_specs=[VMEM] * 2,
        compiler_params=pltpu.CompilerParams(vmem_limit_bytes=8 << 20),
        cost_estimate=pl.CostEstimate(flops=1 << 18, bytes_accessed=1 << 20, transcendentals=0),
    )(kept, arrived, *order)


def paired(array, axis, mask):
    return lax.ppermute(array, axis, [(i, i ^ mask) for i in range(lax.axis_size(axis))])


def halve_all(kept, sent, axis, order):
    mask = 1
    while kept.shape[0] > 1:
        kept, sent = halve(kept, paired(sent, axis, mask), order)
        mask *= 2
    return kept, sent


def turning(chunk_numbers, sub, lanes):
    row_offsets = chunk_numbers[1:2, sub : sub + 2]
    col_shifts = chunk_numbers[4:5, sub : sub + 2]
    to = lax.broadcasted_iota(jnp.int32, (2 * SUB, 2 * SUB), 0)
    of = lax.broadcasted_iota(jnp.int32, (2 * SUB, 2 * SUB), 1)
    turned = jnp.where(of < SUB, row_offsets[:, 0:1], row_offsets[:, 1:2]) & (SUBLANES - 1)
    rows = (to == (of & SUB) + ((of + turned) & (SUB - 1))).astype(jnp.bfloat16)
    to = lax.broadcasted_iota(jnp.int32, (lanes, LANES), 1)
    of = lax.broadcasted_iota(jnp.int32, (lanes, LANES), 0)
    cols = [
        (to == ((of + col_shifts[:, which : which + 1]) & (LANES - 1))).astype(jnp.bfloat16) for which in range(2)
    ]
    return rows, cols


def sum_kernel(kept_ref, arrived_ref, numbers_ref, *rest, hops, first_sub):
    pairs, lanes = kept_ref.shape[1:3]
    group = min(lanes, LANES)
    out_ref = rest[hops or 1]
    numbers = numbers_ref[...].astype(jnp.float32).astype(jnp.int32)
    for pair in range(pairs):
        total = kept_ref[0, pair].astype(jnp.float32) + arrived_ref[0, pair].astype(jnp.float32)
        rows, cols = turning(numbers, first_sub + 2 * pair, group)
        total = lax.dot_general(
            rows, total.astype(jnp.bfloat16), (((1,), (1,)), ((), ())), preferred_element_type=jnp.float32
        ).astype(jnp.bfloat16)
        for which in range(2):
            at = (pair * 2 + which) * SUB
            for left in range(0, lanes, group):
                out_ref[at : at + SUB, left : left + LANES] = jnp.dot(
                    total[which * SUB : (which + 1) * SUB, left : left + group],
                    cols[which],
                    preferred_element_type=jnp.float32,
                ).astype(jnp.bfloat16)
    if hops:
        near_ref = rest[hops + 1]
        for at in range(hops):
            near_ref[at] = rest[at][: near_ref.shape[1], :]
    else:
        both = [ref[...].astype(jnp.float32) for ref in (numbers_ref, rest[0])]
        blank = jnp.zeros((META, out_ref.shape[1] - 2 * both[0].shape[1]), jnp.float32)
        out_ref[pairs * 2 * SUB :, :] = jnp.concatenate(both + [blank], axis=1).astype(jnp.bfloat16)


def sum_parts(kept, arrived, first_sub, own_numbers, hops, other_numbers):
    _, pairs, lanes, _ = kept.shape
    rows = pairs * 2 * SUB
    lanes = max(lanes, LANES)
    out_shape = [jax.ShapeDtypeStruct((rows if hops else rows + META, lanes), jnp.bfloat16)]
    if hops:
        out_shape.append(jax.ShapeDtypeStruct((len(hops), rows, lanes), jnp.bfloat16))
    return pl.pallas_call(
        functools.partial(sum_kernel, hops=len(hops), first_sub=first_sub),
        out_shape=out_shape,
        in_specs=[VMEM] * (3 + len(hops) + len(other_numbers)),
        out_specs=[VMEM] * len(out_shape),
        compiler_params=pltpu.CompilerParams(vmem_limit_bytes=8 << 20),
        cost_estimate=pl.CostEstimate(flops=1 << 20, bytes_accessed=2 << 20, transcendentals=0),
    )(kept, arrived, own_numbers, *hops, *other_numbers)


def across(array, axis):
    return [array] + [paired(array, axis, mask) for mask in range(2, lax.axis_size(axis), 2)]


def touch_plan(starts, planes, cols, spots, others):
    total = starts.shape[0]
    ids = jnp.arange(total, dtype=jnp.int32)
    taken = starts >= 0
    keys = jnp.where(taken, planes, W) * total + ids
    left = jnp.where(taken, planes * BLOCKS + cols // LANES, -1)
    right = jnp.where(taken & (cols % LANES > LANES - SUB), left + 1, -2)
    before = keys[None, :] < keys[:, None]
    after = keys[None, :] > keys[:, None]
    rank = jnp.sum(before.astype(jnp.int32), axis=1)

    def edges(units):
        same = (left[None, :] == units[:, None]) | (right[None, :] == units[:, None])
        first = ~jnp.any(same & before, axis=1)
        last = ~jnp.any(same & after, axis=1)
        return first.astype(jnp.int32) + 2 * last.astype(jnp.int32)

    flags = edges(left) + jnp.where(right >= 0, 4 * edges(right), 0) + 16 * others
    fields = jnp.stack([starts, cols, planes, spots, flags], axis=0)
    moved = jnp.where(rank[None, None, :] == ids[None, :, None], fields[:, None, :], 0)
    table = jnp.sum(moved, axis=2)
    number = jnp.sum(taken.astype(jnp.int32))
    return jnp.concatenate([table, jnp.full((1, total), number, jnp.int32)], axis=0)


def place_kernel(table_ref, near_ref, other_ref, _, out_ref, canvas, sem):
    comp_count = canvas.shape[1]
    number = table_ref[5, 0]
    row = lax.broadcasted_iota(jnp.int32, (SUB + SUBLANES, LANES), 0)
    lane = lax.broadcasted_iota(jnp.int32, (SUB + SUBLANES, LANES), 1)

    def lanes_of(block):
        return pl.ds(pl.multiple_of(block * LANES, LANES), LANES)

    def out_copy(plane, block):
        return pltpu.make_async_copy(
            canvas.at[plane, :, pl.ds(SUB, TU), lanes_of(block)],
            out_ref.at[:, plane, :, lanes_of(block)],
            sem.at[plane, block],
        )

    def clear(plane, block):
        canvas[plane, :, pl.ds(SUB, TU), lanes_of(block)] = jnp.zeros((comp_count, TU, LANES), jnp.float32)

    def when_set(flags, bit, act):
        @pl.when((flags & bit) != 0)
        def _():
            act()

    def patch_of(index):
        spot = table_ref[3, index]
        block = spot >> 16
        at = pl.ds(pl.multiple_of(spot & 0xFFFF, SUB), SUB)
        patch = jnp.where((table_ref[4, index] & 16) != 0, other_ref[block, at, :], near_ref[block, at, :])
        patch = patch.astype(jnp.float32)
        patches = []
        for comp in range(comp_count):
            values = patch[:, comp // 2 * LANES : (comp // 2 + 1) * LANES]
            if comp % 2:
                values = pltpu.roll(values, SUB, 1)
            patches.append(jnp.concatenate([values, values[:SUBLANES]], axis=0))
        return patches

    def add_patch(index, patches):
        start = table_ref[0, index]
        col = table_ref[1, index]
        plane = table_ref[2, index]
        flags = table_ref[4, index]
        block = col >> 7
        shift = col & (LANES - 1)
        skip = start & (SUBLANES - 1)
        rows = pl.ds(pl.multiple_of(start - skip, SUBLANES), SUB + SUBLANES)
        inside = (row >= skip) & (row < skip + SUB)
        when_set(flags, 1, lambda: clear(plane, block))
        here = inside & (lane >= shift) & (lane < shift + SUB)
        for comp in range(comp_count):
            canvas[plane, comp, rows, lanes_of(block)] += jnp.where(here, patches[comp], 0.0)
        when_set(flags, 2, lambda: out_copy(plane, block).start())

        @pl.when(shift > LANES - SUB)
        def _():
            when_set(flags, 4, lambda: clear(plane, block + 1))
            there = inside & (lane < shift + SUB - LANES)
            for comp in range(comp_count):
                canvas[plane, comp, rows, lanes_of(block + 1)] += jnp.where(there, patches[comp], 0.0)
            when_set(flags, 8, lambda: out_copy(plane, block + 1).start())

    def add_two(turn_index, carry):
        index = turn_index * 2
        first, second = patch_of(index), patch_of(index + 1)
        add_patch(index, first)

        @pl.when(index + 1 < number)
        def _():
            add_patch(index + 1, second)

        return carry

    def finish(index, carry):
        block = table_ref[1, index] >> 7
        plane = table_ref[2, index]
        flags = table_ref[4, index]
        when_set(flags, 2, lambda: out_copy(plane, block).wait())
        when_set(flags, 8, lambda: out_copy(plane, block + 1).wait())
        return carry

    lax.fori_loop(0, (number + 1) // 2, add_two, 0)
    lax.fori_loop(0, number, finish, 0)


def place_all(near, other, table, tile_grid):
    comp_count = tile_grid.shape[0]
    return pl.pallas_call(
        place_kernel,
        out_shape=jax.ShapeDtypeStruct(tile_grid.shape, jnp.float32),
        in_specs=[SMEM, VMEM, VMEM, ANY],
        out_specs=ANY,
        scratch_shapes=[
            pltpu.VMEM((W, comp_count, TU + 2 * SUB, NV), jnp.float32),
            pltpu.SemaphoreType.DMA((W, BLOCKS)),
        ],
        input_output_aliases={3: 0},
        compiler_params=pltpu.CompilerParams(vmem_limit_bytes=44 << 20),
        cost_estimate=pl.CostEstimate(flops=0, bytes_accessed=16 << 20, transcendentals=0),
    )(table, near, other, tile_grid)


def body(visibilities, positions, owner, w_plane, row_offset, col_offset):
    peers = lax.axis_size("tm")
    tiles = lax.axis_size("uv")
    sub_count = visibilities.shape[1]
    comp_count = visibilities.shape[0] // peers
    tile = lax.axis_index("uv")
    half = sub_count // 2

    split = half // STEP // 2
    *parts_a, tile_grid = grid_parts(visibilities, positions, peers, 0, (0, half // STEP))
    *parts_b, own_numbers = grid_parts(
        visibilities,
        positions,
        peers,
        1,
        (0, split),
        order=tile_grid,
        numbers=(owner.T, row_offset[None], w_plane[None], col_offset[None]),
    )
    kept_a, sent_a = halve_all(*parts_a, "tm", parts_b[:1])
    parts_b = grid_parts(visibilities, positions, peers, 1, (split, half // STEP), order=sent_a, earlier=parts_b)
    kept_b, sent_b = halve_all(*parts_b, "tm", [])
    arrived_a, arrived_b = (paired(sent, "tm", peers // 2) for sent in (sent_a, sent_b))
    (sum_a,) = sum_parts(kept_a, arrived_a, 0, own_numbers, [], [paired(own_numbers, "uv", 1)])
    hops_a = across(sum_a, "uv")
    sum_b, near_a = sum_parts(kept_b, arrived_b, half, own_numbers, hops_a, [])
    near = jnp.concatenate([near_a, jnp.stack(across(sum_b, "uv"), axis=0)], axis=0)
    other = paired(near, "uv", 1)

    told = jnp.stack([hop[half * SUB :, : 2 * sub_count] for hop in hops_a], axis=1).astype(jnp.float32).astype(jnp.int32)
    chips = told.shape[1]
    told = told.reshape(META, -1)
    entry = jnp.arange(told.shape[1], dtype=jnp.int32)
    chip, sub = entry // (2 * sub_count), entry % sub_count
    others = entry // sub_count % 2
    spots = ((sub // half * chips + chip) << 16) + sub % half * SUB
    ahead = (told[0] - tile) % tiles
    starts = jnp.where(ahead == 0, told[1] + SUB, jnp.where(ahead == tiles - 1, told[1] + SUB - TU, -1))
    table = touch_plan(starts, told[2], told[3] * LANES + told[4], spots, others)
    return place_all(near, other, table, tile_grid)


def solution(mesh):
    placed = (P(None, "uv", "tm"), P(None, "uv", "tm"), P("uv", None), P("uv"), P("uv"), P("uv"))
    return jax.shard_map(
        body, mesh=mesh, in_specs=placed, out_specs=P("tm", None, "uv", None), check_vma=False
    )
```

```python
import functools

import jax
import jax.numpy as jnp
from jax import lax
from jax.experimental import pallas as pl
from jax.experimental.pallas import tpu as pltpu
from jax.sharding import PartitionSpec as P

W = 8
SUB = 64
TAPS = 8
TU = 128
NV = 2048
LANES = 128
SUBLANES = 8
BLOCKS = NV // LANES
META = 16

VMEM = pl.BlockSpec(memory_space=pltpu.VMEM)
SMEM = pl.BlockSpec(memory_space=pltpu.SMEM)
ANY = pl.BlockSpec(memory_space=pl.ANY)


def taper(scaled):
    inner = jnp.maximum(0.0, 1.0 - scaled * scaled)
    return inner * inner


def number_rows(owner, row_offset, w_plane, col_offset):
    rows = [owner, row_offset, w_plane, col_offset // LANES, col_offset % LANES]
    blank = jnp.zeros((META - len(rows), owner.shape[1]), jnp.int32)
    return jnp.concatenate(rows + [blank], axis=0).astype(jnp.float32).astype(jnp.bfloat16)


def grid_kernel(me_ref, values_ref, places_ref, *rest, peers, first, base, turns):
    if first:
        kept_ref, sent_ref, out_ref, values_wide, sums, blank, sem, values, places, in_sem = rest
        all_subs = values.shape[1]
        in_copies = []
        for part in range(2):
            some = pl.ds(part * all_subs // 2, all_subs // 2)
            in_copies += [
                pltpu.make_async_copy(places_ref.at[:, some, :], places.at[:, some, :], in_sem.at[part, 0]),
                pltpu.make_async_copy(values_ref.at[:, some, :], values.at[:, some, :], in_sem.at[part, 1]),
            ]
        for copy in in_copies:
            copy.start()
        blank[...] = jnp.zeros(blank.shape, jnp.float32)
        zero_copies = [pltpu.make_async_copy(blank, out_ref.at[:, plane], sem.at[plane]) for plane in range(W)]
        for copy in zero_copies:
            copy.start()
        values_ref, places_ref = values, places
    else:
        _, owner_ref, row_ref, plane_ref, col_ref, kept_ref, sent_ref, numbers_ref, values_wide, sums = rest
        numbers_ref[...] = number_rows(owner_ref[...], row_ref[...], plane_ref[...], col_ref[...])
    comp_count, sub_count, row_count = values_ref.shape
    rows_each = comp_count // peers * SUB
    cells = lax.broadcasted_iota(jnp.int32, (SUB, row_count), 0).astype(jnp.float32) * (2.0 / TAPS)

    def widen(low, high):
        for comp in range(comp_count):
            at = comp * sub_count
            values_wide[at + low : at + high, :] = values_ref[comp, low:high, :].astype(jnp.float32)

    def one_sub(sub):
        row_taps = taper(cells - places_ref[0, pl.ds(sub, 1), :] * (2.0 / TAPS)).astype(jnp.bfloat16)
        col_taps = taper(cells - places_ref[1, pl.ds(sub, 1), :] * (2.0 / TAPS))
        weighted = jnp.concatenate(
            [
                (values_wide[pl.ds(comp * sub_count + sub, 1), :] * col_taps).astype(jnp.bfloat16)
                for comp in range(comp_count)
            ],
            axis=0,
        )
        return lax.dot_general(
            weighted, row_taps, (((1,), (1,)), ((), ())), preferred_element_type=jnp.float32
        )

    def some_subs(low, step):
        def run(turn, carry):
            for pair in range(step // 2):
                sub = low + turn * step + pair * 2
                sums[pair] = jnp.concatenate([one_sub(sub), one_sub(sub + 1)], axis=1).astype(jnp.bfloat16)
            for pair in range(step // 2):
                for mask in range(peers):
                    rows = pl.ds(pl.multiple_of((me_ref[0] ^ mask) * rows_each, rows_each), rows_each)
                    target = sent_ref if mask % 2 else kept_ref
                    target[mask // 2, (low - base) // 2 + turn * (step // 2) + pair] = sums[pair, rows, :]
            return carry

        return run

    for part, (low, high, step) in enumerate(turns):
        if first:
            for copy in in_copies[2 * part : 2 * part + 2]:
                copy.wait()
            widen(part * all_subs // 2, (part + 1) * all_subs // 2)
        else:
            widen(0, sub_count)
        lax.fori_loop(0, (high - low) // step, some_subs(low, step), 0)
    if first:
        for copy in zero_copies:
            copy.wait()


def grid_parts(values, places, peers, base, turns, order=None, numbers=()):
    comp_count, all_subs, row_count = values.shape
    rows_each = comp_count // peers * SUB
    first = order is None
    me = lax.axis_index("tm").astype(jnp.int32).reshape(1)
    parts_shape = (peers // 2, (turns[-1][1] - base) // 2, rows_each, LANES)
    read = all_subs if first else all_subs // 2
    values_block, places_block = (comp_count, read, row_count), (2, read, row_count)
    out_shape = [jax.ShapeDtypeStruct(parts_shape, jnp.bfloat16)] * 2
    out_specs = [pl.BlockSpec(parts_shape, lambda i: (0, 0, 0, 0))] * 2
    scratch = [
        pltpu.VMEM((comp_count * read, row_count), jnp.float32),
        pltpu.VMEM((max(step for _, _, step in turns) // 2, comp_count * SUB, LANES), jnp.bfloat16),
    ]
    if first:
        values, places = (pltpu.with_memory_space_constraint(array, pltpu.HBM) for array in (values, places))
        in_specs = [pl.BlockSpec(memory_space=pltpu.HBM)] * 2
        out_shape.append(jax.ShapeDtypeStruct((rows_each // SUB, W, TU, NV), jnp.float32))
        out_specs.append(ANY)
        scratch += [
            pltpu.VMEM((rows_each // SUB, TU, NV), jnp.float32),
            pltpu.SemaphoreType.DMA((W,)),
            pltpu.VMEM(values_block, values.dtype),
            pltpu.VMEM(places_block, places.dtype),
            pltpu.SemaphoreType.DMA((2, 2)),
        ]
        more = []
    else:
        whole = pl.BlockSpec((1, all_subs), lambda i: (0, 0))
        in_specs = [pl.BlockSpec(block, lambda i: (0, 1, 0)) for block in (values_block, places_block)]
        in_specs += [ANY] + [whole] * len(numbers)
        out_shape.append(jax.ShapeDtypeStruct((META, all_subs), jnp.bfloat16))
        out_specs.append(pl.BlockSpec((META, all_subs), lambda i: (0, 0)))
        more = [order, *numbers]
    return pl.pallas_call(
        functools.partial(grid_kernel, peers=peers, first=first, base=base, turns=turns),
        grid=(1,),
        out_shape=out_shape,
        in_specs=[SMEM] + in_specs,
        out_specs=out_specs,
        scratch_shapes=scratch,
        compiler_params=pltpu.CompilerParams(vmem_limit_bytes=48 << 20),
        cost_estimate=pl.CostEstimate(
            flops=64 * row_count * SUB * SUB * comp_count,
            bytes_accessed=2 << 20,
            transcendentals=0,
        ),
    )(me, values, places, *more)


def halve_kernel(kept_ref, arrived_ref, *rest):
    next_kept_ref, next_sent_ref = rest[-2:]
    for at in range(kept_ref.shape[0]):
        total = kept_ref[at].astype(jnp.float32) + arrived_ref[at].astype(jnp.float32)
        if at % 2:
            next_sent_ref[at // 2] = total.astype(jnp.bfloat16)
        else:
            next_kept_ref[at // 2] = total


def halve(kept, arrived, order):
    shape = (kept.shape[0] // 2,) + kept.shape[1:]
    return pl.pallas_call(
        halve_kernel,
        out_shape=[jax.ShapeDtypeStruct(shape, jnp.float32), jax.ShapeDtypeStruct(shape, jnp.bfloat16)],
        in_specs=[VMEM] * 2 + [ANY] * len(order),
        out_specs=[VMEM] * 2,
        compiler_params=pltpu.CompilerParams(vmem_limit_bytes=8 << 20),
        cost_estimate=pl.CostEstimate(flops=1 << 18, bytes_accessed=1 << 20, transcendentals=0),
    )(kept, arrived, *order)


def paired(array, axis, mask):
    return lax.ppermute(array, axis, [(i, i ^ mask) for i in range(lax.axis_size(axis))])


def reduce_over(kept, sent, axis, order):
    mask = 1
    arrived = paired(sent, axis, mask)
    while kept.shape[0] > 1:
        kept, sent = halve(kept, arrived, order)
        mask *= 2
        arrived = paired(sent, axis, mask)
    return kept, arrived


def turning(chunk_numbers, sub, lanes):
    row_offsets = chunk_numbers[1:2, sub : sub + 2]
    col_shifts = chunk_numbers[4:5, sub : sub + 2]
    to = lax.broadcasted_iota(jnp.int32, (2 * SUB, 2 * SUB), 0)
    of = lax.broadcasted_iota(jnp.int32, (2 * SUB, 2 * SUB), 1)
    turned = jnp.where(of < SUB, row_offsets[:, 0:1], row_offsets[:, 1:2]) & (SUBLANES - 1)
    rows = (to == (of & SUB) + ((of + turned) & (SUB - 1))).astype(jnp.bfloat16)
    to = lax.broadcasted_iota(jnp.int32, (lanes, LANES), 1)
    of = lax.broadcasted_iota(jnp.int32, (lanes, LANES), 0)
    cols = [
        (to == ((of + col_shifts[:, which : which + 1]) & (LANES - 1))).astype(jnp.bfloat16) for which in range(2)
    ]
    return rows, cols


def sum_kernel(kept_ref, arrived_ref, numbers_ref, *rest, hops, first_sub):
    pairs, lanes = kept_ref.shape[1:3]
    group = min(lanes, LANES)
    out_ref = rest[hops or 1]
    numbers = numbers_ref[...].astype(jnp.float32).astype(jnp.int32)
    for pair in range(pairs):
        total = kept_ref[0, pair].astype(jnp.float32) + arrived_ref[0, pair].astype(jnp.float32)
        rows, cols = turning(numbers, first_sub + 2 * pair, group)
        total = lax.dot_general(
            rows, total.astype(jnp.bfloat16), (((1,), (1,)), ((), ())), preferred_element_type=jnp.float32
        ).astype(jnp.bfloat16)
        for which in range(2):
            at = (pair * 2 + which) * SUB
            for left in range(0, lanes, group):
                out_ref[at : at + SUB, left : left + LANES] = jnp.dot(
                    total[which * SUB : (which + 1) * SUB, left : left + group],
                    cols[which],
                    preferred_element_type=jnp.float32,
                ).astype(jnp.bfloat16)
    if hops:
        near_ref = rest[hops + 1]
        for at in range(hops):
            near_ref[at] = rest[at][: near_ref.shape[1], :]
    else:
        both = [ref[...].astype(jnp.float32) for ref in (numbers_ref, rest[0])]
        blank = jnp.zeros((META, out_ref.shape[1] - 2 * both[0].shape[1]), jnp.float32)
        out_ref[pairs * 2 * SUB :, :] = jnp.concatenate(both + [blank], axis=1).astype(jnp.bfloat16)


def sum_parts(kept, arrived, first_sub, own_numbers, hops, other_numbers):
    _, pairs, lanes, _ = kept.shape
    rows = pairs * 2 * SUB
    lanes = max(lanes, LANES)
    out_shape = [jax.ShapeDtypeStruct((rows if hops else rows + META, lanes), jnp.bfloat16)]
    if hops:
        out_shape.append(jax.ShapeDtypeStruct((len(hops), hops[0].shape[0] - META, lanes), jnp.bfloat16))
    return pl.pallas_call(
        functools.partial(sum_kernel, hops=len(hops), first_sub=first_sub),
        out_shape=out_shape,
        in_specs=[VMEM] * (3 + len(hops) + len(other_numbers)),
        out_specs=[VMEM] * len(out_shape),
        compiler_params=pltpu.CompilerParams(vmem_limit_bytes=8 << 20),
        cost_estimate=pl.CostEstimate(flops=1 << 20, bytes_accessed=2 << 20, transcendentals=0),
    )(kept, arrived, own_numbers, *hops, *other_numbers)


def across(array, axis):
    return [array] + [paired(array, axis, mask) for mask in range(2, lax.axis_size(axis), 2)]


def touch_plan(starts, planes, cols, spots, others):
    total = starts.shape[0]
    ids = jnp.arange(total, dtype=jnp.int32)
    taken = starts >= 0
    keys = jnp.where(taken, planes, W) * total + ids
    left = jnp.where(taken, planes * BLOCKS + cols // LANES, -1)
    right = jnp.where(taken & (cols % LANES > LANES - SUB), left + 1, -2)
    before = keys[None, :] < keys[:, None]
    after = keys[None, :] > keys[:, None]
    rank = jnp.sum(before.astype(jnp.int32), axis=1)

    def edges(units):
        same = (left[None, :] == units[:, None]) | (right[None, :] == units[:, None])
        first = ~jnp.any(same & before, axis=1)
        last = ~jnp.any(same & after, axis=1)
        return first.astype(jnp.int32) + 2 * last.astype(jnp.int32)

    flags = edges(left) + jnp.where(right >= 0, 4 * edges(right), 0) + 16 * others
    fields = jnp.stack([starts, cols, planes, spots, flags], axis=0)
    moved = jnp.where(rank[None, None, :] == ids[None, :, None], fields[:, None, :], 0)
    table = jnp.sum(moved, axis=2)
    number = jnp.sum(taken.astype(jnp.int32))
    return jnp.concatenate([table, jnp.full((1, total), number, jnp.int32)], axis=0)


def place_kernel(table_ref, near_ref, other_ref, _, out_ref, canvas, sem):
    comp_count = canvas.shape[1]
    number = table_ref[5, 0]
    row = lax.broadcasted_iota(jnp.int32, (SUB + SUBLANES, LANES), 0)
    lane = lax.broadcasted_iota(jnp.int32, (SUB + SUBLANES, LANES), 1)

    def lanes_of(block):
        return pl.ds(pl.multiple_of(block * LANES, LANES), LANES)

    def out_copy(plane, block):
        return pltpu.make_async_copy(
            canvas.at[plane, :, pl.ds(SUB, TU), lanes_of(block)],
            out_ref.at[:, plane, :, lanes_of(block)],
            sem.at[plane, block],
        )

    def clear(plane, block):
        canvas[plane, :, pl.ds(SUB, TU), lanes_of(block)] = jnp.zeros((comp_count, TU, LANES), jnp.float32)

    def when_set(flags, bit, act):
        @pl.when((flags & bit) != 0)
        def _():
            act()

    def patch_of(index):
        spot = table_ref[3, index]
        block = spot >> 16
        at = pl.ds(pl.multiple_of(spot & 0xFFFF, SUB), SUB)
        patch = jnp.where((table_ref[4, index] & 16) != 0, other_ref[block, at, :], near_ref[block, at, :])
        patch = patch.astype(jnp.float32)
        patches = []
        for comp in range(comp_count):
            values = patch[:, comp // 2 * LANES : (comp // 2 + 1) * LANES]
            if comp % 2:
                values = pltpu.roll(values, SUB, 1)
            patches.append(jnp.concatenate([values, values[:SUBLANES]], axis=0))
        return patches

    def add_patch(index, patches):
        start = table_ref[0, index]
        col = table_ref[1, index]
        plane = table_ref[2, index]
        flags = table_ref[4, index]
        block = col >> 7
        shift = col & (LANES - 1)
        skip = start & (SUBLANES - 1)
        rows = pl.ds(pl.multiple_of(start - skip, SUBLANES), SUB + SUBLANES)
        inside = (row >= skip) & (row < skip + SUB)
        when_set(flags, 1, lambda: clear(plane, block))
        here = inside & (lane >= shift) & (lane < shift + SUB)
        for comp in range(comp_count):
            canvas[plane, comp, rows, lanes_of(block)] += jnp.where(here, patches[comp], 0.0)
        when_set(flags, 2, lambda: out_copy(plane, block).start())

        @pl.when(shift > LANES - SUB)
        def _():
            when_set(flags, 4, lambda: clear(plane, block + 1))
            there = inside & (lane < shift + SUB - LANES)
            for comp in range(comp_count):
                canvas[plane, comp, rows, lanes_of(block + 1)] += jnp.where(there, patches[comp], 0.0)
            when_set(flags, 8, lambda: out_copy(plane, block + 1).start())

    def add_two(turn_index, carry):
        index = turn_index * 2
        first, second = patch_of(index), patch_of(index + 1)
        add_patch(index, first)

        @pl.when(index + 1 < number)
        def _():
            add_patch(index + 1, second)

        return carry

    def finish(index, carry):
        block = table_ref[1, index] >> 7
        plane = table_ref[2, index]
        flags = table_ref[4, index]
        when_set(flags, 2, lambda: out_copy(plane, block).wait())
        when_set(flags, 8, lambda: out_copy(plane, block + 1).wait())
        return carry

    lax.fori_loop(0, (number + 1) // 2, add_two, 0)
    lax.fori_loop(0, number, finish, 0)


def place_all(near, other, table, tile_grid):
    comp_count = tile_grid.shape[0]
    return pl.pallas_call(
        place_kernel,
        out_shape=jax.ShapeDtypeStruct(tile_grid.shape, jnp.float32),
        in_specs=[SMEM, VMEM, VMEM, ANY],
        out_specs=ANY,
        scratch_shapes=[
            pltpu.VMEM((W, comp_count, TU + 2 * SUB, NV), jnp.float32),
            pltpu.SemaphoreType.DMA((W, BLOCKS)),
        ],
        input_output_aliases={3: 0},
        compiler_params=pltpu.CompilerParams(vmem_limit_bytes=44 << 20),
        cost_estimate=pl.CostEstimate(flops=0, bytes_accessed=16 << 20, transcendentals=0),
    )(table, near, other, tile_grid)


def body(visibilities, positions, owner, w_plane, row_offset, col_offset):
    peers = lax.axis_size("tm")
    tiles = lax.axis_size("uv")
    sub_count = visibilities.shape[1]
    comp_count = visibilities.shape[0] // peers
    tile = lax.axis_index("uv")
    half, more = sub_count // 2, sub_count // 8
    cut = half + more

    *parts_a, tile_grid = grid_parts(
        visibilities, positions, peers, 0, ((0, half, half // 2), (half, cut, more))
    )
    *parts_b, own_numbers = grid_parts(
        visibilities,
        positions,
        peers,
        more,
        ((more, half, half - more),),
        tile_grid,
        (owner.T, row_offset[None], w_plane[None], col_offset[None]),
    )
    reduced_a = reduce_over(*parts_a, "tm", parts_b[:1])
    reduced_b = reduce_over(*parts_b, "tm", [])
    (sum_a,) = sum_parts(*reduced_a, 0, own_numbers, [], [paired(own_numbers, "uv", 1)])
    hops_a = across(sum_a, "uv")
    sum_b, near_a = sum_parts(*reduced_b, cut, own_numbers, hops_a, [])
    near = jnp.concatenate([near_a, jnp.stack(across(sum_b, "uv"), axis=0)], axis=1)
    other = paired(near, "uv", 1)

    told = jnp.stack([hop[cut * SUB :, : 2 * sub_count] for hop in hops_a], axis=1).astype(jnp.float32).astype(jnp.int32)
    told = told.reshape(META, -1)
    entry = jnp.arange(told.shape[1], dtype=jnp.int32)
    chip, others, sub = entry // (2 * sub_count), entry // sub_count % 2, entry % sub_count
    spots = (chip << 16) + sub * SUB
    ahead = (told[0] - tile) % tiles
    starts = jnp.where(ahead == 0, told[1] + SUB, jnp.where(ahead == tiles - 1, told[1] + SUB - TU, -1))
    table = touch_plan(starts, told[2], told[3] * LANES + told[4], spots, others)
    return place_all(near, other, table, tile_grid)


def solution(mesh):
    placed = (P(None, "uv", "tm"), P(None, "uv", "tm"), P("uv", None), P("uv"), P("uv"), P("uv"))
    return jax.shard_map(
        body, mesh=mesh, in_specs=placed, out_specs=P("tm", None, "uv", None), check_vma=False
    )
```

```python
import functools

import jax
import jax.numpy as jnp
from jax import lax
from jax.experimental import pallas as pl
from jax.experimental.pallas import tpu as pltpu
from jax.sharding import PartitionSpec as P

W = 8
SUB = 64
TAPS = 8
TU = 128
NV = 2048
LANES = 128
SUBLANES = 8
BLOCKS = NV // LANES
META = 16
STEP = 4

VMEM = pl.BlockSpec(memory_space=pltpu.VMEM)
SMEM = pl.BlockSpec(memory_space=pltpu.SMEM)
ANY = pl.BlockSpec(memory_space=pl.ANY)


def taper(scaled):
    inner = jnp.maximum(0.0, 1.0 - scaled * scaled)
    return inner * inner


def number_rows(owner, row_offset, w_plane, col_offset):
    rows = [owner, row_offset, w_plane, col_offset // LANES, col_offset % LANES]
    blank = jnp.zeros((META - len(rows), owner.shape[1]), jnp.int32)
    return jnp.concatenate(rows + [blank], axis=0).astype(jnp.float32).astype(jnp.bfloat16)


def grid_kernel(me_ref, values_ref, places_ref, *rest, peers, first, turns, earlier):
    if first:
        kept_ref, sent_ref, out_ref, values_wide, sums, blank, sem, values, places, in_sem = rest
        _, sub_count, row_count = values.shape
        in_copies = [
            pltpu.make_async_copy(values_ref.at[:, pl.ds(0, sub_count), :], values, in_sem.at[0]),
            pltpu.make_async_copy(places_ref.at[:, pl.ds(0, sub_count), :], places, in_sem.at[1]),
        ]
        for copy in in_copies:
            copy.start()
        blank[...] = jnp.zeros(blank.shape, jnp.float32)
        zero_copies = [pltpu.make_async_copy(blank, out_ref.at[:, plane], sem.at[plane]) for plane in range(W)]
        for copy in in_copies:
            copy.wait()
        for copy in zero_copies:
            copy.start()
        values_ref, places_ref = values, places
    else:
        rest = rest[1:]
        if earlier:
            earlier_kept, earlier_sent, kept_ref, sent_ref, values_wide, sums = rest
            done = earlier_kept.shape[1]
            kept_ref[:, :done] = earlier_kept[...]
            sent_ref[:, :done] = earlier_sent[...]
        else:
            owner_ref, row_ref, plane_ref, col_ref, kept_ref, sent_ref, numbers_ref, values_wide, sums = rest
            numbers_ref[...] = number_rows(owner_ref[...], row_ref[...], plane_ref[...], col_ref[...])
    comp_count, sub_count, row_count = values_ref.shape
    rows_each = comp_count // peers * SUB
    for comp in range(comp_count):
        values_wide[comp * sub_count : (comp + 1) * sub_count, :] = values_ref[comp].astype(jnp.float32)
    cells = lax.broadcasted_iota(jnp.int32, (SUB, row_count), 0).astype(jnp.float32) * (2.0 / TAPS)

    def one_sub(sub):
        row_taps = taper(cells - places_ref[0, pl.ds(sub, 1), :] * (2.0 / TAPS)).astype(jnp.bfloat16)
        col_taps = taper(cells - places_ref[1, pl.ds(sub, 1), :] * (2.0 / TAPS))
        weighted = jnp.concatenate(
            [
                (values_wide[pl.ds(comp * sub_count + sub, 1), :] * col_taps).astype(jnp.bfloat16)
                for comp in range(comp_count)
            ],
            axis=0,
        )
        return lax.dot_general(
            weighted, row_taps, (((1,), (1,)), ((), ())), preferred_element_type=jnp.float32
        )

    def some_subs(turn, carry):
        for pair in range(STEP // 2):
            sub = turn * STEP + pair * 2
            sums[pair] = jnp.concatenate([one_sub(sub), one_sub(sub + 1)], axis=1).astype(jnp.bfloat16)
        for pair in range(STEP // 2):
            for mask in range(peers):
                rows = pl.ds(pl.multiple_of((me_ref[0] ^ mask) * rows_each, rows_each), rows_each)
                target = sent_ref if mask % 2 else kept_ref
                target[mask // 2, turn * (STEP // 2) + pair] = sums[pair, rows, :]
        return carry

    lax.fori_loop(*turns, some_subs, 0)
    if first:
        for copy in zero_copies:
            copy.wait()


def grid_parts(values, places, peers, chunk, turns, order=None, numbers=(), earlier=()):
    comp_count, all_subs, row_count = values.shape
    sub_count = all_subs // 2
    rows_each = comp_count // peers * SUB
    first = order is None
    me = lax.axis_index("tm").astype(jnp.int32).reshape(1)
    parts_shape = (peers // 2, turns[1] * STEP // 2, rows_each, LANES)
    values_block, places_block = (comp_count, sub_count, row_count), (2, sub_count, row_count)
    out_shape = [jax.ShapeDtypeStruct(parts_shape, jnp.bfloat16)] * 2
    out_specs = [pl.BlockSpec(parts_shape, lambda i: (0, 0, 0, 0))] * 2
    scratch = [
        pltpu.VMEM((comp_count * sub_count, row_count), jnp.float32),
        pltpu.VMEM((STEP // 2, comp_count * SUB, LANES), jnp.bfloat16),
    ]
    if first:
        values, places = (pltpu.with_memory_space_constraint(array, pltpu.HBM) for array in (values, places))
        in_specs = [pl.BlockSpec(memory_space=pltpu.HBM)] * 2
        out_shape.append(jax.ShapeDtypeStruct((rows_each // SUB, W, TU, NV), jnp.float32))
        out_specs.append(ANY)
        scratch += [
            pltpu.VMEM((rows_each // SUB, TU, NV), jnp.float32),
            pltpu.SemaphoreType.DMA((W,)),
            pltpu.VMEM(values_block, values.dtype),
            pltpu.VMEM(places_block, places.dtype),
            pltpu.SemaphoreType.DMA((2,)),
        ]
        more = []
    else:
        in_specs = [pl.BlockSpec(block, lambda i: (0, chunk, 0)) for block in (values_block, places_block)]
        in_specs += [ANY] + [pl.BlockSpec((1, all_subs), lambda i: (0, 0))] * len(numbers)
        in_specs += [pl.BlockSpec(array.shape, lambda i: (0, 0, 0, 0)) for array in earlier]
        more = [order, *numbers, *earlier]
        if numbers:
            out_shape.append(jax.ShapeDtypeStruct((META, all_subs), jnp.bfloat16))
            out_specs.append(pl.BlockSpec((META, all_subs), lambda i: (0, 0)))
    return pl.pallas_call(
        functools.partial(grid_kernel, peers=peers, first=first, turns=turns, earlier=bool(earlier)),
        grid=(1,),
        out_shape=out_shape,
        in_specs=[SMEM] + in_specs,
        out_specs=out_specs,
        scratch_shapes=scratch,
        compiler_params=pltpu.CompilerParams(vmem_limit_bytes=48 << 20),
        cost_estimate=pl.CostEstimate(
            flops=8 * (turns[1] - turns[0]) * STEP * row_count * SUB * SUB * comp_count,
            bytes_accessed=2 << 20,
            transcendentals=0,
        ),
    )(me, values, places, *more)


def halve_kernel(kept_ref, arrived_ref, *rest):
    next_kept_ref, next_sent_ref = rest[-2:]
    for at in range(kept_ref.shape[0]):
        total = kept_ref[at].astype(jnp.float32) + arrived_ref[at].astype(jnp.float32)
        if at % 2:
            next_sent_ref[at // 2] = total.astype(jnp.bfloat16)
        else:
            next_kept_ref[at // 2] = total


def halve(kept, arrived, order):
    shape = (kept.shape[0] // 2,) + kept.shape[1:]
    return pl.pallas_call(
        halve_kernel,
        out_shape=[jax.ShapeDtypeStruct(shape, jnp.float32), jax.ShapeDtypeStruct(shape, jnp.bfloat16)],
        in_specs=[VMEM] * 2 + [ANY] * len(order),
        out_specs=[VMEM] * 2,
        compiler_params=pltpu.CompilerParams(vmem_limit_bytes=8 << 20),
        cost_estimate=pl.CostEstimate(flops=1 << 18, bytes_accessed=1 << 20, transcendentals=0),
    )(kept, arrived, *order)


def paired(array, axis, mask):
    return lax.ppermute(array, axis, [(i, i ^ mask) for i in range(lax.axis_size(axis))])


def halve_all(kept, sent, axis, order):
    mask = 1
    while kept.shape[0] > 1:
        kept, sent = halve(kept, paired(sent, axis, mask), order)
        mask *= 2
    return kept, sent


def turning(chunk_numbers, sub, lanes):
    row_offsets = chunk_numbers[1:2, sub : sub + 2]
    col_shifts = chunk_numbers[4:5, sub : sub + 2]
    to = lax.broadcasted_iota(jnp.int32, (2 * SUB, 2 * SUB), 0)
    of = lax.broadcasted_iota(jnp.int32, (2 * SUB, 2 * SUB), 1)
    turned = jnp.where(of < SUB, row_offsets[:, 0:1], row_offsets[:, 1:2]) & (SUBLANES - 1)
    rows = (to == (of & SUB) + ((of + turned) & (SUB - 1))).astype(jnp.bfloat16)
    to = lax.broadcasted_iota(jnp.int32, (lanes, LANES), 1)
    of = lax.broadcasted_iota(jnp.int32, (lanes, LANES), 0)
    cols = [
        (to == ((of + col_shifts[:, which : which + 1]) & (LANES - 1))).astype(jnp.bfloat16) for which in range(2)
    ]
    return rows, cols


def sum_kernel(kept_ref, arrived_ref, numbers_ref, *rest, hops, first_sub):
    pairs, lanes = kept_ref.shape[1:3]
    group = min(lanes, LANES)
    out_ref = rest[hops or 1]
    numbers = numbers_ref[...].astype(jnp.float32).astype(jnp.int32)
    for pair in range(pairs):
        total = kept_ref[0, pair].astype(jnp.float32) + arrived_ref[0, pair].astype(jnp.float32)
        rows, cols = turning(numbers, first_sub + 2 * pair, group)
        total = lax.dot_general(
            rows, total.astype(jnp.bfloat16), (((1,), (1,)), ((), ())), preferred_element_type=jnp.float32
        ).astype(jnp.bfloat16)
        for which in range(2):
            at = (pair * 2 + which) * SUB
            for left in range(0, lanes, group):
                out_ref[at : at + SUB, left : left + LANES] = jnp.dot(
                    total[which * SUB : (which + 1) * SUB, left : left + group],
                    cols[which],
                    preferred_element_type=jnp.float32,
                ).astype(jnp.bfloat16)
    if hops:
        near_ref, go_ref = rest[hops + 1 :]
        go_ref[...] = jnp.zeros(go_ref.shape, jnp.int32)
        for at in range(hops):
            near_ref[at] = rest[at][: near_ref.shape[1], :]
    else:
        both = [ref[...].astype(jnp.float32) for ref in (numbers_ref, rest[0])]
        blank = jnp.zeros((META, out_ref.shape[1] - 2 * both[0].shape[1]), jnp.float32)
        out_ref[pairs * 2 * SUB :, :] = jnp.concatenate(both + [blank], axis=1).astype(jnp.bfloat16)


def sum_parts(kept, arrived, first_sub, own_numbers, hops, other_numbers):
    _, pairs, lanes, _ = kept.shape
    rows = pairs * 2 * SUB
    lanes = max(lanes, LANES)
    out_shape = [jax.ShapeDtypeStruct((rows if hops else rows + META, lanes), jnp.bfloat16)]
    if hops:
        out_shape.append(jax.ShapeDtypeStruct((len(hops), rows, lanes), jnp.bfloat16))
        out_shape.append(jax.ShapeDtypeStruct((SUBLANES, LANES), jnp.int32))
    return pl.pallas_call(
        functools.partial(sum_kernel, hops=len(hops), first_sub=first_sub),
        out_shape=out_shape,
        in_specs=[VMEM] * (3 + len(hops) + len(other_numbers)),
        out_specs=[VMEM] * len(out_shape),
        compiler_params=pltpu.CompilerParams(vmem_limit_bytes=8 << 20),
        cost_estimate=pl.CostEstimate(flops=1 << 20, bytes_accessed=2 << 20, transcendentals=0),
    )(kept, arrived, own_numbers, *hops, *other_numbers)


def across(array, axis):
    return [array] + [paired(array, axis, mask) for mask in range(2, lax.axis_size(axis), 2)]


def touch_plan(starts, planes, cols, spots, others):
    total = starts.shape[0]
    ids = jnp.arange(total, dtype=jnp.int32)
    taken = starts >= 0
    keys = jnp.where(taken, planes, W) * total + ids
    left = jnp.where(taken, planes * BLOCKS + cols // LANES, -1)
    right = jnp.where(taken & (cols % LANES > LANES - SUB), left + 1, -2)
    before = keys[None, :] < keys[:, None]
    after = keys[None, :] > keys[:, None]
    rank = jnp.sum(before.astype(jnp.int32), axis=1)

    def edges(units):
        same = (left[None, :] == units[:, None]) | (right[None, :] == units[:, None])
        first = ~jnp.any(same & before, axis=1)
        last = ~jnp.any(same & after, axis=1)
        return first.astype(jnp.int32) + 2 * last.astype(jnp.int32)

    flags = edges(left) + jnp.where(right >= 0, 4 * edges(right), 0) + 16 * others
    fields = jnp.stack([starts, cols, planes, spots, flags], axis=0)
    moved = jnp.where(rank[None, None, :] == ids[None, :, None], fields[:, None, :], 0)
    table = jnp.sum(moved, axis=2)
    number = jnp.sum(taken.astype(jnp.int32))
    return jnp.concatenate([table, jnp.full((1, total), number, jnp.int32)], axis=0)


def place_kernel(table_ref, near_ref, other_ref, _, out_ref, canvas, sem):
    comp_count = canvas.shape[1]
    number = table_ref[5, 0]
    row = lax.broadcasted_iota(jnp.int32, (SUB + SUBLANES, LANES), 0)
    lane = lax.broadcasted_iota(jnp.int32, (SUB + SUBLANES, LANES), 1)

    def lanes_of(block):
        return pl.ds(pl.multiple_of(block * LANES, LANES), LANES)

    def out_copy(plane, block):
        return pltpu.make_async_copy(
            canvas.at[plane, :, pl.ds(SUB, TU), lanes_of(block)],
            out_ref.at[:, plane, :, lanes_of(block)],
            sem.at[plane, block],
        )

    def clear(plane, block):
        canvas[plane, :, pl.ds(SUB, TU), lanes_of(block)] = jnp.zeros((comp_count, TU, LANES), jnp.float32)

    def when_set(flags, bit, act):
        @pl.when((flags & bit) != 0)
        def _():
            act()

    def patch_of(index):
        spot = table_ref[3, index]
        block = spot >> 16
        at = pl.ds(pl.multiple_of(spot & 0xFFFF, SUB), SUB)
        patch = jnp.where((table_ref[4, index] & 16) != 0, other_ref[block, at, :], near_ref[block, at, :])
        patch = patch.astype(jnp.float32)
        patches = []
        for comp in range(comp_count):
            values = patch[:, comp // 2 * LANES : (comp // 2 + 1) * LANES]
            if comp % 2:
                values = pltpu.roll(values, SUB, 1)
            patches.append(jnp.concatenate([values, values[:SUBLANES]], axis=0))
        return patches

    def add_patch(index, patches):
        start = table_ref[0, index]
        col = table_ref[1, index]
        plane = table_ref[2, index]
        flags = table_ref[4, index]
        block = col >> 7
        shift = col & (LANES - 1)
        skip = start & (SUBLANES - 1)
        rows = pl.ds(pl.multiple_of(start - skip, SUBLANES), SUB + SUBLANES)
        inside = (row >= skip) & (row < skip + SUB)
        when_set(flags, 1, lambda: clear(plane, block))
        here = inside & (lane >= shift) & (lane < shift + SUB)
        for comp in range(comp_count):
            canvas[plane, comp, rows, lanes_of(block)] += jnp.where(here, patches[comp], 0.0)
        when_set(flags, 2, lambda: out_copy(plane, block).start())

        @pl.when(shift > LANES - SUB)
        def _():
            when_set(flags, 4, lambda: clear(plane, block + 1))
            there = inside & (lane < shift + SUB - LANES)
            for comp in range(comp_count):
                canvas[plane, comp, rows, lanes_of(block + 1)] += jnp.where(there, patches[comp], 0.0)
            when_set(flags, 8, lambda: out_copy(plane, block + 1).start())

    def add_two(turn_index, carry):
        index = turn_index * 2
        first, second = patch_of(index), patch_of(index + 1)
        add_patch(index, first)

        @pl.when(index + 1 < number)
        def _():
            add_patch(index + 1, second)

        return carry

    def finish(index, carry):
        block = table_ref[1, index] >> 7
        plane = table_ref[2, index]
        flags = table_ref[4, index]
        when_set(flags, 2, lambda: out_copy(plane, block).wait())
        when_set(flags, 8, lambda: out_copy(plane, block + 1).wait())
        return carry

    lax.fori_loop(0, (number + 1) // 2, add_two, 0)
    lax.fori_loop(0, number, finish, 0)


def place_all(near, other, table, tile_grid):
    comp_count = tile_grid.shape[0]
    return pl.pallas_call(
        place_kernel,
        out_shape=jax.ShapeDtypeStruct(tile_grid.shape, jnp.float32),
        in_specs=[SMEM, VMEM, VMEM, ANY],
        out_specs=ANY,
        scratch_shapes=[
            pltpu.VMEM((W, comp_count, TU + 2 * SUB, NV), jnp.float32),
            pltpu.SemaphoreType.DMA((W, BLOCKS)),
        ],
        input_output_aliases={3: 0},
        compiler_params=pltpu.CompilerParams(vmem_limit_bytes=44 << 20),
        cost_estimate=pl.CostEstimate(flops=0, bytes_accessed=16 << 20, transcendentals=0),
    )(table, near, other, tile_grid)


def body(visibilities, positions, owner, w_plane, row_offset, col_offset):
    peers = lax.axis_size("tm")
    tiles = lax.axis_size("uv")
    sub_count = visibilities.shape[1]
    comp_count = visibilities.shape[0] // peers
    tile = lax.axis_index("uv")
    half = sub_count // 2

    split = half // STEP // 2
    *parts_a, tile_grid = grid_parts(visibilities, positions, peers, 0, (0, half // STEP))
    *parts_b, own_numbers = grid_parts(
        visibilities,
        positions,
        peers,
        1,
        (0, split),
        order=tile_grid,
        numbers=(owner.T, row_offset[None], w_plane[None], col_offset[None]),
    )
    other_numbers = paired(own_numbers, "uv", 1)
    kept_a, sent_a = halve_all(*parts_a, "tm", [other_numbers])
    parts_b = grid_parts(visibilities, positions, peers, 1, (split, half // STEP), order=sent_a, earlier=parts_b)
    kept_b, sent_b = halve_all(*parts_b, "tm", [])
    arrived_a, arrived_b = (paired(sent, "tm", peers // 2) for sent in (sent_a, sent_b))
    (sum_a,) = sum_parts(kept_a, arrived_a, 0, own_numbers, [], [other_numbers])
    hops_a = across(sum_a, "uv")
    sum_b, near_a, go = sum_parts(kept_b, arrived_b, half, own_numbers, hops_a, [])
    near = jnp.concatenate([near_a, jnp.stack(across(sum_b, "uv"), axis=0)], axis=0)
    other = paired(near, "uv", 1)

    told = jnp.stack([hop[half * SUB :, : 2 * sub_count] for hop in hops_a], axis=1).astype(jnp.float32).astype(jnp.int32)
    chips = told.shape[1]
    told = told.reshape(META, -1) + go[0, 0]
    entry = jnp.arange(told.shape[1], dtype=jnp.int32)
    chip, sub = entry // (2 * sub_count), entry % sub_count
    others = entry // sub_count % 2
    spots = ((sub // half * chips + chip) << 16) + sub % half * SUB
    ahead = (told[0] - tile) % tiles
    starts = jnp.where(ahead == 0, told[1] + SUB, jnp.where(ahead == tiles - 1, told[1] + SUB - TU, -1))
    table = touch_plan(starts, told[2], told[3] * LANES + told[4], spots, others)
    return place_all(near, other, table, tile_grid)


def solution(mesh):
    placed = (P(None, "uv", "tm"), P(None, "uv", "tm"), P("uv", None), P("uv"), P("uv"), P("uv"))
    return jax.shard_map(
        body, mesh=mesh, in_specs=placed, out_specs=P("tm", None, "uv", None), check_vma=False
    )
```

```python
import functools
import math

import jax
import jax.numpy as jnp
from jax import lax
from jax.experimental import pallas as pl
from jax.experimental.pallas import tpu as pltpu
from jax.sharding import PartitionSpec as P

W = 8
SUB = 64
TAPS = 8
TU = 128
NV = 2048
LANES = 128
SUBLANES = 8
BLOCKS = NV // LANES
META = 16
MIXED = 256
STEP = 4

VMEM = pl.BlockSpec(memory_space=pltpu.VMEM)
SMEM = pl.BlockSpec(memory_space=pltpu.SMEM)
ANY = pl.BlockSpec(memory_space=pl.ANY)


def taper(scaled):
    inner = jnp.maximum(0.0, 1.0 - scaled * scaled)
    return inner * inner


def number_rows(owner, row_offset, w_plane, col_offset):
    rows = [owner, row_offset, w_plane, col_offset // LANES, col_offset % LANES]
    blank = jnp.zeros((META - len(rows), owner.shape[1]), jnp.int32)
    return jnp.concatenate(rows + [blank], axis=0).astype(jnp.float32).astype(jnp.bfloat16)


def grid_kernel(me_ref, values_ref, places_ref, *rest, peers, first, turns, earlier):
    if first:
        kept_ref, sent_ref, out_ref, values_wide, sums, blank, sem, values, places, in_sem = rest
        _, sub_count, row_count = values.shape
        in_copies = [
            pltpu.make_async_copy(values_ref.at[:, pl.ds(0, sub_count), :], values, in_sem.at[0]),
            pltpu.make_async_copy(places_ref.at[:, pl.ds(0, sub_count), :], places, in_sem.at[1]),
        ]
        for copy in in_copies:
            copy.start()
        blank[...] = jnp.zeros(blank.shape, jnp.float32)
        zero_copies = [pltpu.make_async_copy(blank, out_ref.at[:, plane], sem.at[plane]) for plane in range(W)]
        for copy in in_copies:
            copy.wait()
        for copy in zero_copies:
            copy.start()
        values_ref, places_ref = values, places
    else:
        rest = rest[1:]
        if earlier:
            earlier_kept, earlier_sent, kept_ref, sent_ref, values_wide, sums = rest
            done = earlier_kept.shape[1]
            kept_ref[:, :done] = earlier_kept[...]
            sent_ref[:, :done] = earlier_sent[...]
        else:
            owner_ref, row_ref, plane_ref, col_ref, kept_ref, sent_ref, numbers_ref, values_wide, sums = rest
            numbers_ref[...] = number_rows(owner_ref[...], row_ref[...], plane_ref[...], col_ref[...])
    comp_count, sub_count, row_count = values_ref.shape
    rows_each = comp_count // peers * SUB
    for comp in range(comp_count):
        values_wide[comp * sub_count : (comp + 1) * sub_count, :] = values_ref[comp].astype(jnp.float32)
    span = math.gcd(row_count, MIXED)
    cells = lax.broadcasted_iota(jnp.int32, (SUB, span), 0).astype(jnp.float32) * (2.0 / TAPS)

    def one_sub(sub):
        straight = jnp.zeros((comp_count * SUB, SUB), jnp.float32)
        crossed = jnp.zeros((SUB, comp_count * SUB), jnp.float32)
        for at in range(0, row_count, span):
            some = slice(at, at + span)
            row_taps = taper(cells - places_ref[0, pl.ds(sub, 1), some] * (2.0 / TAPS)).astype(jnp.bfloat16)
            col_taps = taper(cells - places_ref[1, pl.ds(sub, 1), some] * (2.0 / TAPS))
            weighted = jnp.concatenate(
                [
                    (values_wide[pl.ds(comp * sub_count + sub, 1), some] * col_taps).astype(jnp.bfloat16)
                    for comp in range(comp_count)
                ],
                axis=0,
            )
            last = (((1,), (1,)), ((), ()))
            if at // span % 2:
                crossed += lax.dot_general(row_taps, weighted, last, preferred_element_type=jnp.float32)
            else:
                straight += lax.dot_general(weighted, row_taps, last, preferred_element_type=jnp.float32)
        return straight + jnp.transpose(crossed)

    def some_subs(turn, carry):
        for pair in range(STEP // 2):
            sub = turn * STEP + pair * 2
            sums[pair] = jnp.concatenate([one_sub(sub), one_sub(sub + 1)], axis=1).astype(jnp.bfloat16)
        for pair in range(STEP // 2):
            for mask in range(peers):
                rows = pl.ds(pl.multiple_of((me_ref[0] ^ mask) * rows_each, rows_each), rows_each)
                target = sent_ref if mask % 2 else kept_ref
                target[mask // 2, turn * (STEP // 2) + pair] = sums[pair, rows, :]
        return carry

    lax.fori_loop(*turns, some_subs, 0)
    if first:
        for copy in zero_copies:
            copy.wait()


def grid_parts(values, places, peers, chunk, turns, order=None, numbers=(), earlier=()):
    comp_count, all_subs, row_count = values.shape
    sub_count = all_subs // 2
    rows_each = comp_count // peers * SUB
    first = order is None
    me = lax.axis_index("tm").astype(jnp.int32).reshape(1)
    parts_shape = (peers // 2, turns[1] * STEP // 2, rows_each, LANES)
    values_block, places_block = (comp_count, sub_count, row_count), (2, sub_count, row_count)
    out_shape = [jax.ShapeDtypeStruct(parts_shape, jnp.bfloat16)] * 2
    out_specs = [pl.BlockSpec(parts_shape, lambda i: (0, 0, 0, 0))] * 2
    scratch = [
        pltpu.VMEM((comp_count * sub_count, row_count), jnp.float32),
        pltpu.VMEM((STEP // 2, comp_count * SUB, LANES), jnp.bfloat16),
    ]
    if first:
        values, places = (pltpu.with_memory_space_constraint(array, pltpu.HBM) for array in (values, places))
        in_specs = [pl.BlockSpec(memory_space=pltpu.HBM)] * 2
        out_shape.append(jax.ShapeDtypeStruct((rows_each // SUB, W, TU, NV), jnp.float32))
        out_specs.append(ANY)
        scratch += [
            pltpu.VMEM((rows_each // SUB, TU, NV), jnp.float32),
            pltpu.SemaphoreType.DMA((W,)),
            pltpu.VMEM(values_block, values.dtype),
            pltpu.VMEM(places_block, places.dtype),
            pltpu.SemaphoreType.DMA((2,)),
        ]
        more = []
    else:
        in_specs = [pl.BlockSpec(block, lambda i: (0, chunk, 0)) for block in (values_block, places_block)]
        in_specs += [ANY] + [pl.BlockSpec((1, all_subs), lambda i: (0, 0))] * len(numbers)
        in_specs += [pl.BlockSpec(array.shape, lambda i: (0, 0, 0, 0)) for array in earlier]
        more = [order, *numbers, *earlier]
        if numbers:
            out_shape.append(jax.ShapeDtypeStruct((META, all_subs), jnp.bfloat16))
            out_specs.append(pl.BlockSpec((META, all_subs), lambda i: (0, 0)))
    return pl.pallas_call(
        functools.partial(grid_kernel, peers=peers, first=first, turns=turns, earlier=bool(earlier)),
        grid=(1,),
        out_shape=out_shape,
        in_specs=[SMEM] + in_specs,
        out_specs=out_specs,
        scratch_shapes=scratch,
        compiler_params=pltpu.CompilerParams(vmem_limit_bytes=48 << 20),
        cost_estimate=pl.CostEstimate(
            flops=8 * (turns[1] - turns[0]) * STEP * row_count * SUB * SUB * comp_count,
            bytes_accessed=2 << 20,
            transcendentals=0,
        ),
    )(me, values, places, *more)


def halve_kernel(kept_ref, arrived_ref, *rest):
    next_kept_ref, next_sent_ref = rest[-2:]
    for at in range(kept_ref.shape[0]):
        total = kept_ref[at].astype(jnp.float32) + arrived_ref[at].astype(jnp.float32)
        if at % 2:
            next_sent_ref[at // 2] = total.astype(jnp.bfloat16)
        else:
            next_kept_ref[at // 2] = total


def halve(kept, arrived, order):
    shape = (kept.shape[0] // 2,) + kept.shape[1:]
    return pl.pallas_call(
        halve_kernel,
        out_shape=[jax.ShapeDtypeStruct(shape, jnp.float32), jax.ShapeDtypeStruct(shape, jnp.bfloat16)],
        in_specs=[VMEM] * 2 + [ANY] * len(order),
        out_specs=[VMEM] * 2,
        compiler_params=pltpu.CompilerParams(vmem_limit_bytes=8 << 20),
        cost_estimate=pl.CostEstimate(flops=1 << 18, bytes_accessed=1 << 20, transcendentals=0),
    )(kept, arrived, *order)


def paired(array, axis, mask):
    return lax.ppermute(array, axis, [(i, i ^ mask) for i in range(lax.axis_size(axis))])


def halve_all(kept, sent, axis, order):
    mask = 1
    while kept.shape[0] > 1:
        kept, sent = halve(kept, paired(sent, axis, mask), order)
        mask *= 2
    return kept, sent


def turning(chunk_numbers, sub, lanes):
    row_offsets = chunk_numbers[1:2, sub : sub + 2]
    col_shifts = chunk_numbers[4:5, sub : sub + 2]
    to = lax.broadcasted_iota(jnp.int32, (2 * SUB, 2 * SUB), 0)
    of = lax.broadcasted_iota(jnp.int32, (2 * SUB, 2 * SUB), 1)
    turned = jnp.where(of < SUB, row_offsets[:, 0:1], row_offsets[:, 1:2]) & (SUBLANES - 1)
    rows = (to == (of & SUB) + ((of + turned) & (SUB - 1))).astype(jnp.bfloat16)
    to = lax.broadcasted_iota(jnp.int32, (lanes, LANES), 1)
    of = lax.broadcasted_iota(jnp.int32, (lanes, LANES), 0)
    cols = [
        (to == ((of + col_shifts[:, which : which + 1]) & (LANES - 1))).astype(jnp.bfloat16) for which in range(2)
    ]
    return rows, cols


def sum_kernel(kept_ref, arrived_ref, numbers_ref, *rest, hops, first_sub):
    pairs, lanes = kept_ref.shape[1:3]
    group = min(lanes, LANES)
    out_ref = rest[hops or 1]
    numbers = numbers_ref[...].astype(jnp.float32).astype(jnp.int32)
    for pair in range(pairs):
        total = kept_ref[0, pair].astype(jnp.float32) + arrived_ref[0, pair].astype(jnp.float32)
        rows, cols = turning(numbers, first_sub + 2 * pair, group)
        total = lax.dot_general(
            rows, total.astype(jnp.bfloat16), (((1,), (1,)), ((), ())), preferred_element_type=jnp.float32
        ).astype(jnp.bfloat16)
        for which in range(2):
            at = (pair * 2 + which) * SUB
            for left in range(0, lanes, group):
                out_ref[at : at + SUB, left : left + LANES] = jnp.dot(
                    total[which * SUB : (which + 1) * SUB, left : left + group],
                    cols[which],
                    preferred_element_type=jnp.float32,
                ).astype(jnp.bfloat16)
    if hops:
        near_ref, go_ref = rest[hops + 1 :]
        go_ref[...] = jnp.zeros(go_ref.shape, jnp.int32)
        for at in range(hops):
            near_ref[at] = rest[at][: near_ref.shape[1], :]
    else:
        both = [ref[...].astype(jnp.float32) for ref in (numbers_ref, rest[0])]
        blank = jnp.zeros((META, out_ref.shape[1] - 2 * both[0].shape[1]), jnp.float32)
        out_ref[pairs * 2 * SUB :, :] = jnp.concatenate(both + [blank], axis=1).astype(jnp.bfloat16)


def sum_parts(kept, arrived, first_sub, own_numbers, hops, other_numbers):
    _, pairs, lanes, _ = kept.shape
    rows = pairs * 2 * SUB
    lanes = max(lanes, LANES)
    out_shape = [jax.ShapeDtypeStruct((rows if hops else rows + META, lanes), jnp.bfloat16)]
    if hops:
        out_shape.append(jax.ShapeDtypeStruct((len(hops), rows, lanes), jnp.bfloat16))
        out_shape.append(jax.ShapeDtypeStruct((SUBLANES, LANES), jnp.int32))
    return pl.pallas_call(
        functools.partial(sum_kernel, hops=len(hops), first_sub=first_sub),
        out_shape=out_shape,
        in_specs=[VMEM] * (3 + len(hops) + len(other_numbers)),
        out_specs=[VMEM] * len(out_shape),
        compiler_params=pltpu.CompilerParams(vmem_limit_bytes=8 << 20),
        cost_estimate=pl.CostEstimate(flops=1 << 20, bytes_accessed=2 << 20, transcendentals=0),
    )(kept, arrived, own_numbers, *hops, *other_numbers)


def across(array, axis):
    return [array] + [paired(array, axis, mask) for mask in range(2, lax.axis_size(axis), 2)]


def touch_plan(starts, planes, cols, spots, others):
    total = starts.shape[0]
    ids = jnp.arange(total, dtype=jnp.int32)
    taken = starts >= 0
    keys = jnp.where(taken, planes, W) * total + ids
    left = jnp.where(taken, planes * BLOCKS + cols // LANES, -1)
    right = jnp.where(taken & (cols % LANES > LANES - SUB), left + 1, -2)
    before = keys[None, :] < keys[:, None]
    after = keys[None, :] > keys[:, None]
    rank = jnp.sum(before.astype(jnp.int32), axis=1)

    def edges(units):
        same = (left[None, :] == units[:, None]) | (right[None, :] == units[:, None])
        first = ~jnp.any(same & before, axis=1)
        last = ~jnp.any(same & after, axis=1)
        return first.astype(jnp.int32) + 2 * last.astype(jnp.int32)

    flags = edges(left) + jnp.where(right >= 0, 4 * edges(right), 0) + 16 * others
    fields = jnp.stack([starts, cols, planes, spots, flags], axis=0)
    moved = jnp.where(rank[None, None, :] == ids[None, :, None], fields[:, None, :], 0)
    table = jnp.sum(moved, axis=2)
    number = jnp.sum(taken.astype(jnp.int32))
    return jnp.concatenate([table, jnp.full((1, total), number, jnp.int32)], axis=0)


def place_kernel(table_ref, near_ref, other_ref, _, out_ref, canvas, sem):
    comp_count = canvas.shape[1]
    number = table_ref[5, 0]
    row = lax.broadcasted_iota(jnp.int32, (1, SUBLANES, LANES), 1)
    lane = lax.broadcasted_iota(jnp.int32, (1, SUBLANES, LANES), 2)

    def lanes_of(block):
        return pl.ds(pl.multiple_of(block * LANES, LANES), LANES)

    def out_copy(plane, block):
        return pltpu.make_async_copy(
            canvas.at[plane, :, pl.ds(SUB, TU), lanes_of(block)],
            out_ref.at[:, plane, :, lanes_of(block)],
            sem.at[plane, block],
        )

    def clear(plane, block):
        canvas[plane, :, pl.ds(SUB, TU), lanes_of(block)] = jnp.zeros((comp_count, TU, LANES), jnp.float32)

    def when_set(flags, bit, act):
        @pl.when((flags & bit) != 0)
        def _():
            act()

    def patch_of(index):
        spot = table_ref[3, index]
        block = spot >> 16
        at = pl.ds(pl.multiple_of(spot & 0xFFFF, SUB), SUB)
        patch = jnp.where((table_ref[4, index] & 16) != 0, other_ref[block, at, :], near_ref[block, at, :])
        patch = patch.astype(jnp.float32)
        patches = []
        skip = table_ref[0, index] & (SUBLANES - 1)
        for comp in range(comp_count):
            values = patch[:, comp // 2 * LANES : (comp // 2 + 1) * LANES]
            if comp % 2:
                values = pltpu.roll(values, SUB, 1)
            values = values.reshape(SUB // SUBLANES, SUBLANES, LANES)
            head = jnp.where(row >= skip, values[:1], 0.0)
            tail = jnp.where(row < skip, values[:1], 0.0)
            patches.append(jnp.concatenate([head, values[1:], tail], axis=0))
        return patches

    def add_patch(index, patches):
        start = table_ref[0, index]
        col = table_ref[1, index]
        plane = table_ref[2, index]
        flags = table_ref[4, index]
        block = col >> 7
        shift = col & (LANES - 1)
        rows = pl.ds(pl.multiple_of(start & ~(SUBLANES - 1), SUBLANES), SUB + SUBLANES)

        def add(at, here):
            for comp in range(comp_count):
                values = jnp.where(here, patches[comp], 0.0).reshape(SUB + SUBLANES, LANES)
                canvas[plane, comp, rows, lanes_of(at)] += values

        when_set(flags, 1, lambda: clear(plane, block))
        add(block, (lane >= shift) & (lane < shift + SUB))
        when_set(flags, 2, lambda: out_copy(plane, block).start())

        @pl.when(shift > LANES - SUB)
        def _():
            when_set(flags, 4, lambda: clear(plane, block + 1))
            add(block + 1, lane < shift + SUB - LANES)
            when_set(flags, 8, lambda: out_copy(plane, block + 1).start())

    def add_two(turn_index, carry):
        index = turn_index * 4
        several = [patch_of(index + more) for more in range(4)]
        add_patch(index, several[0])
        for more in range(1, 4):

            @pl.when(index + more < number)
            def _(more=more):
                add_patch(index + more, several[more])

        return carry

    def finish(index, carry):
        block = table_ref[1, index] >> 7
        plane = table_ref[2, index]
        flags = table_ref[4, index]
        when_set(flags, 2, lambda: out_copy(plane, block).wait())
        when_set(flags, 8, lambda: out_copy(plane, block + 1).wait())
        return carry

    lax.fori_loop(0, (number + 3) // 4, add_two, 0)
    lax.fori_loop(0, number, finish, 0)


def place_all(near, other, table, tile_grid):
    comp_count = tile_grid.shape[0]
    return pl.pallas_call(
        place_kernel,
        out_shape=jax.ShapeDtypeStruct(tile_grid.shape, jnp.float32),
        in_specs=[SMEM, VMEM, VMEM, ANY],
        out_specs=ANY,
        scratch_shapes=[
            pltpu.VMEM((W, comp_count, TU + 2 * SUB, NV), jnp.float32),
            pltpu.SemaphoreType.DMA((W, BLOCKS)),
        ],
        input_output_aliases={3: 0},
        compiler_params=pltpu.CompilerParams(vmem_limit_bytes=44 << 20),
        cost_estimate=pl.CostEstimate(flops=0, bytes_accessed=16 << 20, transcendentals=0),
    )(table, near, other, tile_grid)


def body(visibilities, positions, owner, w_plane, row_offset, col_offset):
    peers = lax.axis_size("tm")
    tiles = lax.axis_size("uv")
    sub_count = visibilities.shape[1]
    comp_count = visibilities.shape[0] // peers
    tile = lax.axis_index("uv")
    half = sub_count // 2

    split = half // STEP // 2
    *parts_a, tile_grid = grid_parts(visibilities, positions, peers, 0, (0, half // STEP))
    *parts_b, own_numbers = grid_parts(
        visibilities,
        positions,
        peers,
        1,
        (0, split),
        order=tile_grid,
        numbers=(owner.T, row_offset[None], w_plane[None], col_offset[None]),
    )
    other_numbers = paired(own_numbers, "uv", 1)
    kept_a, sent_a = halve_all(*parts_a, "tm", [other_numbers])
    parts_b = grid_parts(visibilities, positions, peers, 1, (split, half // STEP), order=sent_a, earlier=parts_b)
    kept_b, sent_b = halve_all(*parts_b, "tm", [])
    arrived_a, arrived_b = (paired(sent, "tm", peers // 2) for sent in (sent_a, sent_b))
    (sum_a,) = sum_parts(kept_a, arrived_a, 0, own_numbers, [], [other_numbers])
    hops_a = across(sum_a, "uv")
    sum_b, near_a, go = sum_parts(kept_b, arrived_b, half, own_numbers, hops_a, [])
    near = jnp.concatenate([near_a, jnp.stack(across(sum_b, "uv"), axis=0)], axis=0)
    other = paired(near, "uv", 1)

    told = jnp.stack([hop[half * SUB :, : 2 * sub_count] for hop in hops_a], axis=1).astype(jnp.float32).astype(jnp.int32)
    chips = told.shape[1]
    told = told.reshape(META, -1) + go[0, 0]
    entry = jnp.arange(told.shape[1], dtype=jnp.int32)
    chip, sub = entry // (2 * sub_count), entry % sub_count
    others = entry // sub_count % 2
    spots = ((sub // half * chips + chip) << 16) + sub % half * SUB
    ahead = (told[0] - tile) % tiles
    starts = jnp.where(ahead == 0, told[1] + SUB, jnp.where(ahead == tiles - 1, told[1] + SUB - TU, -1))
    table = touch_plan(starts, told[2], told[3] * LANES + told[4], spots, others)
    return place_all(near, other, table, tile_grid)


def solution(mesh):
    placed = (P(None, "uv", "tm"), P(None, "uv", "tm"), P("uv", None), P("uv"), P("uv"), P("uv"))
    return jax.shard_map(
        body, mesh=mesh, in_specs=placed, out_specs=P("tm", None, "uv", None), check_vma=False
    )
```

```python
import functools
import math

import jax
import jax.numpy as jnp
from jax import lax
from jax.experimental import pallas as pl
from jax.experimental.pallas import tpu as pltpu
from jax.sharding import PartitionSpec as P

W = 8
SUB = 64
TAPS = 8
TU = 128
NV = 2048
LANES = 128
SUBLANES = 8
BLOCKS = NV // LANES
META = 16
MIXED = 256
STEP = 4

VMEM = pl.BlockSpec(memory_space=pltpu.VMEM)
SMEM = pl.BlockSpec(memory_space=pltpu.SMEM)
ANY = pl.BlockSpec(memory_space=pl.ANY)


def taper(scaled):
    inner = jnp.maximum(0.0, 1.0 - scaled * scaled)
    return inner * inner


def number_rows(owner, row_offset, w_plane, col_offset):
    rows = [owner, row_offset, w_plane, col_offset // LANES, col_offset % LANES]
    blank = jnp.zeros((META - len(rows), owner.shape[1]), jnp.int32)
    return jnp.concatenate(rows + [blank], axis=0).astype(jnp.float32).astype(jnp.bfloat16)


def grid_kernel(me_ref, values_ref, places_ref, *rest, peers, first, turns, earlier):
    if first:
        places_from, (kept_ref, sent_ref, out_ref, numbers_ref), rest = rest[:4], rest[4:8], rest[8:]
        values_wide, sums, blank, sem, values, places, in_sem, numbers, numbers_sem = rest
        number_copies = [
            pltpu.make_async_copy(source, numbers.at[at], numbers_sem.at[at]) for at, source in enumerate(places_from)
        ]
        for copy in number_copies:
            copy.start()
        _, sub_count, row_count = values.shape
        in_copies = [
            pltpu.make_async_copy(values_ref.at[:, pl.ds(0, sub_count), :], values, in_sem.at[0]),
            pltpu.make_async_copy(places_ref.at[:, pl.ds(0, sub_count), :], places, in_sem.at[1]),
        ]
        for copy in in_copies:
            copy.start()
        blank[...] = jnp.zeros(blank.shape, jnp.float32)
        zero_copies = [pltpu.make_async_copy(blank, out_ref.at[:, plane], sem.at[plane]) for plane in range(W)]
        for copy in in_copies + number_copies:
            copy.wait()
        for copy in zero_copies:
            copy.start()
        numbers_ref[...] = number_rows(*(numbers[at] for at in range(4)))
        values_ref, places_ref = values, places
    else:
        rest = rest[1:]
        if earlier:
            earlier_kept, earlier_sent, kept_ref, sent_ref, values_wide, sums = rest
            done = earlier_kept.shape[1]
            kept_ref[:, :done] = earlier_kept[...]
            sent_ref[:, :done] = earlier_sent[...]
        else:
            kept_ref, sent_ref, values_wide, sums = rest
    comp_count, sub_count, row_count = values_ref.shape
    rows_each = comp_count // peers * SUB
    for comp in range(comp_count):
        values_wide[comp * sub_count : (comp + 1) * sub_count, :] = values_ref[comp].astype(jnp.float32)
    span = math.gcd(row_count, MIXED)
    cells = lax.broadcasted_iota(jnp.int32, (SUB, span), 0).astype(jnp.float32) * (2.0 / TAPS)

    def one_sub(sub):
        straight = jnp.zeros((comp_count * SUB, SUB), jnp.float32)
        crossed = jnp.zeros((SUB, comp_count * SUB), jnp.float32)
        for at in range(0, row_count, span):
            some = slice(at, at + span)
            row_taps = taper(cells - places_ref[0, pl.ds(sub, 1), some] * (2.0 / TAPS)).astype(jnp.bfloat16)
            col_taps = taper(cells - places_ref[1, pl.ds(sub, 1), some] * (2.0 / TAPS))
            weighted = jnp.concatenate(
                [
                    (values_wide[pl.ds(comp * sub_count + sub, 1), some] * col_taps).astype(jnp.bfloat16)
                    for comp in range(comp_count)
                ],
                axis=0,
            )
            last = (((1,), (1,)), ((), ()))
            if at // span % 2:
                crossed += lax.dot_general(row_taps, weighted, last, preferred_element_type=jnp.float32)
            else:
                straight += lax.dot_general(weighted, row_taps, last, preferred_element_type=jnp.float32)
        return straight + jnp.transpose(crossed)

    def some_subs(turn, carry):
        for pair in range(STEP // 2):
            sub = turn * STEP + pair * 2
            sums[pair] = jnp.concatenate([one_sub(sub), one_sub(sub + 1)], axis=1).astype(jnp.bfloat16)
        for pair in range(STEP // 2):
            for mask in range(peers):
                rows = pl.ds(pl.multiple_of((me_ref[0] ^ mask) * rows_each, rows_each), rows_each)
                target = sent_ref if mask % 2 else kept_ref
                target[mask // 2, turn * (STEP // 2) + pair] = sums[pair, rows, :]
        return carry

    lax.fori_loop(*turns, some_subs, 0)
    if first:
        for copy in zero_copies:
            copy.wait()


def grid_parts(values, places, peers, chunk, turns, order=None, numbers=(), earlier=()):
    comp_count, all_subs, row_count = values.shape
    sub_count = all_subs // 2
    rows_each = comp_count // peers * SUB
    first = order is None
    me = lax.axis_index("tm").astype(jnp.int32).reshape(1)
    parts_shape = (peers // 2, turns[1] * STEP // 2, rows_each, LANES)
    values_block, places_block = (comp_count, sub_count, row_count), (2, sub_count, row_count)
    out_shape = [jax.ShapeDtypeStruct(parts_shape, jnp.bfloat16)] * 2
    out_specs = [pl.BlockSpec(parts_shape, lambda i: (0, 0, 0, 0))] * 2
    scratch = [
        pltpu.VMEM((comp_count * sub_count, row_count), jnp.float32),
        pltpu.VMEM((STEP // 2, comp_count * SUB, LANES), jnp.bfloat16),
    ]
    if first:
        values, places = (pltpu.with_memory_space_constraint(array, pltpu.HBM) for array in (values, places))
        in_specs = [pl.BlockSpec(memory_space=pltpu.HBM)] * 2
        in_specs += [pl.BlockSpec(memory_space=pltpu.HBM)] * len(numbers)
        out_shape.append(jax.ShapeDtypeStruct((rows_each // SUB, W, TU, NV), jnp.float32))
        out_shape.append(jax.ShapeDtypeStruct((META, all_subs), jnp.bfloat16))
        out_specs += [ANY, pl.BlockSpec((META, all_subs), lambda i: (0, 0))]
        scratch += [
            pltpu.VMEM((rows_each // SUB, TU, NV), jnp.float32),
            pltpu.SemaphoreType.DMA((W,)),
            pltpu.VMEM(values_block, values.dtype),
            pltpu.VMEM(places_block, places.dtype),
            pltpu.SemaphoreType.DMA((2,)),
            pltpu.VMEM((len(numbers), 1, all_subs), jnp.int32),
            pltpu.SemaphoreType.DMA((len(numbers),)),
        ]
        more = [pltpu.with_memory_space_constraint(array, pltpu.HBM) for array in numbers]
    else:
        in_specs = [pl.BlockSpec(block, lambda i: (0, chunk, 0)) for block in (values_block, places_block)]
        in_specs.append(ANY)
        in_specs += [pl.BlockSpec(array.shape, lambda i: (0, 0, 0, 0)) for array in earlier]
        more = [order, *earlier]
    return pl.pallas_call(
        functools.partial(grid_kernel, peers=peers, first=first, turns=turns, earlier=bool(earlier)),
        grid=(1,),
        out_shape=out_shape,
        in_specs=[SMEM] + in_specs,
        out_specs=out_specs,
        scratch_shapes=scratch,
        compiler_params=pltpu.CompilerParams(vmem_limit_bytes=48 << 20),
        cost_estimate=pl.CostEstimate(
            flops=8 * (turns[1] - turns[0]) * STEP * row_count * SUB * SUB * comp_count,
            bytes_accessed=2 << 20,
            transcendentals=0,
        ),
    )(me, values, places, *more)


def halve_kernel(kept_ref, arrived_ref, *rest):
    next_kept_ref, next_sent_ref = rest[-2:]
    for at in range(kept_ref.shape[0]):
        total = kept_ref[at].astype(jnp.float32) + arrived_ref[at].astype(jnp.float32)
        if at % 2:
            next_sent_ref[at // 2] = total.astype(jnp.bfloat16)
        else:
            next_kept_ref[at // 2] = total


def halve(kept, arrived, order):
    shape = (kept.shape[0] // 2,) + kept.shape[1:]
    return pl.pallas_call(
        halve_kernel,
        out_shape=[jax.ShapeDtypeStruct(shape, jnp.float32), jax.ShapeDtypeStruct(shape, jnp.bfloat16)],
        in_specs=[VMEM] * 2 + [ANY] * len(order),
        out_specs=[VMEM] * 2,
        compiler_params=pltpu.CompilerParams(vmem_limit_bytes=8 << 20),
        cost_estimate=pl.CostEstimate(flops=1 << 18, bytes_accessed=1 << 20, transcendentals=0),
    )(kept, arrived, *order)


def paired(array, axis, mask):
    return lax.ppermute(array, axis, [(i, i ^ mask) for i in range(lax.axis_size(axis))])


def halve_all(kept, sent, axis, order):
    mask = 1
    while kept.shape[0] > 1:
        kept, sent = halve(kept, paired(sent, axis, mask), order)
        mask *= 2
    return kept, sent


def turning(chunk_numbers, sub, lanes):
    row_offsets = chunk_numbers[1:2, sub : sub + 2]
    col_shifts = chunk_numbers[4:5, sub : sub + 2]
    to = lax.broadcasted_iota(jnp.int32, (2 * SUB, 2 * SUB), 0)
    of = lax.broadcasted_iota(jnp.int32, (2 * SUB, 2 * SUB), 1)
    turned = jnp.where(of < SUB, row_offsets[:, 0:1], row_offsets[:, 1:2]) & (SUBLANES - 1)
    rows = (to == (of & SUB) + ((of + turned) & (SUB - 1))).astype(jnp.bfloat16)
    to = lax.broadcasted_iota(jnp.int32, (lanes, LANES), 1)
    of = lax.broadcasted_iota(jnp.int32, (lanes, LANES), 0)
    cols = [
        (to == ((of + col_shifts[:, which : which + 1]) & (LANES - 1))).astype(jnp.bfloat16) for which in range(2)
    ]
    return rows, cols


def sum_kernel(kept_ref, arrived_ref, numbers_ref, *rest, hops, first_sub):
    pairs, lanes = kept_ref.shape[1:3]
    group = min(lanes, LANES)
    out_ref = rest[hops or 1]
    numbers = numbers_ref[...].astype(jnp.float32).astype(jnp.int32)
    for pair in range(pairs):
        total = kept_ref[0, pair].astype(jnp.float32) + arrived_ref[0, pair].astype(jnp.float32)
        rows, cols = turning(numbers, first_sub + 2 * pair, group)
        total = lax.dot_general(
            rows, total.astype(jnp.bfloat16), (((1,), (1,)), ((), ())), preferred_element_type=jnp.float32
        ).astype(jnp.bfloat16)
        for which in range(2):
            at = (pair * 2 + which) * SUB
            for left in range(0, lanes, group):
                out_ref[at : at + SUB, left : left + LANES] = jnp.dot(
                    total[which * SUB : (which + 1) * SUB, left : left + group],
                    cols[which],
                    preferred_element_type=jnp.float32,
                ).astype(jnp.bfloat16)
    if hops:
        near_ref, go_ref = rest[hops + 1 :]
        go_ref[...] = jnp.zeros(go_ref.shape, jnp.int32)
        for at in range(hops):
            near_ref[at] = rest[at][: near_ref.shape[1], :]
    else:
        both = [ref[...].astype(jnp.float32) for ref in (numbers_ref, rest[0])]
        blank = jnp.zeros((META, out_ref.shape[1] - 2 * both[0].shape[1]), jnp.float32)
        out_ref[pairs * 2 * SUB :, :] = jnp.concatenate(both + [blank], axis=1).astype(jnp.bfloat16)


def sum_parts(kept, arrived, first_sub, own_numbers, hops, other_numbers):
    _, pairs, lanes, _ = kept.shape
    rows = pairs * 2 * SUB
    lanes = max(lanes, LANES)
    out_shape = [jax.ShapeDtypeStruct((rows if hops else rows + META, lanes), jnp.bfloat16)]
    if hops:
        out_shape.append(jax.ShapeDtypeStruct((len(hops), rows, lanes), jnp.bfloat16))
        out_shape.append(jax.ShapeDtypeStruct((SUBLANES, LANES), jnp.int32))
    return pl.pallas_call(
        functools.partial(sum_kernel, hops=len(hops), first_sub=first_sub),
        out_shape=out_shape,
        in_specs=[VMEM] * (3 + len(hops) + len(other_numbers)),
        out_specs=[VMEM] * len(out_shape),
        compiler_params=pltpu.CompilerParams(vmem_limit_bytes=8 << 20),
        cost_estimate=pl.CostEstimate(flops=1 << 20, bytes_accessed=2 << 20, transcendentals=0),
    )(kept, arrived, own_numbers, *hops, *other_numbers)


def across(array, axis):
    return [array] + [paired(array, axis, mask) for mask in range(2, lax.axis_size(axis), 2)]


def touch_plan(starts, planes, cols, spots, others):
    total = starts.shape[0]
    ids = jnp.arange(total, dtype=jnp.int32)
    taken = starts >= 0
    keys = jnp.where(taken, planes, W) * total + ids
    left = jnp.where(taken, planes * BLOCKS + cols // LANES, -1)
    right = jnp.where(taken & (cols % LANES > LANES - SUB), left + 1, -2)
    before = keys[None, :] < keys[:, None]
    after = keys[None, :] > keys[:, None]
    rank = jnp.sum(before.astype(jnp.int32), axis=1)

    def edges(units):
        same = (left[None, :] == units[:, None]) | (right[None, :] == units[:, None])
        first = ~jnp.any(same & before, axis=1)
        last = ~jnp.any(same & after, axis=1)
        return first.astype(jnp.int32) + 2 * last.astype(jnp.int32)

    flags = edges(left) + jnp.where(right >= 0, 4 * edges(right), 0) + 16 * others
    fields = jnp.stack([starts, cols, planes, spots, flags], axis=0)
    moved = jnp.where(rank[None, None, :] == ids[None, :, None], fields[:, None, :], 0)
    table = jnp.sum(moved, axis=2)
    number = jnp.sum(taken.astype(jnp.int32))
    return jnp.concatenate([table, jnp.full((1, total), number, jnp.int32)], axis=0)


def place_kernel(table_ref, near_ref, other_ref, _, out_ref, canvas, sem):
    comp_count = canvas.shape[1]
    number = table_ref[5, 0]
    row = lax.broadcasted_iota(jnp.int32, (1, SUBLANES, LANES), 1)
    lane = lax.broadcasted_iota(jnp.int32, (1, SUBLANES, LANES), 2)

    def lanes_of(block):
        return pl.ds(pl.multiple_of(block * LANES, LANES), LANES)

    def out_copy(plane, block):
        return pltpu.make_async_copy(
            canvas.at[plane, :, pl.ds(SUB, TU), lanes_of(block)],
            out_ref.at[:, plane, :, lanes_of(block)],
            sem.at[plane, block],
        )

    def clear(plane, block):
        canvas[plane, :, pl.ds(SUB, TU), lanes_of(block)] = jnp.zeros((comp_count, TU, LANES), jnp.float32)

    def when_set(flags, bit, act):
        @pl.when((flags & bit) != 0)
        def _():
            act()

    def patch_of(index):
        spot = table_ref[3, index]
        block = spot >> 16
        at = pl.ds(pl.multiple_of(spot & 0xFFFF, SUB), SUB)
        patch = jnp.where((table_ref[4, index] & 16) != 0, other_ref[block, at, :], near_ref[block, at, :])
        patch = patch.astype(jnp.float32)
        patches = []
        skip = table_ref[0, index] & (SUBLANES - 1)
        for comp in range(comp_count):
            values = patch[:, comp // 2 * LANES : (comp // 2 + 1) * LANES]
            if comp % 2:
                values = pltpu.roll(values, SUB, 1)
            values = values.reshape(SUB // SUBLANES, SUBLANES, LANES)
            head = jnp.where(row >= skip, values[:1], 0.0)
            tail = jnp.where(row < skip, values[:1], 0.0)
            patches.append(jnp.concatenate([head, values[1:], tail], axis=0))
        return patches

    def add_patch(index, patches):
        start = table_ref[0, index]
        col = table_ref[1, index]
        plane = table_ref[2, index]
        flags = table_ref[4, index]
        block = col >> 7
        shift = col & (LANES - 1)
        rows = pl.ds(pl.multiple_of(start & ~(SUBLANES - 1), SUBLANES), SUB + SUBLANES)

        def add(at, here):
            for comp in range(comp_count):
                values = jnp.where(here, patches[comp], 0.0).reshape(SUB + SUBLANES, LANES)
                canvas[plane, comp, rows, lanes_of(at)] += values

        when_set(flags, 1, lambda: clear(plane, block))
        add(block, (lane >= shift) & (lane < shift + SUB))
        when_set(flags, 2, lambda: out_copy(plane, block).start())

        @pl.when(shift > LANES - SUB)
        def _():
            when_set(flags, 4, lambda: clear(plane, block + 1))
            add(block + 1, lane < shift + SUB - LANES)
            when_set(flags, 8, lambda: out_copy(plane, block + 1).start())

    def add_two(turn_index, carry):
        index = turn_index * 4
        several = [patch_of(index + more) for more in range(4)]
        add_patch(index, several[0])
        for more in range(1, 4):

            @pl.when(index + more < number)
            def _(more=more):
                add_patch(index + more, several[more])

        return carry

    def finish(index, carry):
        block = table_ref[1, index] >> 7
        plane = table_ref[2, index]
        flags = table_ref[4, index]
        when_set(flags, 2, lambda: out_copy(plane, block).wait())
        when_set(flags, 8, lambda: out_copy(plane, block + 1).wait())
        return carry

    lax.fori_loop(0, (number + 3) // 4, add_two, 0)
    lax.fori_loop(0, number, finish, 0)


def place_all(near, other, table, tile_grid):
    comp_count = tile_grid.shape[0]
    return pl.pallas_call(
        place_kernel,
        out_shape=jax.ShapeDtypeStruct(tile_grid.shape, jnp.float32),
        in_specs=[SMEM, VMEM, VMEM, ANY],
        out_specs=ANY,
        scratch_shapes=[
            pltpu.VMEM((W, comp_count, TU + 2 * SUB, NV), jnp.float32),
            pltpu.SemaphoreType.DMA((W, BLOCKS)),
        ],
        input_output_aliases={3: 0},
        compiler_params=pltpu.CompilerParams(vmem_limit_bytes=44 << 20),
        cost_estimate=pl.CostEstimate(flops=0, bytes_accessed=16 << 20, transcendentals=0),
    )(table, near, other, tile_grid)


def body(visibilities, positions, owner, w_plane, row_offset, col_offset):
    peers = lax.axis_size("tm")
    tiles = lax.axis_size("uv")
    sub_count = visibilities.shape[1]
    comp_count = visibilities.shape[0] // peers
    tile = lax.axis_index("uv")
    half = sub_count // 2

    split = half // STEP // 2
    *parts_a, tile_grid, own_numbers = grid_parts(
        visibilities,
        positions,
        peers,
        0,
        (0, half // STEP),
        numbers=(owner.T, row_offset[None], w_plane[None], col_offset[None]),
    )
    other_numbers = paired(own_numbers, "uv", 1)
    parts_b = grid_parts(visibilities, positions, peers, 1, (0, split), order=tile_grid)
    kept_a, sent_a = halve_all(*parts_a, "tm", [parts_b[0], other_numbers])
    parts_b = grid_parts(visibilities, positions, peers, 1, (split, half // STEP), order=sent_a, earlier=parts_b)
    kept_b, sent_b = halve_all(*parts_b, "tm", [])
    arrived_a, arrived_b = (paired(sent, "tm", peers // 2) for sent in (sent_a, sent_b))
    (sum_a,) = sum_parts(kept_a, arrived_a, 0, own_numbers, [], [other_numbers])
    hops_a = across(sum_a, "uv")
    sum_b, near_a, go = sum_parts(kept_b, arrived_b, half, own_numbers, hops_a, [])
    near = jnp.concatenate([near_a, jnp.stack(across(sum_b, "uv"), axis=0)], axis=0)
    other = paired(near, "uv", 1)

    told = jnp.stack([hop[half * SUB :, : 2 * sub_count] for hop in hops_a], axis=1).astype(jnp.float32).astype(jnp.int32)
    chips = told.shape[1]
    told = told.reshape(META, -1) + go[0, 0]
    entry = jnp.arange(told.shape[1], dtype=jnp.int32)
    chip, sub = entry // (2 * sub_count), entry % sub_count
    others = entry // sub_count % 2
    spots = ((sub // half * chips + chip) << 16) + sub % half * SUB
    ahead = (told[0] - tile) % tiles
    starts = jnp.where(ahead == 0, told[1] + SUB, jnp.where(ahead == tiles - 1, told[1] + SUB - TU, -1))
    table = touch_plan(starts, told[2], told[3] * LANES + told[4], spots, others)
    return place_all(near, other, table, tile_grid)


def solution(mesh):
    placed = (P(None, "uv", "tm"), P(None, "uv", "tm"), P("uv", None), P("uv"), P("uv"), P("uv"))
    return jax.shard_map(
        body, mesh=mesh, in_specs=placed, out_specs=P("tm", None, "uv", None), check_vma=False
    )
```

```python
import functools
import math

import jax
import jax.numpy as jnp
from jax import lax
from jax.experimental import pallas as pl
from jax.experimental.pallas import tpu as pltpu
from jax.sharding import PartitionSpec as P

W = 8
SUB = 64
TAPS = 8
TU = 128
NV = 2048
LANES = 128
SUBLANES = 8
BLOCKS = NV // LANES
META = 16
MIXED = 256

VMEM = pl.BlockSpec(memory_space=pltpu.VMEM)
SMEM = pl.BlockSpec(memory_space=pltpu.SMEM)
ANY = pl.BlockSpec(memory_space=pl.ANY)


def taper(scaled):
    inner = jnp.maximum(0.0, 1.0 - scaled * scaled)
    return inner * inner


def number_rows(owner, row_offset, w_plane, col_offset):
    rows = [owner, row_offset, w_plane, col_offset // LANES, col_offset % LANES]
    blank = jnp.zeros((META - len(rows), owner.shape[1]), jnp.int32)
    return jnp.concatenate(rows + [blank], axis=0).astype(jnp.float32).astype(jnp.bfloat16)


def grid_kernel(me_ref, values_ref, places_ref, *rest, peers, first, subs, step, earlier):
    if first:
        places_from, (kept_ref, sent_ref, out_ref, numbers_ref), rest = rest[:4], rest[4:8], rest[8:]
        values_wide, sums, blank, sem, values, places, in_sem, numbers, numbers_sem = rest
        number_copies = [
            pltpu.make_async_copy(source, numbers.at[at], numbers_sem.at[at]) for at, source in enumerate(places_from)
        ]
        for copy in number_copies:
            copy.start()
        _, sub_count, row_count = values.shape
        in_copies = [
            pltpu.make_async_copy(values_ref.at[:, pl.ds(0, sub_count), :], values, in_sem.at[0]),
            pltpu.make_async_copy(places_ref.at[:, pl.ds(0, sub_count), :], places, in_sem.at[1]),
        ]
        for copy in in_copies:
            copy.start()
        blank[...] = jnp.zeros(blank.shape, jnp.float32)
        zero_copies = [pltpu.make_async_copy(blank, out_ref.at[:, plane], sem.at[plane]) for plane in range(W)]
        for copy in in_copies + number_copies:
            copy.wait()
        for copy in zero_copies:
            copy.start()
        numbers_ref[...] = number_rows(*(numbers[at] for at in range(4)))
        values_ref, places_ref = values, places
    else:
        rest = rest[1:]
        if earlier:
            earlier_kept, earlier_sent, kept_ref, sent_ref, values_wide, sums = rest
            done = earlier_kept.shape[1]
            kept_ref[:, :done] = earlier_kept[...]
            sent_ref[:, :done] = earlier_sent[...]
        else:
            kept_ref, sent_ref, values_wide, sums = rest
    comp_count, sub_count, row_count = values_ref.shape
    rows_each = comp_count // peers * SUB
    for comp in range(comp_count):
        values_wide[comp * sub_count : (comp + 1) * sub_count, :] = values_ref[comp].astype(jnp.float32)
    span = math.gcd(row_count, MIXED)
    cells = lax.broadcasted_iota(jnp.int32, (SUB, span), 0).astype(jnp.float32) * (2.0 / TAPS)

    def one_sub(sub):
        straight = jnp.zeros((comp_count * SUB, SUB), jnp.float32)
        crossed = jnp.zeros((SUB, comp_count * SUB), jnp.float32)
        for at in range(0, row_count, span):
            some = slice(at, at + span)
            row_taps = taper(cells - places_ref[0, pl.ds(sub, 1), some] * (2.0 / TAPS)).astype(jnp.bfloat16)
            col_taps = taper(cells - places_ref[1, pl.ds(sub, 1), some] * (2.0 / TAPS))
            weighted = jnp.concatenate(
                [
                    (values_wide[pl.ds(comp * sub_count + sub, 1), some] * col_taps).astype(jnp.bfloat16)
                    for comp in range(comp_count)
                ],
                axis=0,
            )
            last = (((1,), (1,)), ((), ()))
            if at // span % 2:
                crossed += lax.dot_general(row_taps, weighted, last, preferred_element_type=jnp.float32)
            else:
                straight += lax.dot_general(weighted, row_taps, last, preferred_element_type=jnp.float32)
        return straight + jnp.transpose(crossed)

    def some_subs(turn, carry):
        for pair in range(step // 2):
            sub = turn * step + pair * 2
            sums[pair] = jnp.concatenate([one_sub(sub), one_sub(sub + 1)], axis=1).astype(jnp.bfloat16)
        for pair in range(step // 2):
            for mask in range(peers):
                rows = pl.ds(pl.multiple_of((me_ref[0] ^ mask) * rows_each, rows_each), rows_each)
                target = sent_ref if mask % 2 else kept_ref
                target[mask // 2, turn * (step // 2) + pair] = sums[pair, rows, :]
        return carry

    lax.fori_loop(subs[0] // step, subs[1] // step, some_subs, 0)
    if first:
        for copy in zero_copies:
            copy.wait()


def grid_parts(values, places, peers, chunk, subs, step, order=None, numbers=(), earlier=()):
    comp_count, all_subs, row_count = values.shape
    sub_count = all_subs // 2
    rows_each = comp_count // peers * SUB
    first = order is None
    me = lax.axis_index("tm").astype(jnp.int32).reshape(1)
    parts_shape = (peers // 2, subs[1] // 2, rows_each, LANES)
    values_block, places_block = (comp_count, sub_count, row_count), (2, sub_count, row_count)
    out_shape = [jax.ShapeDtypeStruct(parts_shape, jnp.bfloat16)] * 2
    out_specs = [pl.BlockSpec(parts_shape, lambda i: (0, 0, 0, 0))] * 2
    scratch = [
        pltpu.VMEM((comp_count * sub_count, row_count), jnp.float32),
        pltpu.VMEM((step // 2, comp_count * SUB, LANES), jnp.bfloat16),
    ]
    if first:
        values, places = (pltpu.with_memory_space_constraint(array, pltpu.HBM) for array in (values, places))
        in_specs = [pl.BlockSpec(memory_space=pltpu.HBM)] * 2
        in_specs += [pl.BlockSpec(memory_space=pltpu.HBM)] * len(numbers)
        out_shape.append(jax.ShapeDtypeStruct((rows_each // SUB, W, TU, NV), jnp.float32))
        out_shape.append(jax.ShapeDtypeStruct((META, all_subs), jnp.bfloat16))
        out_specs += [ANY, pl.BlockSpec((META, all_subs), lambda i: (0, 0))]
        scratch += [
            pltpu.VMEM((rows_each // SUB, TU, NV), jnp.float32),
            pltpu.SemaphoreType.DMA((W,)),
            pltpu.VMEM(values_block, values.dtype),
            pltpu.VMEM(places_block, places.dtype),
            pltpu.SemaphoreType.DMA((2,)),
            pltpu.VMEM((len(numbers), 1, all_subs), jnp.int32),
            pltpu.SemaphoreType.DMA((len(numbers),)),
        ]
        more = [pltpu.with_memory_space_constraint(array, pltpu.HBM) for array in numbers]
    else:
        in_specs = [pl.BlockSpec(block, lambda i: (0, chunk, 0)) for block in (values_block, places_block)]
        in_specs.append(ANY)
        in_specs += [pl.BlockSpec(array.shape, lambda i: (0, 0, 0, 0)) for array in earlier]
        more = [order, *earlier]
    return pl.pallas_call(
        functools.partial(grid_kernel, peers=peers, first=first, subs=subs, step=step, earlier=bool(earlier)),
        grid=(1,),
        out_shape=out_shape,
        in_specs=[SMEM] + in_specs,
        out_specs=out_specs,
        scratch_shapes=scratch,
        compiler_params=pltpu.CompilerParams(vmem_limit_bytes=48 << 20),
        cost_estimate=pl.CostEstimate(
            flops=8 * (subs[1] - subs[0]) * row_count * SUB * SUB * comp_count,
            bytes_accessed=2 << 20,
            transcendentals=0,
        ),
    )(me, values, places, *more)


def halve_kernel(kept_ref, arrived_ref, *rest):
    next_kept_ref, next_sent_ref = rest[-2:]
    for at in range(kept_ref.shape[0]):
        total = kept_ref[at].astype(jnp.float32) + arrived_ref[at].astype(jnp.float32)
        if at % 2:
            next_sent_ref[at // 2] = total.astype(jnp.bfloat16)
        else:
            next_kept_ref[at // 2] = total


def halve(kept, arrived, order):
    shape = (kept.shape[0] // 2,) + kept.shape[1:]
    return pl.pallas_call(
        halve_kernel,
        out_shape=[jax.ShapeDtypeStruct(shape, jnp.float32), jax.ShapeDtypeStruct(shape, jnp.bfloat16)],
        in_specs=[VMEM] * 2 + [ANY] * len(order),
        out_specs=[VMEM] * 2,
        compiler_params=pltpu.CompilerParams(vmem_limit_bytes=8 << 20),
        cost_estimate=pl.CostEstimate(flops=1 << 18, bytes_accessed=1 << 20, transcendentals=0),
    )(kept, arrived, *order)


def paired(array, axis, mask):
    return lax.ppermute(array, axis, [(i, i ^ mask) for i in range(lax.axis_size(axis))])


def halve_all(kept, sent, axis, order):
    mask = 1
    while kept.shape[0] > 1:
        kept, sent = halve(kept, paired(sent, axis, mask), order)
        mask *= 2
    return kept, sent


def turning(chunk_numbers, sub, lanes):
    row_offsets = chunk_numbers[1:2, sub : sub + 2]
    col_shifts = chunk_numbers[4:5, sub : sub + 2]
    to = lax.broadcasted_iota(jnp.int32, (2 * SUB, 2 * SUB), 0)
    of = lax.broadcasted_iota(jnp.int32, (2 * SUB, 2 * SUB), 1)
    turned = jnp.where(of < SUB, row_offsets[:, 0:1], row_offsets[:, 1:2]) & (SUBLANES - 1)
    rows = (to == (of & SUB) + ((of + turned) & (SUB - 1))).astype(jnp.bfloat16)
    to = lax.broadcasted_iota(jnp.int32, (lanes, LANES), 1)
    of = lax.broadcasted_iota(jnp.int32, (lanes, LANES), 0)
    cols = [
        (to == ((of + col_shifts[:, which : which + 1]) & (LANES - 1))).astype(jnp.bfloat16) for which in range(2)
    ]
    return rows, cols


def sum_kernel(kept_ref, arrived_ref, numbers_ref, *rest, hops, first_sub):
    pairs, lanes = kept_ref.shape[1:3]
    group = min(lanes, LANES)
    out_ref = rest[hops or 1]
    numbers = numbers_ref[...].astype(jnp.float32).astype(jnp.int32)
    for pair in range(pairs):
        total = kept_ref[0, pair].astype(jnp.float32) + arrived_ref[0, pair].astype(jnp.float32)
        rows, cols = turning(numbers, first_sub + 2 * pair, group)
        total = lax.dot_general(
            rows, total.astype(jnp.bfloat16), (((1,), (1,)), ((), ())), preferred_element_type=jnp.float32
        ).astype(jnp.bfloat16)
        for which in range(2):
            at = (pair * 2 + which) * SUB
            for left in range(0, lanes, group):
                out_ref[at : at + SUB, left : left + LANES] = jnp.dot(
                    total[which * SUB : (which + 1) * SUB, left : left + group],
                    cols[which],
                    preferred_element_type=jnp.float32,
                ).astype(jnp.bfloat16)
    if hops:
        near_ref, go_ref = rest[hops + 1 :]
        go_ref[...] = jnp.zeros(go_ref.shape, jnp.int32)
        for at in range(hops):
            near_ref[at] = rest[at][: near_ref.shape[1], :]
    else:
        both = [ref[...].astype(jnp.float32) for ref in (numbers_ref, rest[0])]
        blank = jnp.zeros((META, out_ref.shape[1] - 2 * both[0].shape[1]), jnp.float32)
        out_ref[pairs * 2 * SUB :, :] = jnp.concatenate(both + [blank], axis=1).astype(jnp.bfloat16)


def sum_parts(kept, arrived, first_sub, own_numbers, hops, other_numbers):
    _, pairs, lanes, _ = kept.shape
    rows = pairs * 2 * SUB
    lanes = max(lanes, LANES)
    out_shape = [jax.ShapeDtypeStruct((rows if hops else rows + META, lanes), jnp.bfloat16)]
    if hops:
        out_shape.append(jax.ShapeDtypeStruct((len(hops), rows, lanes), jnp.bfloat16))
        out_shape.append(jax.ShapeDtypeStruct((SUBLANES, LANES), jnp.int32))
    return pl.pallas_call(
        functools.partial(sum_kernel, hops=len(hops), first_sub=first_sub),
        out_shape=out_shape,
        in_specs=[VMEM] * (3 + len(hops) + len(other_numbers)),
        out_specs=[VMEM] * len(out_shape),
        compiler_params=pltpu.CompilerParams(vmem_limit_bytes=8 << 20),
        cost_estimate=pl.CostEstimate(flops=1 << 20, bytes_accessed=2 << 20, transcendentals=0),
    )(kept, arrived, own_numbers, *hops, *other_numbers)


def across(array, axis):
    return [array] + [paired(array, axis, mask) for mask in range(2, lax.axis_size(axis), 2)]


def touch_plan(starts, planes, cols, spots, others):
    total = starts.shape[0]
    ids = jnp.arange(total, dtype=jnp.int32)
    taken = starts >= 0
    keys = jnp.where(taken, planes, W) * total + ids
    left = jnp.where(taken, planes * BLOCKS + cols // LANES, -1)
    right = jnp.where(taken & (cols % LANES > LANES - SUB), left + 1, -2)
    before = keys[None, :] < keys[:, None]
    after = keys[None, :] > keys[:, None]
    rank = jnp.sum(before.astype(jnp.int32), axis=1)

    def edges(units):
        same = (left[None, :] == units[:, None]) | (right[None, :] == units[:, None])
        first = ~jnp.any(same & before, axis=1)
        last = ~jnp.any(same & after, axis=1)
        return first.astype(jnp.int32) + 2 * last.astype(jnp.int32)

    flags = edges(left) + jnp.where(right >= 0, 4 * edges(right), 0) + 16 * others
    fields = jnp.stack([starts, cols, planes, spots, flags], axis=0)
    moved = jnp.where(rank[None, None, :] == ids[None, :, None], fields[:, None, :], 0)
    table = jnp.sum(moved, axis=2)
    number = jnp.sum(taken.astype(jnp.int32))
    return jnp.concatenate([table, jnp.full((1, total), number, jnp.int32)], axis=0)


def place_kernel(table_ref, near_ref, other_ref, _, out_ref, canvas, sem):
    comp_count = canvas.shape[1]
    number = table_ref[5, 0]
    row = lax.broadcasted_iota(jnp.int32, (1, SUBLANES, LANES), 1)
    lane = lax.broadcasted_iota(jnp.int32, (1, SUBLANES, LANES), 2)

    def lanes_of(block):
        return pl.ds(pl.multiple_of(block * LANES, LANES), LANES)

    def out_copy(plane, block):
        return pltpu.make_async_copy(
            canvas.at[plane, :, pl.ds(SUB, TU), lanes_of(block)],
            out_ref.at[:, plane, :, lanes_of(block)],
            sem.at[plane, block],
        )

    def clear(plane, block):
        canvas[plane, :, pl.ds(SUB, TU), lanes_of(block)] = jnp.zeros((comp_count, TU, LANES), jnp.float32)

    def when_set(flags, bit, act):
        @pl.when((flags & bit) != 0)
        def _():
            act()

    def patch_of(index):
        spot = table_ref[3, index]
        block = spot >> 16
        at = pl.ds(pl.multiple_of(spot & 0xFFFF, SUB), SUB)
        patch = jnp.where((table_ref[4, index] & 16) != 0, other_ref[block, at, :], near_ref[block, at, :])
        patch = patch.astype(jnp.float32)
        patches = []
        skip = table_ref[0, index] & (SUBLANES - 1)
        for comp in range(comp_count):
            values = patch[:, comp // 2 * LANES : (comp // 2 + 1) * LANES]
            if comp % 2:
                values = pltpu.roll(values, SUB, 1)
            values = values.reshape(SUB // SUBLANES, SUBLANES, LANES)
            head = jnp.where(row >= skip, values[:1], 0.0)
            tail = jnp.where(row < skip, values[:1], 0.0)
            patches.append(jnp.concatenate([head, values[1:], tail], axis=0))
        return patches

    def add_patch(index, patches):
        start = table_ref[0, index]
        col = table_ref[1, index]
        plane = table_ref[2, index]
        flags = table_ref[4, index]
        block = col >> 7
        shift = col & (LANES - 1)
        rows = pl.ds(pl.multiple_of(start & ~(SUBLANES - 1), SUBLANES), SUB + SUBLANES)

        def add(at, here):
            for comp in range(comp_count):
                values = jnp.where(here, patches[comp], 0.0).reshape(SUB + SUBLANES, LANES)
                canvas[plane, comp, rows, lanes_of(at)] += values

        when_set(flags, 1, lambda: clear(plane, block))
        add(block, (lane >= shift) & (lane < shift + SUB))
        when_set(flags, 2, lambda: out_copy(plane, block).start())

        @pl.when(shift > LANES - SUB)
        def _():
            when_set(flags, 4, lambda: clear(plane, block + 1))
            add(block + 1, lane < shift + SUB - LANES)
            when_set(flags, 8, lambda: out_copy(plane, block + 1).start())

    def add_two(turn_index, carry):
        index = turn_index * 4
        several = [patch_of(index + more) for more in range(4)]
        add_patch(index, several[0])
        for more in range(1, 4):

            @pl.when(index + more < number)
            def _(more=more):
                add_patch(index + more, several[more])

        return carry

    def finish(index, carry):
        block = table_ref[1, index] >> 7
        plane = table_ref[2, index]
        flags = table_ref[4, index]
        when_set(flags, 2, lambda: out_copy(plane, block).wait())
        when_set(flags, 8, lambda: out_copy(plane, block + 1).wait())
        return carry

    lax.fori_loop(0, (number + 3) // 4, add_two, 0)
    lax.fori_loop(0, number, finish, 0)


def place_all(near, other, table, tile_grid):
    comp_count = tile_grid.shape[0]
    return pl.pallas_call(
        place_kernel,
        out_shape=jax.ShapeDtypeStruct(tile_grid.shape, jnp.float32),
        in_specs=[SMEM, VMEM, VMEM, ANY],
        out_specs=ANY,
        scratch_shapes=[
            pltpu.VMEM((W, comp_count, TU + 2 * SUB, NV), jnp.float32),
            pltpu.SemaphoreType.DMA((W, BLOCKS)),
        ],
        input_output_aliases={3: 0},
        compiler_params=pltpu.CompilerParams(vmem_limit_bytes=44 << 20),
        cost_estimate=pl.CostEstimate(flops=0, bytes_accessed=16 << 20, transcendentals=0),
    )(table, near, other, tile_grid)


def body(visibilities, positions, owner, w_plane, row_offset, col_offset):
    peers = lax.axis_size("tm")
    tiles = lax.axis_size("uv")
    sub_count = visibilities.shape[1]
    comp_count = visibilities.shape[0] // peers
    tile = lax.axis_index("uv")
    half = sub_count // 2

    split = half * 3 // 4
    *parts_a, tile_grid, own_numbers = grid_parts(
        visibilities,
        positions,
        peers,
        0,
        (0, half),
        half // 2,
        numbers=(owner.T, row_offset[None], w_plane[None], col_offset[None]),
    )
    other_numbers = paired(own_numbers, "uv", 1)
    parts_b = grid_parts(visibilities, positions, peers, 1, (0, split), split, order=tile_grid)
    kept_a, sent_a = halve_all(*parts_a, "tm", [parts_b[0], other_numbers])
    parts_b = grid_parts(
        visibilities, positions, peers, 1, (split, half), half - split, order=sent_a, earlier=parts_b
    )
    kept_b, sent_b = halve_all(*parts_b, "tm", [])
    arrived_a, arrived_b = (paired(sent, "tm", peers // 2) for sent in (sent_a, sent_b))
    (sum_a,) = sum_parts(kept_a, arrived_a, 0, own_numbers, [], [other_numbers])
    hops_a = across(sum_a, "uv")
    sum_b, near_a, go = sum_parts(kept_b, arrived_b, half, own_numbers, hops_a, [])
    near = jnp.concatenate([near_a, jnp.stack(across(sum_b, "uv"), axis=0)], axis=0)
    other = paired(near, "uv", 1)

    told = jnp.stack([hop[half * SUB :, : 2 * sub_count] for hop in hops_a], axis=1).astype(jnp.float32).astype(jnp.int32)
    chips = told.shape[1]
    told = told.reshape(META, -1) + go[0, 0]
    entry = jnp.arange(told.shape[1], dtype=jnp.int32)
    chip, sub = entry // (2 * sub_count), entry % sub_count
    others = entry // sub_count % 2
    spots = ((sub // half * chips + chip) << 16) + sub % half * SUB
    ahead = (told[0] - tile) % tiles
    starts = jnp.where(ahead == 0, told[1] + SUB, jnp.where(ahead == tiles - 1, told[1] + SUB - TU, -1))
    table = touch_plan(starts, told[2], told[3] * LANES + told[4], spots, others)
    return place_all(near, other, table, tile_grid)


def solution(mesh):
    placed = (P(None, "uv", "tm"), P(None, "uv", "tm"), P("uv", None), P("uv"), P("uv"), P("uv"))
    return jax.shard_map(
        body, mesh=mesh, in_specs=placed, out_specs=P("tm", None, "uv", None), check_vma=False
    )
```

```python
import functools
import math

import jax
import jax.numpy as jnp
from jax import lax
from jax.experimental import pallas as pl
from jax.experimental.pallas import tpu as pltpu
from jax.sharding import PartitionSpec as P

W = 8
SUB = 64
TAPS = 8
TU = 128
NV = 2048
LANES = 128
SUBLANES = 8
BLOCKS = NV // LANES
META = 16
MIXED = 256
STEP = 4

VMEM = pl.BlockSpec(memory_space=pltpu.VMEM)
SMEM = pl.BlockSpec(memory_space=pltpu.SMEM)
ANY = pl.BlockSpec(memory_space=pl.ANY)


def taper(scaled):
    inner = jnp.maximum(0.0, 1.0 - scaled * scaled)
    return inner * inner


def number_rows(owner, row_offset, w_plane, col_offset):
    rows = [owner, row_offset, w_plane, col_offset // LANES, col_offset % LANES]
    blank = jnp.zeros((META - len(rows), owner.shape[1]), jnp.int32)
    return jnp.concatenate(rows + [blank], axis=0).astype(jnp.float32).astype(jnp.bfloat16)


def grid_kernel(me_ref, values_ref, places_ref, *rest, peers, first, turns, earlier):
    if first:
        kept_ref, sent_ref, out_ref, values_wide, sums, blank, sem, values, places, in_sem = rest
        _, sub_count, row_count = values.shape
        in_copies = [
            pltpu.make_async_copy(values_ref.at[:, pl.ds(0, sub_count), :], values, in_sem.at[0]),
            pltpu.make_async_copy(places_ref.at[:, pl.ds(0, sub_count), :], places, in_sem.at[1]),
        ]
        for copy in in_copies:
            copy.start()
        blank[...] = jnp.zeros(blank.shape, jnp.float32)
        zero_copies = [pltpu.make_async_copy(blank, out_ref.at[:, plane], sem.at[plane]) for plane in range(W)]
        for copy in in_copies:
            copy.wait()
        for copy in zero_copies:
            copy.start()
        values_ref, places_ref = values, places
    else:
        rest = rest[1:]
        if earlier:
            earlier_kept, earlier_sent, kept_ref, sent_ref, values_wide, sums = rest
            done = earlier_kept.shape[1]
            kept_ref[:, :done] = earlier_kept[...]
            sent_ref[:, :done] = earlier_sent[...]
        else:
            owner_ref, row_ref, plane_ref, col_ref, kept_ref, sent_ref, numbers_ref, values_wide, sums = rest
            numbers_ref[...] = number_rows(owner_ref[...], row_ref[...], plane_ref[...], col_ref[...])
    comp_count, sub_count, row_count = values_ref.shape
    rows_each = comp_count // peers * SUB
    for comp in range(comp_count):
        values_wide[comp * sub_count : (comp + 1) * sub_count, :] = values_ref[comp].astype(jnp.float32)
    span = math.gcd(row_count, MIXED)
    cells = lax.broadcasted_iota(jnp.int32, (SUB, span), 0).astype(jnp.float32) * (2.0 / TAPS)

    def one_sub(sub):
        straight = jnp.zeros((comp_count * SUB, SUB), jnp.float32)
        crossed = jnp.zeros((SUB, comp_count * SUB), jnp.float32)
        for at in range(0, row_count, span):
            some = slice(at, at + span)
            row_taps = taper(cells - places_ref[0, pl.ds(sub, 1), some] * (2.0 / TAPS)).astype(jnp.bfloat16)
            col_taps = taper(cells - places_ref[1, pl.ds(sub, 1), some] * (2.0 / TAPS))
            weighted = jnp.concatenate(
                [
                    (values_wide[pl.ds(comp * sub_count + sub, 1), some] * col_taps).astype(jnp.bfloat16)
                    for comp in range(comp_count)
                ],
                axis=0,
            )
            last = (((1,), (1,)), ((), ()))
            if at // span % 2:
                crossed += lax.dot_general(row_taps, weighted, last, preferred_element_type=jnp.float32)
            else:
                straight += lax.dot_general(weighted, row_taps, last, preferred_element_type=jnp.float32)
        return straight + jnp.transpose(crossed)

    def some_subs(turn, carry):
        for pair in range(STEP // 2):
            sub = turn * STEP + pair * 2
            sums[pair] = jnp.concatenate([one_sub(sub), one_sub(sub + 1)], axis=1).astype(jnp.bfloat16)
        for pair in range(STEP // 2):
            for mask in range(peers):
                rows = pl.ds(pl.multiple_of((me_ref[0] ^ mask) * rows_each, rows_each), rows_each)
                target = sent_ref if mask % 2 else kept_ref
                target[mask // 2, turn * (STEP // 2) + pair] = sums[pair, rows, :]
        return carry

    lax.fori_loop(*turns, some_subs, 0)
    if first:
        for copy in zero_copies:
            copy.wait()


def grid_parts(values, places, peers, chunk, turns, order=None, numbers=(), earlier=()):
    comp_count, all_subs, row_count = values.shape
    sub_count = all_subs // 2
    rows_each = comp_count // peers * SUB
    first = order is None
    me = lax.axis_index("tm").astype(jnp.int32).reshape(1)
    parts_shape = (peers // 2, turns[1] * STEP // 2, rows_each, LANES)
    values_block, places_block = (comp_count, sub_count, row_count), (2, sub_count, row_count)
    out_shape = [jax.ShapeDtypeStruct(parts_shape, jnp.bfloat16)] * 2
    out_specs = [pl.BlockSpec(parts_shape, lambda i: (0, 0, 0, 0))] * 2
    scratch = [
        pltpu.VMEM((comp_count * sub_count, row_count), jnp.float32),
        pltpu.VMEM((STEP // 2, comp_count * SUB, LANES), jnp.bfloat16),
    ]
    if first:
        values, places = (pltpu.with_memory_space_constraint(array, pltpu.HBM) for array in (values, places))
        in_specs = [pl.BlockSpec(memory_space=pltpu.HBM)] * 2
        out_shape.append(jax.ShapeDtypeStruct((rows_each // SUB, W, TU, NV), jnp.float32))
        out_specs.append(ANY)
        scratch += [
            pltpu.VMEM((rows_each // SUB, TU, NV), jnp.float32),
            pltpu.SemaphoreType.DMA((W,)),
            pltpu.VMEM(values_block, values.dtype),
            pltpu.VMEM(places_block, places.dtype),
            pltpu.SemaphoreType.DMA((2,)),
        ]
        more = []
    else:
        in_specs = [pl.BlockSpec(block, lambda i: (0, chunk, 0)) for block in (values_block, places_block)]
        in_specs += [ANY] + [pl.BlockSpec((1, all_subs), lambda i: (0, 0))] * len(numbers)
        in_specs += [pl.BlockSpec(array.shape, lambda i: (0, 0, 0, 0)) for array in earlier]
        more = [order, *numbers, *earlier]
        if numbers:
            out_shape.append(jax.ShapeDtypeStruct((META, all_subs), jnp.bfloat16))
            out_specs.append(pl.BlockSpec((META, all_subs), lambda i: (0, 0)))
    return pl.pallas_call(
        functools.partial(grid_kernel, peers=peers, first=first, turns=turns, earlier=bool(earlier)),
        grid=(1,),
        out_shape=out_shape,
        in_specs=[SMEM] + in_specs,
        out_specs=out_specs,
        scratch_shapes=scratch,
        compiler_params=pltpu.CompilerParams(vmem_limit_bytes=48 << 20),
        cost_estimate=pl.CostEstimate(
            flops=8 * (turns[1] - turns[0]) * STEP * row_count * SUB * SUB * comp_count,
            bytes_accessed=2 << 20,
            transcendentals=0,
        ),
    )(me, values, places, *more)


def halve_kernel(kept_ref, arrived_ref, *rest):
    next_kept_ref, next_sent_ref = rest[-2:]
    for at in range(kept_ref.shape[0]):
        total = kept_ref[at].astype(jnp.float32) + arrived_ref[at].astype(jnp.float32)
        if at % 2:
            next_sent_ref[at // 2] = total.astype(jnp.bfloat16)
        else:
            next_kept_ref[at // 2] = total


def halve(kept, arrived, order):
    shape = (kept.shape[0] // 2,) + kept.shape[1:]
    return pl.pallas_call(
        halve_kernel,
        out_shape=[jax.ShapeDtypeStruct(shape, jnp.float32), jax.ShapeDtypeStruct(shape, jnp.bfloat16)],
        in_specs=[VMEM] * 2 + [ANY] * len(order),
        out_specs=[VMEM] * 2,
        compiler_params=pltpu.CompilerParams(vmem_limit_bytes=8 << 20),
        cost_estimate=pl.CostEstimate(flops=1 << 18, bytes_accessed=1 << 20, transcendentals=0),
    )(kept, arrived, *order)


def paired(array, axis, mask):
    return lax.ppermute(array, axis, [(i, i ^ mask) for i in range(lax.axis_size(axis))])


def halve_all(kept, sent, axis, order):
    mask = 1
    while kept.shape[0] > 1:
        kept, sent = halve(kept, paired(sent, axis, mask), order)
        mask *= 2
    return kept, sent


def turning(chunk_numbers, sub, lanes):
    row_offsets = chunk_numbers[1:2, sub : sub + 2]
    col_shifts = chunk_numbers[4:5, sub : sub + 2]
    to = lax.broadcasted_iota(jnp.int32, (2 * SUB, 2 * SUB), 0)
    of = lax.broadcasted_iota(jnp.int32, (2 * SUB, 2 * SUB), 1)
    turned = jnp.where(of < SUB, row_offsets[:, 0:1], row_offsets[:, 1:2]) & (SUBLANES - 1)
    rows = (to == (of & SUB) + ((of + turned) & (SUB - 1))).astype(jnp.bfloat16)
    to = lax.broadcasted_iota(jnp.int32, (lanes, LANES), 1)
    of = lax.broadcasted_iota(jnp.int32, (lanes, LANES), 0)
    cols = [
        (to == ((of + col_shifts[:, which : which + 1]) & (LANES - 1))).astype(jnp.bfloat16) for which in range(2)
    ]
    return rows, cols


def sum_kernel(kept_ref, arrived_ref, numbers_ref, *rest, hops, first_sub):
    pairs, lanes = kept_ref.shape[1:3]
    group = min(lanes, LANES)
    out_ref = rest[hops or 1]
    numbers = numbers_ref[...].astype(jnp.float32).astype(jnp.int32)
    for pair in range(pairs):
        total = kept_ref[0, pair].astype(jnp.float32) + arrived_ref[0, pair].astype(jnp.float32)
        rows, cols = turning(numbers, first_sub + 2 * pair, group)
        total = lax.dot_general(
            rows, total.astype(jnp.bfloat16), (((1,), (1,)), ((), ())), preferred_element_type=jnp.float32
        ).astype(jnp.bfloat16)
        for which in range(2):
            at = (pair * 2 + which) * SUB
            for left in range(0, lanes, group):
                out_ref[at : at + SUB, left : left + LANES] = jnp.dot(
                    total[which * SUB : (which + 1) * SUB, left : left + group],
                    cols[which],
                    preferred_element_type=jnp.float32,
                ).astype(jnp.bfloat16)
    if hops:
        near_ref, go_ref = rest[hops + 1 :]
        go_ref[...] = jnp.zeros(go_ref.shape, jnp.int32)
        for at in range(hops):
            near_ref[at] = rest[at][: near_ref.shape[1], :]
    else:
        both = [ref[...].astype(jnp.float32) for ref in (numbers_ref, rest[0])]
        blank = jnp.zeros((META, out_ref.shape[1] - 2 * both[0].shape[1]), jnp.float32)
        out_ref[pairs * 2 * SUB :, :] = jnp.concatenate(both + [blank], axis=1).astype(jnp.bfloat16)


def sum_parts(kept, arrived, first_sub, own_numbers, hops, other_numbers):
    _, pairs, lanes, _ = kept.shape
    rows = pairs * 2 * SUB
    lanes = max(lanes, LANES)
    out_shape = [jax.ShapeDtypeStruct((rows if hops else rows + META, lanes), jnp.bfloat16)]
    if hops:
        out_shape.append(jax.ShapeDtypeStruct((len(hops), rows, lanes), jnp.bfloat16))
        out_shape.append(jax.ShapeDtypeStruct((SUBLANES, LANES), jnp.int32))
    return pl.pallas_call(
        functools.partial(sum_kernel, hops=len(hops), first_sub=first_sub),
        out_shape=out_shape,
        in_specs=[VMEM] * (3 + len(hops) + len(other_numbers)),
        out_specs=[VMEM] * len(out_shape),
        compiler_params=pltpu.CompilerParams(vmem_limit_bytes=8 << 20),
        cost_estimate=pl.CostEstimate(flops=1 << 20, bytes_accessed=2 << 20, transcendentals=0),
    )(kept, arrived, own_numbers, *hops, *other_numbers)


def across(array, axis):
    return [array] + [paired(array, axis, mask) for mask in range(2, lax.axis_size(axis), 2)]


def touch_plan(starts, planes, cols, spots, others):
    total = starts.shape[0]
    ids = jnp.arange(total, dtype=jnp.int32)
    taken = starts >= 0
    keys = jnp.where(taken, planes, W) * total + ids
    left = jnp.where(taken, planes * BLOCKS + cols // LANES, -1)
    right = jnp.where(taken & (cols % LANES > LANES - SUB), left + 1, -2)
    before = keys[None, :] < keys[:, None]
    after = keys[None, :] > keys[:, None]
    rank = jnp.sum(before.astype(jnp.int32), axis=1)

    def edges(units):
        same = (left[None, :] == units[:, None]) | (right[None, :] == units[:, None])
        first = ~jnp.any(same & before, axis=1)
        last = ~jnp.any(same & after, axis=1)
        return first.astype(jnp.int32) + 2 * last.astype(jnp.int32)

    flags = edges(left) + jnp.where(right >= 0, 4 * edges(right), 0) + 16 * others
    fields = jnp.stack([starts, cols, planes, spots, flags], axis=0)
    moved = jnp.where(rank[None, None, :] == ids[None, :, None], fields[:, None, :], 0)
    table = jnp.sum(moved, axis=2)
    number = jnp.sum(taken.astype(jnp.int32))
    return jnp.concatenate([table, jnp.full((1, total), number, jnp.int32)], axis=0)


def place_kernel(table_ref, near_ref, other_ref, _, out_ref, canvas, sem):
    comp_count = canvas.shape[1]
    number = table_ref[5, 0]
    row = lax.broadcasted_iota(jnp.int32, (1, SUBLANES, LANES), 1)
    lane = lax.broadcasted_iota(jnp.int32, (1, SUBLANES, LANES), 2)

    def lanes_of(block):
        return pl.ds(pl.multiple_of(block * LANES, LANES), LANES)

    def out_copy(plane, block):
        return pltpu.make_async_copy(
            canvas.at[plane, :, pl.ds(SUB, TU), lanes_of(block)],
            out_ref.at[:, plane, :, lanes_of(block)],
            sem.at[plane, block],
        )

    def clear(plane, block):
        canvas[plane, :, pl.ds(SUB, TU), lanes_of(block)] = jnp.zeros((comp_count, TU, LANES), jnp.float32)

    def when_set(flags, bit, act):
        @pl.when((flags & bit) != 0)
        def _():
            act()

    def patch_of(index):
        spot = table_ref[3, index]
        block = spot >> 16
        at = pl.ds(pl.multiple_of(spot & 0xFFFF, SUB), SUB)
        patch = jnp.where((table_ref[4, index] & 16) != 0, other_ref[block, at, :], near_ref[block, at, :])
        patch = patch.astype(jnp.float32)
        patches = []
        skip = table_ref[0, index] & (SUBLANES - 1)
        for comp in range(comp_count):
            values = patch[:, comp // 2 * LANES : (comp // 2 + 1) * LANES]
            if comp % 2:
                values = pltpu.roll(values, SUB, 1)
            values = values.reshape(SUB // SUBLANES, SUBLANES, LANES)
            head = jnp.where(row >= skip, values[:1], 0.0)
            tail = jnp.where(row < skip, values[:1], 0.0)
            patches.append(jnp.concatenate([head, values[1:], tail], axis=0))
        return patches

    def add_patch(index, patches):
        start = table_ref[0, index]
        col = table_ref[1, index]
        plane = table_ref[2, index]
        flags = table_ref[4, index]
        block = col >> 7
        shift = col & (LANES - 1)
        rows = pl.ds(pl.multiple_of(start & ~(SUBLANES - 1), SUBLANES), SUB + SUBLANES)

        def add(at, here):
            for comp in range(comp_count):
                values = jnp.where(here, patches[comp], 0.0).reshape(SUB + SUBLANES, LANES)
                canvas[plane, comp, rows, lanes_of(at)] += values

        when_set(flags, 1, lambda: clear(plane, block))
        add(block, (lane >= shift) & (lane < shift + SUB))
        when_set(flags, 2, lambda: out_copy(plane, block).start())

        @pl.when(shift > LANES - SUB)
        def _():
            when_set(flags, 4, lambda: clear(plane, block + 1))
            add(block + 1, lane < shift + SUB - LANES)
            when_set(flags, 8, lambda: out_copy(plane, block + 1).start())

    def add_two(turn_index, carry):
        index = turn_index * 4
        several = [patch_of(index + more) for more in range(4)]
        add_patch(index, several[0])
        for more in range(1, 4):

            @pl.when(index + more < number)
            def _(more=more):
                add_patch(index + more, several[more])

        return carry

    def finish(index, carry):
        block = table_ref[1, index] >> 7
        plane = table_ref[2, index]
        flags = table_ref[4, index]
        when_set(flags, 2, lambda: out_copy(plane, block).wait())
        when_set(flags, 8, lambda: out_copy(plane, block + 1).wait())
        return carry

    lax.fori_loop(0, (number + 3) // 4, add_two, 0)
    lax.fori_loop(0, number, finish, 0)


def place_all(near, other, table, tile_grid):
    comp_count = tile_grid.shape[0]
    return pl.pallas_call(
        place_kernel,
        out_shape=jax.ShapeDtypeStruct(tile_grid.shape, jnp.float32),
        in_specs=[SMEM, VMEM, VMEM, ANY],
        out_specs=ANY,
        scratch_shapes=[
            pltpu.VMEM((W, comp_count, TU + 2 * SUB, NV), jnp.float32),
            pltpu.SemaphoreType.DMA((W, BLOCKS)),
        ],
        input_output_aliases={3: 0},
        compiler_params=pltpu.CompilerParams(vmem_limit_bytes=44 << 20),
        cost_estimate=pl.CostEstimate(flops=0, bytes_accessed=16 << 20, transcendentals=0),
    )(table, near, other, tile_grid)


def body(visibilities, positions, owner, w_plane, row_offset, col_offset):
    peers = lax.axis_size("tm")
    tiles = lax.axis_size("uv")
    sub_count = visibilities.shape[1]
    comp_count = visibilities.shape[0] // peers
    tile = lax.axis_index("uv")
    half = sub_count // 2

    split = half // STEP // 2
    *parts_a, tile_grid = grid_parts(visibilities, positions, peers, 0, (0, half // STEP))
    *parts_b, own_numbers = grid_parts(
        visibilities,
        positions,
        peers,
        1,
        (0, split),
        order=tile_grid,
        numbers=(owner.T, row_offset[None], w_plane[None], col_offset[None]),
    )
    other_numbers = paired(own_numbers, "uv", 1)
    kept_a, sent_a = halve_all(*parts_a, "tm", [other_numbers])
    parts_b = grid_parts(visibilities, positions, peers, 1, (split, half // STEP), order=sent_a, earlier=parts_b)
    kept_b, sent_b = halve_all(*parts_b, "tm", [])
    arrived_a, arrived_b = (paired(sent, "tm", peers // 2) for sent in (sent_a, sent_b))
    (sum_a,) = sum_parts(kept_a, arrived_a, 0, own_numbers, [], [other_numbers])
    hops_a = across(sum_a, "uv")
    sum_b, near_a, go = sum_parts(kept_b, arrived_b, half, own_numbers, hops_a, [])
    near = jnp.concatenate([near_a, jnp.stack(across(sum_b, "uv"), axis=0)], axis=0)
    other = paired(near, "uv", 1)

    told = jnp.stack([hop[half * SUB :, : 2 * sub_count] for hop in hops_a], axis=1).astype(jnp.float32).astype(jnp.int32)
    chips = told.shape[1]
    told = told.reshape(META, -1)
    entry = jnp.arange(told.shape[1], dtype=jnp.int32)
    chip, sub = entry // (2 * sub_count), entry % sub_count
    others = entry // sub_count % 2
    spots = ((sub // half * chips + chip) << 16) + sub % half * SUB
    ahead = (told[0] - tile + go[0, 0]) % tiles
    starts = jnp.where(ahead == 0, told[1] + SUB, jnp.where(ahead == tiles - 1, told[1] + SUB - TU, -1))
    table = touch_plan(starts, told[2], told[3] * LANES + told[4], spots, others)
    return place_all(near, other, table, tile_grid)


def solution(mesh):
    placed = (P(None, "uv", "tm"), P(None, "uv", "tm"), P("uv", None), P("uv"), P("uv"), P("uv"))
    return jax.shard_map(
        body, mesh=mesh, in_specs=placed, out_specs=P("tm", None, "uv", None), check_vma=False
    )
```
